32 devices in a mesh: tm: 8 (over y, x, core), space: 4 (over z).
Axes of the slice: x: 2, y: 2, z: 4, core: 2. Of those that a mesh axis runs over, the one named last changes fastest.
Arguments:
- hits: int32 [64, 128, 256], P('tm', 'space'), may hold values from 0 to 12
- misses: int32 [64, 128, 256], P('tm', 'space'), may hold values from 0 to 12
Outputs:
- occupancy: float32 [64, 128, 256], P('tm', 'space')
- spread: float32 [64, 128, 256], P('tm', 'space')
The draws below stay inside these ranges and needn't reach their ends.
All inputs are finite; a program needn't handle non-finite values.
Results may differ from the reference program's by a relative error of at most 0.00019.
Values sent between devices are 32-bit elements; how exact they have to be, the bound alone decides.
A program may use at most 64 MiB of HBM per device.

```python
import math
import jax
import jax.numpy as jnp
from jax import lax

COLS = 256
RADIUS = 7
SCALE_T = 64
FRAMES = 64
ROWS = 128


def count_caps(key):
    base_key = jax.random.fold_in(key, 17)
    keys = jax.random.split(base_key, 8)
    shape = (FRAMES, ROWS, COLS)
    frame_index = lax.broadcasted_iota(jnp.int32, shape, 0)
    row_index = lax.broadcasted_iota(jnp.int32, shape, 1)
    column_index = lax.broadcasted_iota(jnp.int32, shape, 2)
    blob_count = 6
    centre_row = jax.random.randint(keys[0], (blob_count,), 0, ROWS, dtype=jnp.int32)
    centre_column = jax.random.randint(keys[1], (blob_count,), 0, COLS, dtype=jnp.int32)
    speed_row = jax.random.randint(keys[2], (blob_count,), -3, 4, dtype=jnp.int32)
    speed_column = jax.random.randint(keys[3], (blob_count,), -3, 4, dtype=jnp.int32)
    half_row = max(ROWS // 6, 3)
    half_column = max(COLS // 6, 3)
    inside = jnp.zeros(shape, jnp.bool_)
    for blob in range(blob_count):
        place_row = jnp.mod(centre_row[blob] + jnp.floor_divide(speed_row[blob] * frame_index, 3), ROWS)
        place_column = jnp.mod(centre_column[blob] + jnp.floor_divide(speed_column[blob] * frame_index, 3), COLS)
        gap_row = jnp.mod(row_index - place_row, ROWS)
        gap_row = jnp.minimum(gap_row, ROWS - gap_row)
        gap_column = jnp.mod(column_index - place_column, COLS)
        gap_column = jnp.minimum(gap_column, COLS - gap_column)
        inside = jnp.logical_or(inside, gap_row * half_column + gap_column * half_row <= half_row * half_column)
    window_count = 4
    start_frame = jax.random.randint(keys[4], (window_count,), 0, FRAMES, dtype=jnp.int32)
    start_row = jax.random.randint(keys[5], (window_count,), 0, ROWS, dtype=jnp.int32)
    start_column = jax.random.randint(keys[6], (window_count,), 0, COLS, dtype=jnp.int32)
    span_frame = max(FRAMES // 3, 1)
    span_row = max(ROWS // 3, 1)
    span_column = max(COLS // 3, 1)
    blind = jnp.zeros(shape, jnp.bool_)
    for window in range(window_count):
        in_time = jnp.mod(frame_index - start_frame[window], FRAMES) < span_frame
        in_rows = jnp.mod(row_index - start_row[window], ROWS) < span_row
        in_columns = jnp.mod(column_index - start_column[window], COLS) < span_column
        blind = jnp.logical_or(blind, jnp.logical_and(in_time, jnp.logical_and(in_rows, in_columns)))
    level = 1 + jnp.floor_divide(row_index * 4, ROWS)
    hit_cap = jnp.where(inside, 12, level - 1)
    miss_cap = jnp.where(inside, level - 1, 12)
    hit_cap = jnp.where(blind, 0, hit_cap).astype(jnp.int32)
    miss_cap = jnp.where(blind, 0, miss_cap).astype(jnp.int32)
    return (hit_cap, miss_cap, keys[7])


def draw_hits(key, part):
    hit_cap, miss_cap, count_key = count_caps(key)
    return jax.random.randint(jax.random.fold_in(count_key, 1), (FRAMES, ROWS, COLS), 0, hit_cap + 1, dtype=jnp.int32)


def draw_misses(key, part):
    hit_cap, miss_cap, count_key = count_caps(key)
    return jax.random.randint(jax.random.fold_in(count_key, 2), (FRAMES, ROWS, COLS), 0, miss_cap + 1, dtype=jnp.int32)


def setup_inputs(seed: int = 0) -> dict:
    streams_of = jax.random.split(jax.random.key(seed), 3)
    hits = draw_hits(jax.random.fold_in(streams_of[2], 71), 0)
    misses = draw_misses(jax.random.fold_in(streams_of[2], 71), 0)
    return dict(hits=hits, misses=misses)


sigma_cells = 3.0
prior_var = 4.0

def mat_mul(a, b):
    return (a[0] * b[0] + a[1] * b[2], a[0] * b[1] + a[1] * b[3], a[2] * b[0] + a[3] * b[2], a[2] * b[1] + a[3] * b[3])

def mat_add(a, b):
    return tuple((x + y for x, y in zip(a, b)))

def mat_sub(a, b):
    return tuple((x - y for x, y in zip(a, b)))

def transpose(a):
    return (a[0], a[2], a[1], a[3])

def as_full(s):
    return (s[0], s[1], s[1], s[2])

def as_sym(a):
    return (a[0], 0.5 * (a[1] + a[2]), a[3])

def mat_vec(a, v):
    return (a[0] * v[0] + a[1] * v[1], a[2] * v[0] + a[3] * v[1])

def vec_add(u, v):
    return (u[0] + v[0], u[1] + v[1])

def vec_sub(u, v):
    return (u[0] - v[0], u[1] - v[1])

def inverse(a):
    determ = a[0] * a[3] - a[1] * a[2]
    return (a[3] / determ, -a[1] / determ, -a[2] / determ, a[0] / determ)

def dynamics():
    decay_rate = math.sqrt(3.0) / SCALE_T
    factor = math.exp(-decay_rate)
    transit = (factor * (1.0 + decay_rate), factor, -factor * decay_rate * decay_rate, factor * (1.0 - decay_rate))
    prior_p = (prior_var, 0.0, prior_var * decay_rate * decay_rate)
    carried = mat_mul(mat_mul(transit, as_full(prior_p)), transpose(transit))
    noise_q = (prior_p[0] - carried[0], prior_p[1] - 0.5 * (carried[1] + carried[2]), prior_p[2] - carried[3])
    return (transit, prior_p, noise_q)

def kernel_taps():
    offsets = jnp.arange(-RADIUS, RADIUS + 1).astype(jnp.float32)
    weights = jnp.exp(-offsets * offsets / (2.0 * sigma_cells * sigma_cells))
    return weights / jnp.sum(weights)

def band_matrix(col_count):
    offsets = jnp.arange(-RADIUS, RADIUS + 1).astype(jnp.float32)
    total = jnp.sum(jnp.exp(-offsets * offsets / (2.0 * sigma_cells * sigma_cells)))
    index = jnp.arange(col_count)
    offset = (index[:, None] - index[None, :]).astype(jnp.float32)
    weights = jnp.exp(-offset * offset / (2.0 * sigma_cells * sigma_cells)) / total
    return jnp.where(jnp.abs(offset) <= RADIUS, weights, jnp.zeros_like(weights))

def reference(hits, misses):
    count_total = (hits + misses).astype(jnp.float32)
    hit_plus = hits.astype(jnp.float32) + 1.0
    miss_plus = misses.astype(jnp.float32) + 1.0
    both_plus = hit_plus + miss_plus
    weight = count_total * hit_plus * miss_plus / (both_plus * both_plus)
    logit = jnp.log(hit_plus / miss_plus)
    channels = jnp.stack([weight * logit, weight])
    row_count = channels.shape[2]
    col_count = channels.shape[3]
    padded = jnp.pad(channels, ((0, 0), (0, 0), (RADIUS, RADIUS), (0, 0)))
    taps_row = kernel_taps()
    rowsum = jnp.zeros_like(channels)
    for shift_row in range(2 * RADIUS + 1):
        rowsum = rowsum + taps_row[shift_row] * padded[:, :, shift_row:shift_row + row_count, :]
    colsum = jnp.dot(rowsum.reshape(-1, col_count), band_matrix(col_count), precision=lax.Precision.HIGHEST, preferred_element_type=jnp.float32).reshape(channels.shape)
    numerator = colsum[0]
    denominator = colsum[1]
    transit, prior_p, noise_q = dynamics()
    zeros_cell = jnp.zeros(numerator.shape[1:], jnp.float32)
    start = (zeros_cell, zeros_cell, zeros_cell + prior_p[0], zeros_cell + prior_p[1], zeros_cell + prior_p[2])

    def advance(state_in, frame_data):
        num_val, den_val = frame_data
        mean_a, mean_b, cov_aa, cov_ab, cov_bb = state_in
        scale_s = 1.0 + cov_aa * den_val
        moved = (num_val - den_val * mean_a) / scale_s
        gain_a = cov_aa * den_val / scale_s
        gain_b = cov_ab * den_val / scale_s
        filt = (mean_a + cov_aa * moved, mean_b + cov_ab * moved, cov_aa - gain_a * cov_aa, cov_ab - gain_a * cov_ab, cov_bb - gain_b * cov_ab)
        pred_mean = mat_vec(transit, filt[:2])
        pred_cov = as_sym(mat_add(mat_mul(mat_mul(transit, as_full(filt[2:])), transpose(transit)), as_full(noise_q)))
        return (pred_mean + pred_cov, filt)
    ignored, filtered = lax.scan(advance, start, (numerator, denominator))

    def retreat(state_in, filt_frame):
        later_mean = state_in[:2]
        later_cov = state_in[2:]
        mean_two = filt_frame[:2]
        cov = as_full(filt_frame[2:])
        predicted = mat_add(mat_mul(mat_mul(transit, cov), transpose(transit)), as_full(noise_q))
        gain_mat = mat_mul(mat_mul(cov, transpose(transit)), inverse(predicted))
        spread_gap = mat_sub(as_full(later_cov), predicted)
        new_cov = as_sym(mat_add(cov, mat_mul(mat_mul(gain_mat, spread_gap), transpose(gain_mat))))
        new_mean = vec_add(mean_two, mat_vec(gain_mat, vec_sub(later_mean, mat_vec(transit, mean_two))))
        result = new_mean + new_cov
        return (result, result)
    last_state = tuple((part[-1] for part in filtered))
    head_states = tuple((part[:-1] for part in filtered))
    ignored_two, smoothed = lax.scan(retreat, last_state, head_states, reverse=True)
    mean_value = jnp.concatenate([smoothed[0], last_state[0][None]], axis=0)
    var_value = jnp.concatenate([smoothed[2], last_state[2][None]], axis=0)
    return (jax.nn.sigmoid(mean_value), var_value)
```

```python
import functools
import math

import jax
import jax.numpy as jnp
from jax import lax
from jax.experimental import pallas as pl
from jax.experimental.pallas import tpu as pltpu
from jax.sharding import PartitionSpec as P

RADIUS = 7
SCALE_T = 64
SUB = 8
LANES = 128
SAVED = 7

sigma_cells = 3.0
prior_var = 4.0


def dynamics():
    rate = math.sqrt(3.0) / SCALE_T
    factor = math.exp(-rate)
    a, b, c, d = (
        factor * (1.0 + rate),
        factor,
        -factor * rate * rate,
        factor * (1.0 - rate),
    )
    p0, p1 = prior_var, prior_var * rate * rate
    noise = (
        p0 - (a * a * p0 + b * b * p1),
        -(a * c * p0 + b * d * p1),
        p1 - (c * c * p0 + d * d * p1),
    )
    return (a, b, c, d), (p0, p1), noise


def taps():
    raw = [math.exp(-o * o / (2.0 * sigma_cells**2)) for o in range(-RADIUS, RADIUS + 1)]
    total = sum(raw)
    return [r / total for r in raw], total


def corner(j, groups, halves):
    pair, edge = j // 2, j % 2
    side = pair // halves
    group = edge * side * (groups - 1) + (1 - edge) * (1 + side)
    return group * SUB, (pair % halves) * LANES


def spread_out(landed, occ, spr, sems):
    groups, halves = occ.shape[1] // SUB, occ.shape[2] // LANES
    copies = []
    for j in range(groups * halves):
        row0, col0 = corner(j, groups, halves)
        for k, out in enumerate((occ, spr)):
            copies.append(pltpu.make_async_copy(
                landed.at[j, k], out.at[:, row0 : row0 + SUB, col0 : col0 + LANES],
                sems.at[j, k]))
    for copy in copies:
        copy.start()
    for copy in copies:
        copy.wait()


def kernel(tm_count, space_count, hits_hbm, misses_hbm, landed, hits, misses, chan, horiz,
           window, send, recv, saved, back, halo_send, halo_recv, go_send, go_recv, ret_send, ret_recv, load):
    load_hits = pltpu.make_async_copy(hits_hbm, hits, load.at[0])
    load_misses = pltpu.make_async_copy(misses_hbm, misses, load.at[1])
    load_hits.start()
    load_misses.start()
    frames, rows, cols = hits.shape
    groups = rows // SUB
    halves = cols // LANES
    chunks = (rows // SUB) * halves
    stride = tm_count // chunks
    me = lax.axis_index("tm")
    tile = lax.axis_index("space")
    mine = me // stride
    (ta, tb, tc, td), (prior0, prior1), (q00, q01, q11) = dynamics()
    weights, total = taps()
    has_up = tile > 0
    has_down = tile < space_count - 1
    barrier = pltpu.get_barrier_semaphore()

    def greet(k, carry):
        pl.semaphore_signal(barrier, inc=1, device_id={"tm": (me + k) % tm_count})
        return carry

    lax.fori_loop(1, tm_count, greet, 0)

    @pl.when(has_up)
    def _():
        pl.semaphore_signal(barrier, inc=1, device_id={"space": tile - 1})

    @pl.when(has_down)
    def _():
        pl.semaphore_signal(barrier, inc=1, device_id={"space": tile + 1})

    own = pl.ds(SUB, rows)
    load_hits.wait()
    load_misses.wait()

    def observe(f, carry):
        h, m = hits[f], misses[f]
        hp = h.astype(jnp.float32) + 1.0
        mp = m.astype(jnp.float32) + 1.0
        both = hp + mp
        weight = (h + m).astype(jnp.float32) * hp * mp / (both * both)
        chan[0, f, own, :] = weight * jnp.log(hp / mp)
        chan[1, f, own, :] = weight
        return carry

    lax.fori_loop(0, frames, observe, 0)

    @pl.when(jnp.logical_not(has_up))
    def _():
        chan[:, :, 0:SUB, :] = jnp.zeros((2, frames, SUB, cols), jnp.float32)

    @pl.when(jnp.logical_not(has_down))
    def _():
        chan[:, :, SUB + rows :, :] = jnp.zeros((2, frames, SUB, cols), jnp.float32)

    neighbours = has_up.astype(jnp.int32) + has_down.astype(jnp.int32)
    pl.semaphore_wait(barrier, tm_count - 1 + neighbours)

    to_down = pltpu.make_async_remote_copy(
        src_ref=chan.at[:, :, pl.ds(rows, SUB), :],
        dst_ref=chan.at[:, :, pl.ds(0, SUB), :],
        send_sem=halo_send.at[0], recv_sem=halo_recv.at[0],
        device_id={"space": tile + 1})
    to_up = pltpu.make_async_remote_copy(
        src_ref=chan.at[:, :, pl.ds(SUB, SUB), :],
        dst_ref=chan.at[:, :, pl.ds(SUB + rows, SUB), :],
        send_sem=halo_send.at[1], recv_sem=halo_recv.at[1],
        device_id={"space": tile - 1})

    @pl.when(has_down)
    def _():
        to_down.start()

    @pl.when(has_up)
    def _():
        to_up.start()

    offset = (lax.broadcasted_iota(jnp.int32, (cols, cols), 0)
              - lax.broadcasted_iota(jnp.int32, (cols, cols), 1))
    far = offset.astype(jnp.float32)
    band = jnp.where(jnp.abs(offset) <= RADIUS,
                     jnp.exp(-far * far / (2.0 * sigma_cells**2)) / total, 0.0)

    band_high = band.astype(jnp.bfloat16)
    band_low = (band - band_high.astype(jnp.float32)).astype(jnp.bfloat16)

    def across(start, size):
        flat = chan[:, :, start : start + size, :].reshape(2 * frames * size, cols)
        high = flat.astype(jnp.bfloat16)
        low = (flat - high.astype(jnp.float32)).astype(jnp.bfloat16)
        dot = functools.partial(jnp.dot, preferred_element_type=jnp.float32)
        out = dot(high, band_high) + (dot(low, band_high) + dot(high, band_low))
        horiz[:, :, start : start + size, :] = out.reshape(2, frames, size, cols)

    def down_chunk(j):
        row0, col0 = corner(j, groups, halves)
        row0, col0 = pl.multiple_of(row0, SUB), pl.multiple_of(col0, LANES)
        window[...] = horiz[:, :, pl.ds(row0, 3 * SUB), pl.ds(col0, LANES)]

        def at(s):
            first = SUB - RADIUS + s
            return window[:, :, first : first + SUB, :]

        out = weights[RADIUS] * at(RADIUS)
        for s in range(RADIUS):
            out = out + weights[s] * (at(s) + at(2 * RADIUS - s))
        return out

    def go_copy(j):
        return pltpu.make_async_remote_copy(
            src_ref=send.at[j], dst_ref=recv.at[me], send_sem=go_send.at[j],
            recv_sem=go_recv.at[me], device_id={"tm": j * stride})

    def scatter(edge):
        def step(k, carry):
            pairs = chunks // 2
            j = 2 * ((mine // 2 + k) % pairs) + edge
            send[j] = down_chunk(j)

            @pl.when(j * stride != me)
            def _():
                go_copy(j).start()

            @pl.when(j * stride == me)
            def _():
                recv[me] = send[j]

            return carry

        lax.fori_loop(1, chunks // 2 + 1, step, 0)

    across(SUB, rows)
    scatter(0)

    @pl.when(has_up)
    def _():
        to_down.wait_recv()

    @pl.when(has_down)
    def _():
        to_up.wait_recv()

    across(0, SUB)
    across(SUB + rows, SUB)
    scatter(1)

    def back_copy(i):
        return pltpu.make_async_remote_copy(
            src_ref=back.at[i], dst_ref=landed.at[mine], send_sem=ret_send.at[i],
            recv_sem=ret_recv.at[mine], device_id={"tm": i})

    def smooth():
        def forward(i, state):
            @pl.when(i != me)
            def _():
                pltpu.make_async_remote_copy(
                    src_ref=send.at[0], dst_ref=recv.at[i], send_sem=go_send.at[0],
                    recv_sem=go_recv.at[i], device_id={"tm": i}).wait_recv()

            m0, m1, p00, p01, p11 = state
            for f in range(frames):
                num, den = recv[i, 0, f], recv[i, 1, f]
                inv = 1.0 / (1.0 + p00 * den)
                w = den * inv
                e = (num - den * m0) * inv
                k1 = p01 * w
                m0, m1 = m0 + p00 * e, m1 + p01 * e
                p11 = p11 - k1 * p01
                p00, p01 = p00 * inv, p01 * inv
                for slot, value in enumerate((inv, w, e, k1, m0, p00, p01)):
                    saved[i, f, slot] = value
                m0, m1 = ta * m0 + tb * m1, tc * m0 + td * m1
                p00, p01, p11 = (
                    (ta * ta) * p00 + (2.0 * ta * tb) * p01 + ((tb * tb) * p11 + q00),
                    (ta * tc) * p00 + (ta * td + tb * tc) * p01 + ((tb * td) * p11 + q01),
                    (tc * tc) * p00 + (2.0 * tc * td) * p01 + ((td * td) * p11 + q11),
                )
            return m0, m1, p00, p01, p11

        zero = jnp.zeros((SUB, LANES), jnp.float32)
        lax.fori_loop(0, tm_count, forward, (zero, zero, zero + prior0, zero, zero + prior1))

        def backward(n, state):
            i = tm_count - 1 - n
            u0, u1, n00, n01, n11 = state
            for f in reversed(range(frames)):
                inv, w, e, k1, m0, p00, p01 = (saved[i, f, slot] for slot in range(SAVED))
                mean = m0 + p00 * u0 + p01 * u1
                back[i, 0, f] = 1.0 / (1.0 + jnp.exp(-mean))
                back[i, 1, f] = p00 - (
                    p00 * p00 * n00 + 2.0 * (p00 * p01) * n01 + p01 * p01 * n11)
                r0 = e + inv * u0 - k1 * u1
                l00 = w + (inv * inv) * n00 - (2.0 * inv * k1) * n01 + (k1 * k1) * n11
                l01 = inv * n01 - k1 * n11
                u0, u1 = ta * r0 + tc * u1, tb * r0 + td * u1
                n00, n01, n11 = (
                    (ta * ta) * l00 + ((2.0 * ta * tc) * l01 + (tc * tc) * n11),
                    (ta * tb) * l00 + ((ta * td + tb * tc) * l01 + (tc * td) * n11),
                    (tb * tb) * l00 + ((2.0 * tb * td) * l01 + (td * td) * n11),
                )

            return u0, u1, n00, n01, n11

        lax.fori_loop(0, tm_count, backward, (zero,) * 5)

        def give(k, carry):
            back_copy((me + k) % tm_count).start()
            return carry

        lax.fori_loop(1, tm_count, give, 0)
        landed[mine] = back[me]

    if stride == 1:
        smooth()
    else:
        pl.when(me % stride == 0)(smooth)

    def place(k, carry):
        j = (mine + k) % chunks

        @pl.when(j * stride != me)
        def _():
            pltpu.make_async_remote_copy(
                src_ref=back.at[0], dst_ref=landed.at[j], send_sem=ret_send.at[0],
                recv_sem=ret_recv.at[j], device_id={"tm": j * stride}).wait_recv()

        return carry

    lax.fori_loop(0, chunks, place, 0)

    @pl.when(has_down)
    def _():
        to_down.wait_send()

    @pl.when(has_up)
    def _():
        to_up.wait_send()

    def sent(j, carry):
        @pl.when(j * stride != me)
        def _():
            go_copy(j).wait_send()

        return carry

    lax.fori_loop(0, chunks, sent, 0)

    def returned(i, carry):
        @pl.when(jnp.logical_and(i != me, me % stride == 0))
        def _():
            back_copy(i).wait_send()

        return carry

    lax.fori_loop(0, tm_count, returned, 0)


def solution(mesh):
    tm_count, space_count = mesh.shape["tm"], mesh.shape["space"]

    def body(hits, misses):
        frames, rows, cols = hits.shape
        chunks = (rows // SUB) * (cols // LANES)
        cells = (SUB, LANES)
        vmem = pl.BlockSpec(memory_space=pltpu.VMEM)
        out = jax.ShapeDtypeStruct(hits.shape, jnp.float32)
        landed = pl.pallas_call(
            functools.partial(kernel, tm_count, space_count),
            out_shape=pltpu.VMEM((chunks, 2, frames) + cells, jnp.float32),
            in_specs=[pl.BlockSpec(memory_space=pltpu.HBM)] * 2,
            out_specs=vmem,
            scratch_shapes=[
                pltpu.VMEM(hits.shape, jnp.int32),
                pltpu.VMEM(hits.shape, jnp.int32),
                pltpu.VMEM((2, frames, rows + 2 * SUB, cols), jnp.float32),
                pltpu.VMEM((2, frames, rows + 2 * SUB, cols), jnp.float32),
                pltpu.VMEM((2, frames, 3 * SUB, LANES), jnp.float32),
                pltpu.VMEM((chunks, 2, frames) + cells, jnp.float32),
                pltpu.VMEM((tm_count, 2, frames) + cells, jnp.float32),
                pltpu.VMEM((tm_count, frames, SAVED) + cells, jnp.float32),
                pltpu.VMEM((tm_count, 2, frames) + cells, jnp.float32),
                pltpu.SemaphoreType.DMA((2,)),
                pltpu.SemaphoreType.DMA((2,)),
                pltpu.SemaphoreType.DMA((chunks,)),
                pltpu.SemaphoreType.DMA((tm_count,)),
                pltpu.SemaphoreType.DMA((tm_count,)),
                pltpu.SemaphoreType.DMA((chunks,)),
                pltpu.SemaphoreType.DMA((2,)),
            ],
            compiler_params=pltpu.CompilerParams(
                collective_id=0, has_side_effects=True, vmem_limit_bytes=49152 * 1024),
        )(pltpu.with_memory_space_constraint(hits, pltpu.HBM), pltpu.with_memory_space_constraint(misses, pltpu.HBM))
        hbm = pl.BlockSpec(memory_space=pltpu.HBM)
        return pl.pallas_call(
            spread_out,
            out_shape=(out, out),
            in_specs=[vmem],
            out_specs=(hbm, hbm),
            scratch_shapes=[pltpu.SemaphoreType.DMA((chunks, 2))],
            compiler_params=pltpu.CompilerParams(vmem_limit_bytes=8 * 1024 * 1024),
        )(landed)

    placed = P("tm", "space", None)
    return jax.shard_map(body, mesh=mesh, in_specs=(placed, placed),
                         out_specs=(placed, placed), check_vma=False)
```

```python
import functools
import math

import jax
import jax.numpy as jnp
from jax import lax
from jax.experimental import pallas as pl
from jax.experimental.pallas import tpu as pltpu
from jax.sharding import PartitionSpec as P

RADIUS = 7
SCALE_T = 64
SUB = 8
LANES = 128
CORES = 2
VALUES = 14
STATE = slice(0, 5)
INFO = slice(9, 14)
SAVED = 7

sigma_cells = 3.0
prior_var = 4.0


def dynamics():
    q = math.sqrt(3.0) / SCALE_T
    decay = math.exp(-q)
    p0, p1 = prior_var, prior_var * q * q
    prior = (p0, q * p0, q * q * p0 + p1)
    a, b, c = prior
    noise = (
        a - decay**2 * (a + 2.0 * b + c),
        b - decay**2 * (b + c),
        c - decay**2 * c,
    )
    return decay, prior, noise


def taps():
    raw = [math.exp(-o * o / (2.0 * sigma_cells**2)) for o in range(-RADIUS, RADIUS + 1)]
    total = sum(raw)
    return [r / total for r in raw], total


def inverse(x):
    r = pl.reciprocal(x, approx=True)
    return r * (2.0 - x * r)


def absorb(x, y, g):
    x00, x01, x11 = x
    y00, y01, y11 = y
    d00 = 1.0 + (x00 * y00 + x01 * y01)
    d01 = x00 * y01 + x01 * y11
    d10 = x01 * y00 + x11 * y01
    d11 = 1.0 + (x01 * y01 + x11 * y11)
    inv = inverse(d00 * d11 - d01 * d10)
    det = x00 * x11 - x01 * x01
    out = ((x00 + y11 * det) * inv, (x01 - y01 * det) * inv, (x11 + y00 * det) * inv)
    vec = ((d11 * g[0] - d01 * g[1]) * inv, (d00 * g[1] - d10 * g[0]) * inv)
    return out, vec


def congruent(a, s):
    a00, a01, a10, a11 = a
    s00, s01, s11 = s
    u0, u1 = a00 * s00 + a01 * s01, a00 * s01 + a01 * s11
    v0, v1 = a10 * s00 + a11 * s01, a10 * s01 + a11 * s11
    return u0 * a00 + u1 * a01, u0 * a10 + u1 * a11, v0 * a10 + v1 * a11


def symv(s, v):
    return s[0] * v[0] + s[1] * v[1], s[1] * v[0] + s[2] * v[1]


def matv(a, v):
    return a[0] * v[0] + a[1] * v[1], a[2] * v[0] + a[3] * v[1]


def add(*parts):
    return tuple(sum(p[1:], p[0]) for p in zip(*parts))


def carry_state(state, block):
    mean, cov = state[:2], state[2:]
    shift = symv(cov, block[9:11])
    cov, mean = absorb(cov, block[11:14], add(mean, shift))
    a = block[5:9]
    return add(matv(a, mean), block[0:2]) + add(congruent(a, cov), block[2:5])


def carry_info(block, info):
    vec, mat = info[:2], info[2:]
    pulled = symv(mat, block[0:2])
    s, v = absorb(mat, block[2:5], (vec[0] - pulled[0], vec[1] - pulled[1]))
    a00, a01, a10, a11 = block[5:9]
    back = (a00, a10, a01, a11)
    return add(matv(back, v), block[9:11]) + add(congruent(back, s), block[11:14])


def join(one, two):
    state = carry_state(one[0:5], two)
    info = carry_info(one, two[9:14])
    c, j = one[2:5], two[11:14]
    d00 = 1.0 + (c[0] * j[0] + c[1] * j[1])
    d01 = c[0] * j[1] + c[1] * j[2]
    d10 = c[1] * j[0] + c[2] * j[1]
    d11 = 1.0 + (c[1] * j[1] + c[2] * j[2])
    inv = inverse(d00 * d11 - d01 * d10)
    a00, a01, a10, a11 = one[5:9]
    m = (
        (d11 * a00 - d01 * a10) * inv,
        (d11 * a01 - d01 * a11) * inv,
        (d00 * a10 - d10 * a00) * inv,
        (d00 * a11 - d10 * a01) * inv,
    )
    b00, b01, b10, b11 = two[5:9]
    a = (
        b00 * m[0] + b01 * m[2],
        b00 * m[1] + b01 * m[3],
        b10 * m[0] + b11 * m[2],
        b10 * m[1] + b11 * m[3],
    )
    return state + a + info


def kernel(tm_count, space_count, hits_hbm, misses_hbm, landed, hits, misses, chan, field,
           give, obs, elem, incl, got, pre, suf, saved, res, load, halo_send, halo_recv,
           pair_send, pair_recv, level_send, level_recv, res_send, res_recv):
    load_hits = pltpu.make_async_copy(hits_hbm, hits, load.at[0])
    load_misses = pltpu.make_async_copy(misses_hbm, misses, load.at[1])
    load_hits.start()
    load_misses.start()
    frames, rows, cols = hits.shape
    span = CORES * frames
    chips = tm_count // CORES
    levels = chips.bit_length() - 1
    me = lax.axis_index("tm")
    tile = lax.axis_index("space")
    chip, core = me // CORES, me % CORES
    partner = me + 1 - 2 * core
    decay, prior, noise = dynamics()
    weights, total = taps()
    has_up = tile > 0
    has_down = tile < space_count - 1
    barrier = pltpu.get_barrier_semaphore()

    @pl.when(has_up)
    def _():
        pl.semaphore_signal(barrier, inc=1, device_id={"space": tile - 1})
        pl.semaphore_signal(barrier, inc=1, device_id={"tm": partner, "space": tile - 1})

    @pl.when(has_down)
    def _():
        pl.semaphore_signal(barrier, inc=1, device_id={"space": tile + 1})
        pl.semaphore_signal(barrier, inc=1, device_id={"tm": partner, "space": tile + 1})

    pl.semaphore_signal(barrier, inc=1, device_id={"tm": partner})

    def greet(k, carry):
        pl.semaphore_signal(barrier, inc=1,
                            device_id={"tm": CORES * ((chip + k) % chips) + core})
        return carry

    lax.fori_loop(1, chips, greet, 0)

    own = pl.ds(core * frames, frames)
    other = pl.ds((1 - core) * frames, frames)
    cells = (2 * SUB, LANES)

    @pl.when(jnp.logical_not(has_up))
    def _():
        field[:, :, 0:SUB, :] = jnp.zeros((2, span, SUB, LANES), jnp.float32)

    @pl.when(jnp.logical_not(has_down))
    def _():
        field[:, :, SUB + rows :, :] = jnp.zeros((2, span, SUB, LANES), jnp.float32)

    @pl.when(chip == 0)
    def _():
        for p in range(2):
            for k, value in enumerate((0.0, 0.0) + prior):
                pre[p, k] = jnp.full(cells, value, jnp.float32)

    @pl.when(chip == chips - 1)
    def _():
        suf[:, INFO] = jnp.zeros((2, 5) + cells, jnp.float32)

    column = lax.broadcasted_iota(jnp.int32, (cols, cols), 1) + core * LANES
    column = jnp.where(column >= cols, column - cols, column)
    offset = lax.broadcasted_iota(jnp.int32, (cols, cols), 0) - column
    far = offset.astype(jnp.float32)
    band = jnp.where(jnp.abs(offset) <= RADIUS,
                     jnp.exp(-far * far / (2.0 * sigma_cells**2)) / total, 0.0)
    band_high = band.astype(jnp.bfloat16)
    band_low = (band - band_high.astype(jnp.float32)).astype(jnp.bfloat16)

    load_hits.wait()
    load_misses.wait()
    late = core.astype(jnp.float32)
    base = 1.0 + late * (decay**frames - 1.0)
    base2 = 1.0 + late * (decay ** (2 * frames) - 1.0)
    for f in range(frames):
        h, m = hits[f], misses[f]
        hp = h.astype(jnp.float32) + 1.0
        mp = m.astype(jnp.float32) + 1.0
        inv = inverse(hp + mp)
        weight = (h + m).astype(jnp.float32) * (hp * inv) * (mp * inv)
        chan[0, f] = weight * (jnp.log(hp) - jnp.log(mp)) * (base * decay**f)
        chan[1, f] = weight * (base2 * decay ** (2 * f))

    dot = functools.partial(jnp.dot, preferred_element_type=jnp.float32)
    for c in range(2):
        flat = chan[c].reshape(frames * rows, cols)
        high = flat.astype(jnp.bfloat16)
        low = (flat - high.astype(jnp.float32)).astype(jnp.bfloat16)
        out = dot(high, band_high) + (dot(low, band_high) + dot(high, band_low))
        out = out.reshape(frames, rows, cols)
        field[c, own, SUB : SUB + rows, :] = out[:, :, :LANES]
        give[c] = out[:, :, LANES:]

    neighbours = has_up.astype(jnp.int32) + has_down.astype(jnp.int32)
    pl.semaphore_wait(barrier, chips + 2 * neighbours)

    top, bottom = pl.ds(0, SUB), pl.ds(SUB + rows, SUB)

    def halo(direction, crossed):
        step = 1 - 2 * direction
        where = bottom if direction else top
        if crossed:
            row = pl.ds(0, SUB) if direction else pl.ds(rows - SUB, SUB)
            source, target = give.at[:, :, row, :], {"tm": partner, "space": tile + step}
        else:
            row = pl.ds(SUB, SUB) if direction else pl.ds(rows, SUB)
            source, target = field.at[:, own, row, :], {"space": tile + step}
        return pltpu.make_async_remote_copy(
            src_ref=source, dst_ref=field.at[:, own, where, :],
            send_sem=halo_send.at[direction, crossed],
            recv_sem=halo_recv.at[direction, core], device_id=target)

    def halo_arrived(direction, sender):
        where = bottom if direction else top
        part = field.at[:, pl.ds(sender * frames, frames), where, :]
        pltpu.make_async_remote_copy(
            src_ref=part, dst_ref=part, send_sem=halo_send.at[direction, 0],
            recv_sem=halo_recv.at[direction, sender], device_id={"tm": partner}).wait_recv()

    for direction, there in ((0, has_down), (1, has_up)):
        @pl.when(there)
        def _():
            for crossed in range(2):
                halo(direction, crossed).start()

    to_partner = pltpu.make_async_remote_copy(
        src_ref=give, dst_ref=field.at[:, own, pl.ds(SUB, rows), :],
        send_sem=pair_send.at[0], recv_sem=pair_recv.at[0], device_id={"tm": partner})
    to_partner.start()

    phases = (tuple(range(1, rows // SUB - 1)), (0, rows // SUB - 1))

    def down(c, t, group):
        def at(s):
            first = group * SUB + SUB - RADIUS + s
            return field[c, t, first : first + SUB, :]

        out = weights[RADIUS] * at(RADIUS)
        for s in range(RADIUS):
            out = out + weights[s] * (at(s) + at(2 * RADIUS - s))
        return out

    first = (chip == 0).astype(jnp.float32)

    def scaled_noise(t):
        return tuple(v * decay ** (-2 * (t + 1)) for v in noise)

    def summary(p):
        zero = jnp.zeros(cells, jnp.float32)
        m0 = m1 = a01 = c0 = eta0 = eta1 = j00 = j01 = j11 = zero
        a00 = c1 = zero + 1.0
        p00, p01, p11 = (zero + v * first for v in prior)
        for t in range(span):
            for c in range(2):
                for k, group in enumerate(phases[p]):
                    obs[p, c, t, k * SUB : k * SUB + SUB, :] = down(c, t, group)
            num, den = obs[p, 0, t], obs[p, 1, t]
            inv = inverse(1.0 + p00 * den)
            w = den * inv
            e = (num - den * m0) * inv
            k1 = p01 * w
            m0, m1 = m0 + p00 * e, m1 + p01 * e
            p11 = p11 - k1 * p01
            p00, p01 = p00 * inv, p01 * inv
            eta0, eta1 = eta0 + a00 * e, eta1 + a01 * e
            w0, w1 = w * a00, w * a01
            j00, j01, j11 = j00 + w0 * a00, j01 + w0 * a01, j11 + w1 * a01
            c0, c1 = c0 - k1 * a00, c1 - k1 * a01
            a00, a01 = a00 * inv, a01 * inv
            q00, q01, q11 = scaled_noise(t)
            m0 = m0 + m1
            a00, a01 = a00 + c0, a01 + c1
            r = p01 + p11
            p00, p01, p11 = (p00 + p01) + (r + q00), r + q01, p11 + q11
        s, s2 = decay**span, decay ** (2 * span)
        block = (m0 * s, m1 * s, p00 * s2, p01 * s2, p11 * s2,
                 a00 * s, a01 * s, c0 * s, c1 * s, eta0, eta1, j00, j01, j11)
        for k, value in enumerate(block):
            elem[p, k] = value

    def values(ref, part):
        return tuple(ref[k] for k in range(part.start, part.stop))

    def put(ref, part, items):
        for k, item in zip(range(part.start, part.stop), items):
            ref[k] = item

    full = slice(0, VALUES)

    def level_copy(p, level, d, target, part):
        src = elem.at[p] if level == 0 else incl.at[p, level - 1]
        cut = pl.ds(part.start, part.stop - part.start)
        return pltpu.make_async_remote_copy(
            src_ref=src.at[cut], dst_ref=got.at[p, level, cut],
            send_sem=level_send.at[p, level, d], recv_sem=level_recv.at[p, level],
            device_id={"tm": CORES * target + core})

    def branches(level):
        size = 1 << level
        ends = chip % (2 * size) == size - 1
        starts = chip % (2 * size) == size
        if chips == 2 * size:
            return ((ends, STATE),), ((starts, INFO),)
        lone = chip == size - 1
        last = chip == chips - size
        return (((lone, STATE), (jnp.logical_and(ends, jnp.logical_not(lone)), full)),
                ((last, INFO), (jnp.logical_and(starts, jnp.logical_not(last)), full)))

    def each_send(p, level, act):
        size = 1 << level
        lefts, rights = branches(level)
        for group, step in ((lefts, 1), (rights, -1)):
            for condition, part in group:
                @pl.when(condition)
                def _():
                    for d in range(size):
                        act(level_copy(p, level, d, chip + step * (d + 1), part))

    def send_level(p, level):
        if level:
            out = incl.at[p, level - 1]
            lefts, rights = branches(level)
            for condition, part in lefts:
                @pl.when(condition)
                def _():
                    one, two = values(pre.at[p], part), values(elem.at[p], full)
                    put(out, part, carry_state(one, two) if part is STATE else join(one, two))
            for condition, part in rights:
                @pl.when(condition)
                def _():
                    one, two = values(elem.at[p], full), values(suf.at[p], part)
                    put(out, part, carry_info(one, two) if part is INFO else join(one, two))
        each_send(p, level, lambda copy: copy.start())

    def take_level(p, level):
        size = 1 << level
        right = (chip // size) % 2 == 1
        left = jnp.logical_not(right)
        if chips == 2 * size:
            cases = ((right, STATE, True), (left, INFO, False))
        else:
            low, high = chip < 2 * size, chip >= chips - 2 * size
            cases = (
                (jnp.logical_and(right, low), STATE, True),
                (jnp.logical_and(right, jnp.logical_not(low)), full, True),
                (jnp.logical_and(left, high), INFO, False),
                (jnp.logical_and(left, jnp.logical_not(high)), full, False),
            )
        for condition, part, earlier in cases:
            @pl.when(condition)
            def _():
                level_copy(p, level, 0, chip, part).wait_recv()
                bare = chip % size == (0 if earlier else size - 1)
                mine = pre.at[p] if earlier else suf.at[p]

                def keep():
                    put(mine, part, values(got.at[p, level], part))

                def merge():
                    new = values(got.at[p, level], part)
                    old = values(mine, full)
                    if part is STATE:
                        put(mine, part, carry_state(new, old))
                    elif part is INFO:
                        put(mine, part, carry_info(old, new))
                    else:
                        put(mine, part, join(new, old) if earlier else join(old, new))

                if size == 1:
                    keep()
                else:
                    pl.when(bare)(keep)
                    pl.when(jnp.logical_not(bare))(merge)

    def smooth(p):
        m0, m1, p00, p01, p11 = values(pre.at[p], STATE)
        for t in range(span):
            num, den = obs[p, 0, t], obs[p, 1, t]
            inv = inverse(1.0 + p00 * den)
            w = den * inv
            e = (num - den * m0) * inv
            k1 = p01 * w
            m0, m1 = m0 + p00 * e, m1 + p01 * e
            p11 = p11 - k1 * p01
            p00, p01 = p00 * inv, p01 * inv
            for slot, value in enumerate((inv, w, e, k1, m0, p00, p01)):
                saved[t, slot] = value
            q00, q01, q11 = scaled_noise(t)
            m0 = m0 + m1
            r = p01 + p11
            p00, p01, p11 = (p00 + p01) + (r + q00), r + q01, p11 + q11

        i0, i1, i00, i01, i11 = values(suf.at[p], INFO)
        s, s2 = decay**span, decay ** (2 * span)
        mat = (i00 * s2, i01 * s2, i11 * s2)
        pulled = symv(mat, (m0, m1))
        (n00, n01, n11), (u0, u1) = absorb(mat, (p00, p01, p11),
                                           (i0 * s - pulled[0], i1 * s - pulled[1]))
        for t in reversed(range(span)):
            u1 = u0 + u1
            both = n00 + n01
            n01, n11 = both, both + (n01 + n11)
            inv, w, e, k1, m0, p00, p01 = (saved[t, slot] for slot in range(SAVED))
            mean = m0 + p00 * u0 + p01 * u1
            g0, g1 = p00 * n00 + p01 * n01, p00 * n01 + p01 * n11
            occupancy = inverse(1.0 + jnp.exp(mean * -(decay**t)))
            spread = (p00 - (p00 * g0 + p01 * g1)) * decay ** (2 * t)
            for k, group in enumerate(phases[p]):
                res[0, t, group * SUB : group * SUB + SUB, :] = occupancy[k * SUB : k * SUB + SUB]
                res[1, t, group * SUB : group * SUB + SUB, :] = spread[k * SUB : k * SUB + SUB]
            u0 = e + inv * u0 - k1 * u1
            l01 = inv * n01 - k1 * n11
            n00 = w + inv * (inv * n00 - k1 * n01) - k1 * l01
            n01 = l01

    half = pl.ds(pl.multiple_of(core * LANES, LANES), LANES)
    bands = ((slice(SUB, rows - SUB),), (slice(0, SUB), slice(rows - SUB, rows)))

    def result_copy(p, k):
        band_rows = bands[p][k]
        cut = pl.ds(band_rows.start, band_rows.stop - band_rows.start)
        return pltpu.make_async_remote_copy(
            src_ref=res.at[:, other, cut, :], dst_ref=landed.at[:, :, cut, half],
            send_sem=res_send.at[p, k], recv_sem=res_recv.at[p, k], device_id={"tm": partner})

    def finish(p):
        smooth(p)
        for k in range(len(bands[p])):
            result_copy(p, k).start()
        for band_rows in bands[p]:
            landed[:, :, band_rows, half] = res[:, own, band_rows, :]

    to_partner.wait_recv()
    summary(0)
    send_level(0, 0)
    for direction, there in ((0, has_up), (1, has_down)):
        @pl.when(there)
        def _():
            for sender in range(CORES):
                halo_arrived(direction, sender)
    summary(1)
    send_level(1, 0)
    for level in range(levels):
        for p in range(2):
            take_level(p, level)
            if level + 1 < levels:
                send_level(p, level + 1)
            else:
                finish(p)

    for p in range(2):
        for k in range(len(bands[p])):
            result_copy(p, k).wait_recv()
    for p in range(2):
        for k in range(len(bands[p])):
            result_copy(p, k).wait_send()
    for p in range(2):
        for level in range(levels):
            each_send(p, level, lambda copy: copy.wait_send())
    for direction, there in ((0, has_down), (1, has_up)):
        @pl.when(there)
        def _():
            for crossed in range(2):
                halo(direction, crossed).wait_send()
    to_partner.wait_send()


def hand_out(landed, occupancy, spread, sems):
    copies = [pltpu.make_async_copy(landed.at[k], out, sems.at[k])
              for k, out in enumerate((occupancy, spread))]
    for copy in copies:
        copy.start()
    for copy in copies:
        copy.wait()


def solution(mesh):
    tm_count, space_count = mesh.shape["tm"], mesh.shape["space"]

    def body(hits, misses):
        frames, rows, cols = hits.shape
        span, chips = CORES * frames, tm_count // CORES
        levels = chips.bit_length() - 1
        cells = (2 * SUB, LANES)
        assert rows == 4 * SUB and cols == CORES * LANES and chips == 1 << levels
        f32 = jnp.float32
        hbm = pl.BlockSpec(memory_space=pltpu.HBM)
        vmem = pl.BlockSpec(memory_space=pltpu.VMEM)
        dma = pltpu.SemaphoreType.DMA
        landed = pl.pallas_call(
            functools.partial(kernel, tm_count, space_count),
            out_shape=pltpu.VMEM((2, frames, rows, cols), f32),
            in_specs=[hbm] * 2,
            out_specs=vmem,
            scratch_shapes=[
                pltpu.VMEM(hits.shape, jnp.int32),
                pltpu.VMEM(hits.shape, jnp.int32),
                pltpu.VMEM((2, frames, rows, cols), f32),
                pltpu.VMEM((2, span, rows + 2 * SUB, LANES), f32),
                pltpu.VMEM((2, frames, rows, LANES), f32),
                pltpu.VMEM((2, 2, span) + cells, f32),
                pltpu.VMEM((2, VALUES) + cells, f32),
                pltpu.VMEM((2, levels - 1, VALUES) + cells, f32),
                pltpu.VMEM((2, levels, VALUES) + cells, f32),
                pltpu.VMEM((2, VALUES) + cells, f32),
                pltpu.VMEM((2, VALUES) + cells, f32),
                pltpu.VMEM((span, SAVED) + cells, f32),
                pltpu.VMEM((2, span, rows, LANES), f32),
                dma((2,)),
                dma((2, 2)),
                dma((2, 2)),
                dma((1,)),
                dma((1,)),
                dma((2, levels, chips // 2)),
                dma((2, levels)),
                dma((2, 2)),
                dma((2, 2)),
            ],
            compiler_params=pltpu.CompilerParams(
                collective_id=0, has_side_effects=True, vmem_limit_bytes=32 * 1024 * 1024),
        )(pltpu.with_memory_space_constraint(hits, pltpu.HBM),
          pltpu.with_memory_space_constraint(misses, pltpu.HBM))
        out = jax.ShapeDtypeStruct(hits.shape, f32)
        return pl.pallas_call(
            hand_out,
            out_shape=(out, out),
            in_specs=[vmem],
            out_specs=(hbm, hbm),
            scratch_shapes=[dma((2,))],
            compiler_params=pltpu.CompilerParams(vmem_limit_bytes=8 * 1024 * 1024),
        )(landed)

    placed = P("tm", "space", None)
    return jax.shard_map(body, mesh=mesh, in_specs=(placed, placed),
                         out_specs=(placed, placed), check_vma=False)
```

```python
import functools
import math

import jax
import jax.numpy as jnp
from jax import lax
from jax.experimental import pallas as pl
from jax.experimental.pallas import tpu as pltpu
from jax.sharding import PartitionSpec as P

RADIUS = 7
SCALE_T = 64
SUB = 8
LANES = 128
CORES = 2
VALUES = 14
STATE = slice(0, 5)
INFO = slice(9, 14)
SAVED = 7

sigma_cells = 3.0
prior_var = 4.0


def dynamics():
    q = math.sqrt(3.0) / SCALE_T
    decay = math.exp(-q)
    p0, p1 = prior_var, prior_var * q * q
    prior = (p0, q * p0, q * q * p0 + p1)
    a, b, c = prior
    noise = (
        a - decay**2 * (a + 2.0 * b + c),
        b - decay**2 * (b + c),
        c - decay**2 * c,
    )
    return decay, prior, noise


def taps():
    raw = [math.exp(-o * o / (2.0 * sigma_cells**2)) for o in range(-RADIUS, RADIUS + 1)]
    total = sum(raw)
    return [r / total for r in raw], total


def inverse(x):
    r = pl.reciprocal(x, approx=True)
    return r * (2.0 - x * r)


def absorb(x, y, g):
    x00, x01, x11 = x
    y00, y01, y11 = y
    d00 = 1.0 + (x00 * y00 + x01 * y01)
    d01 = x00 * y01 + x01 * y11
    d10 = x01 * y00 + x11 * y01
    d11 = 1.0 + (x01 * y01 + x11 * y11)
    inv = inverse(d00 * d11 - d01 * d10)
    det = x00 * x11 - x01 * x01
    out = ((x00 + y11 * det) * inv, (x01 - y01 * det) * inv, (x11 + y00 * det) * inv)
    vec = ((d11 * g[0] - d01 * g[1]) * inv, (d00 * g[1] - d10 * g[0]) * inv)
    return out, vec


def congruent(a, s):
    a00, a01, a10, a11 = a
    s00, s01, s11 = s
    u0, u1 = a00 * s00 + a01 * s01, a00 * s01 + a01 * s11
    v0, v1 = a10 * s00 + a11 * s01, a10 * s01 + a11 * s11
    return u0 * a00 + u1 * a01, u0 * a10 + u1 * a11, v0 * a10 + v1 * a11


def symv(s, v):
    return s[0] * v[0] + s[1] * v[1], s[1] * v[0] + s[2] * v[1]


def matv(a, v):
    return a[0] * v[0] + a[1] * v[1], a[2] * v[0] + a[3] * v[1]


def add(*parts):
    return tuple(sum(p[1:], p[0]) for p in zip(*parts))


def carry_state(state, block):
    mean, cov = state[:2], state[2:]
    shift = symv(cov, block[9:11])
    cov, mean = absorb(cov, block[11:14], add(mean, shift))
    a = block[5:9]
    return add(matv(a, mean), block[0:2]) + add(congruent(a, cov), block[2:5])


def carry_info(block, info):
    vec, mat = info[:2], info[2:]
    pulled = symv(mat, block[0:2])
    s, v = absorb(mat, block[2:5], (vec[0] - pulled[0], vec[1] - pulled[1]))
    a00, a01, a10, a11 = block[5:9]
    back = (a00, a10, a01, a11)
    return add(matv(back, v), block[9:11]) + add(congruent(back, s), block[11:14])


def join(one, two):
    state = carry_state(one[0:5], two)
    info = carry_info(one, two[9:14])
    c, j = one[2:5], two[11:14]
    d00 = 1.0 + (c[0] * j[0] + c[1] * j[1])
    d01 = c[0] * j[1] + c[1] * j[2]
    d10 = c[1] * j[0] + c[2] * j[1]
    d11 = 1.0 + (c[1] * j[1] + c[2] * j[2])
    inv = inverse(d00 * d11 - d01 * d10)
    a00, a01, a10, a11 = one[5:9]
    m = (
        (d11 * a00 - d01 * a10) * inv,
        (d11 * a01 - d01 * a11) * inv,
        (d00 * a10 - d10 * a00) * inv,
        (d00 * a11 - d10 * a01) * inv,
    )
    b00, b01, b10, b11 = two[5:9]
    a = (
        b00 * m[0] + b01 * m[2],
        b00 * m[1] + b01 * m[3],
        b10 * m[0] + b11 * m[2],
        b10 * m[1] + b11 * m[3],
    )
    return state + a + info


def kernel(tm_count, space_count, hits_hbm, misses_hbm, landed, hits, misses, chan, field,
           give, obs, elem, incl, got, pre, suf, after, saved, res, load, halo_send, halo_recv,
           pair_send, pair_recv, level_send, level_recv, res_send, res_recv):
    frames, rows, cols = hits.shape
    parts = ((slice(0, SUB), slice(rows - SUB, rows)), (slice(SUB, rows - SUB),))

    def loads(part):
        return [pltpu.make_async_copy(src.at[:, cut, :], dst.at[:, cut, :], load.at[k, part, j])
                for j, cut in enumerate(parts[part])
                for k, (src, dst) in enumerate(((hits_hbm, hits), (misses_hbm, misses)))]

    for part in range(2):
        for copy in loads(part):
            copy.start()
    span = CORES * frames
    chips = tm_count // CORES
    levels = chips.bit_length() - 1
    me = lax.axis_index("tm")
    tile = lax.axis_index("space")
    chip, core = me // CORES, me % CORES
    partner = me + 1 - 2 * core
    decay, prior, noise = dynamics()
    weights, total = taps()
    has_up = tile > 0
    has_down = tile < space_count - 1
    barrier = pltpu.get_barrier_semaphore()

    @pl.when(has_up)
    def _():
        pl.semaphore_signal(barrier, inc=1, device_id={"space": tile - 1})
        pl.semaphore_signal(barrier, inc=1, device_id={"tm": partner, "space": tile - 1})

    @pl.when(has_down)
    def _():
        pl.semaphore_signal(barrier, inc=1, device_id={"space": tile + 1})
        pl.semaphore_signal(barrier, inc=1, device_id={"tm": partner, "space": tile + 1})

    pl.semaphore_signal(barrier, inc=1, device_id={"tm": partner})

    def greet(k, carry):
        pl.semaphore_signal(barrier, inc=1,
                            device_id={"tm": CORES * ((chip + k) % chips) + core})
        return carry

    lax.fori_loop(1, chips, greet, 0)

    own = pl.ds(core * frames, frames)
    other = pl.ds((1 - core) * frames, frames)
    cells = (2 * SUB, LANES)

    @pl.when(jnp.logical_not(has_up))
    def _():
        field[:, :, 0:SUB, :] = jnp.zeros((2, span, SUB, LANES), jnp.float32)

    @pl.when(jnp.logical_not(has_down))
    def _():
        field[:, :, SUB + rows :, :] = jnp.zeros((2, span, SUB, LANES), jnp.float32)

    @pl.when(chip == 0)
    def _():
        for p in range(2):
            for k, value in enumerate((0.0, 0.0) + prior):
                pre[p, k] = jnp.full(cells, value, jnp.float32)

    @pl.when(chip == chips - 1)
    def _():
        suf[:, INFO] = jnp.zeros((2, 5) + cells, jnp.float32)

    column = lax.broadcasted_iota(jnp.int32, (cols, cols), 1) + core * LANES
    column = jnp.where(column >= cols, column - cols, column)
    offset = lax.broadcasted_iota(jnp.int32, (cols, cols), 0) - column
    far = offset.astype(jnp.float32)
    band = jnp.where(jnp.abs(offset) <= RADIUS,
                     jnp.exp(-far * far / (2.0 * sigma_cells**2)) / total, 0.0)
    band_high = band.astype(jnp.bfloat16)
    band_low = (band - band_high.astype(jnp.float32)).astype(jnp.bfloat16)

    late = core.astype(jnp.float32)
    base = 1.0 + late * (decay**frames - 1.0)
    base2 = 1.0 + late * (decay ** (2 * frames) - 1.0)
    dot = functools.partial(jnp.dot, preferred_element_type=jnp.float32)

    def prepare(part):
        for copy in loads(part):
            copy.wait()
        for cut in parts[part]:
            size = cut.stop - cut.start
            for f in range(frames):
                h, m = hits[f, cut, :], misses[f, cut, :]
                hp = h.astype(jnp.float32) + 1.0
                mp = m.astype(jnp.float32) + 1.0
                inv = inverse(hp + mp)
                weight = (h + m).astype(jnp.float32) * (hp * inv) * (mp * inv)
                chan[0, f, cut, :] = weight * (jnp.log(hp) - jnp.log(mp)) * (base * decay**f)
                chan[1, f, cut, :] = weight * (base2 * decay ** (2 * f))
        for cut in parts[part]:
            size = cut.stop - cut.start
            flat = chan[:, :, cut, :].reshape(2 * frames * size, cols)
            high = flat.astype(jnp.bfloat16)
            low = (flat - high.astype(jnp.float32)).astype(jnp.bfloat16)
            out = dot(high, band_high) + (dot(low, band_high) + dot(high, band_low))
            out = out.reshape(2, frames, size, cols)
            field[:, own, SUB + cut.start : SUB + cut.stop, :] = out[..., :LANES]
            give[:, :, cut, :] = out[..., LANES:]

    prepare(0)
    neighbours = has_up.astype(jnp.int32) + has_down.astype(jnp.int32)
    pl.semaphore_wait(barrier, chips + 2 * neighbours)

    top, bottom = pl.ds(SUB - RADIUS, RADIUS), pl.ds(SUB + rows, RADIUS)

    def halo(direction, crossed):
        step = 1 - 2 * direction
        where = bottom if direction else top
        if crossed:
            row = pl.ds(0, RADIUS) if direction else pl.ds(rows - RADIUS, RADIUS)
            source, target = give.at[:, :, row, :], {"tm": partner, "space": tile + step}
        else:
            row = pl.ds(SUB, RADIUS) if direction else pl.ds(SUB + rows - RADIUS, RADIUS)
            source, target = field.at[:, own, row, :], {"space": tile + step}
        return pltpu.make_async_remote_copy(
            src_ref=source, dst_ref=field.at[:, own, where, :],
            send_sem=halo_send.at[direction, crossed],
            recv_sem=halo_recv.at[direction, core], device_id=target)

    def halo_arrived(direction, sender):
        where = bottom if direction else top
        part = field.at[:, pl.ds(sender * frames, frames), where, :]
        pltpu.make_async_remote_copy(
            src_ref=part, dst_ref=part, send_sem=halo_send.at[direction, 0],
            recv_sem=halo_recv.at[direction, sender], device_id={"tm": partner}).wait_recv()

    for direction, there in ((0, has_down), (1, has_up)):
        @pl.when(there)
        def _():
            for crossed in range(2):
                halo(direction, crossed).start()

    prepare(1)
    to_partner = pltpu.make_async_remote_copy(
        src_ref=give, dst_ref=field.at[:, own, pl.ds(SUB, rows), :],
        send_sem=pair_send.at[0], recv_sem=pair_recv.at[0], device_id={"tm": partner})
    to_partner.start()

    phases = (tuple(range(1, rows // SUB - 1)), (0, rows // SUB - 1))

    def down(c, t, group):
        def at(s):
            first = group * SUB + SUB - RADIUS + s
            return field[c, t, first : first + SUB, :]

        out = weights[RADIUS] * at(RADIUS)
        for s in range(RADIUS):
            out = out + weights[s] * (at(s) + at(2 * RADIUS - s))
        return out

    first = (chip == 0).astype(jnp.float32)

    def scaled_noise(t):
        return tuple(v * decay ** (-2 * (t + 1)) for v in noise)

    def summary(p):
        zero = jnp.zeros(cells, jnp.float32)
        m0 = m1 = a01 = c0 = eta0 = eta1 = j00 = j01 = j11 = zero
        a00 = c1 = zero + 1.0
        p00, p01, p11 = (zero + v * first for v in prior)
        for t in range(span):
            for c in range(2):
                for k, group in enumerate(phases[p]):
                    obs[p, c, t, k * SUB : k * SUB + SUB, :] = down(c, t, group)
            num, den = obs[p, 0, t], obs[p, 1, t]
            inv = inverse(1.0 + p00 * den)
            w = den * inv
            e = (num - den * m0) * inv
            k1 = p01 * w
            m0, m1 = m0 + p00 * e, m1 + p01 * e
            p11 = p11 - k1 * p01
            p00, p01 = p00 * inv, p01 * inv
            eta0, eta1 = eta0 + a00 * e, eta1 + a01 * e
            w0, w1 = w * a00, w * a01
            j00, j01, j11 = j00 + w0 * a00, j01 + w0 * a01, j11 + w1 * a01
            c0, c1 = c0 - k1 * a00, c1 - k1 * a01
            a00, a01 = a00 * inv, a01 * inv
            q00, q01, q11 = scaled_noise(t)
            m0 = m0 + m1
            a00, a01 = a00 + c0, a01 + c1
            r = p01 + p11
            p00, p01, p11 = (p00 + p01) + (r + q00), r + q01, p11 + q11
        s, s2 = decay**span, decay ** (2 * span)
        block = (m0 * s, m1 * s, p00 * s2, p01 * s2, p11 * s2,
                 a00 * s, a01 * s, c0 * s, c1 * s, eta0, eta1, j00, j01, j11)
        for k, value in enumerate(block):
            elem[p, k] = value

    def values(ref, part):
        return tuple(ref[k] for k in range(part.start, part.stop))

    def put(ref, part, items):
        for k, item in zip(range(part.start, part.stop), items):
            ref[k] = item

    full = slice(0, VALUES)

    def level_copy(p, level, d, target, part):
        src = elem.at[p] if level == 0 else incl.at[p, level - 1]
        cut = pl.ds(part.start, part.stop - part.start)
        return pltpu.make_async_remote_copy(
            src_ref=src.at[cut], dst_ref=got.at[p, level, cut],
            send_sem=level_send.at[p, level, d], recv_sem=level_recv.at[p, level],
            device_id={"tm": CORES * target + core})

    def branches(level):
        size = 1 << level
        ends = chip % (2 * size) == size - 1
        starts = chip % (2 * size) == size
        if chips == 2 * size:
            return ((ends, STATE),), ((starts, INFO),)
        lone = chip == size - 1
        last = chip == chips - size
        return (((lone, STATE), (jnp.logical_and(ends, jnp.logical_not(lone)), full)),
                ((last, INFO), (jnp.logical_and(starts, jnp.logical_not(last)), full)))

    def each_send(p, level, act):
        size = 1 << level
        lefts, rights = branches(level)
        for group, step in ((lefts, 1), (rights, -1)):
            for condition, part in group:
                @pl.when(condition)
                def _():
                    for d in range(size):
                        act(level_copy(p, level, d, chip + step * (d + 1), part))

    def send_level(p, level):
        if level:
            out = incl.at[p, level - 1]
            lefts, rights = branches(level)
            for condition, part in lefts:
                @pl.when(condition)
                def _():
                    one, two = values(pre.at[p], part), values(elem.at[p], full)
                    put(out, part, carry_state(one, two) if part is STATE else join(one, two))
            for condition, part in rights:
                @pl.when(condition)
                def _():
                    one, two = values(elem.at[p], full), values(suf.at[p], part)
                    put(out, part, carry_info(one, two) if part is INFO else join(one, two))
        each_send(p, level, lambda copy: copy.start())

    def take_level(p, level):
        size = 1 << level
        right = (chip // size) % 2 == 1
        left = jnp.logical_not(right)
        if chips == 2 * size:
            cases = ((right, STATE, True), (left, INFO, False))
        else:
            low, high = chip < 2 * size, chip >= chips - 2 * size
            cases = (
                (jnp.logical_and(right, low), STATE, True),
                (jnp.logical_and(right, jnp.logical_not(low)), full, True),
                (jnp.logical_and(left, high), INFO, False),
                (jnp.logical_and(left, jnp.logical_not(high)), full, False),
            )
        for condition, part, earlier in cases:
            @pl.when(condition)
            def _():
                level_copy(p, level, 0, chip, part).wait_recv()
                bare = chip % size == (0 if earlier else size - 1)
                mine = pre.at[p] if earlier else suf.at[p]

                def keep():
                    put(mine, part, values(got.at[p, level], part))

                def merge():
                    new = values(got.at[p, level], part)
                    old = values(mine, full)
                    if part is STATE:
                        put(mine, part, carry_state(new, old))
                    elif part is INFO:
                        put(mine, part, carry_info(old, new))
                    else:
                        put(mine, part, join(new, old) if earlier else join(old, new))

                if size == 1:
                    keep()
                else:
                    pl.when(bare)(keep)
                    pl.when(jnp.logical_not(bare))(merge)

    hops = (((1, STATE), (3, STATE)), ((0, full), (3, full)), ((0, full), (3, full)), ((0, INFO), (2, INFO)))

    def direct_copy(p, sender, d, relayed=False):
        if relayed:
            src, target, part = incl.at[p, 0], 3 - sender, STATE if sender == 1 else INFO
        else:
            src, (target, part) = elem.at[p], hops[sender][d]
        cut = pl.ds(part.start, part.stop - part.start)
        return pltpu.make_async_remote_copy(
            src_ref=src.at[cut], dst_ref=got.at[p, sender, cut],
            send_sem=level_send.at[p, d], recv_sem=level_recv.at[p, sender],
            device_id={"tm": CORES * target + core})

    def direct_each(p, act):
        for sender in range(4):
            @pl.when(chip == sender)
            def _():
                for d in range(2):
                    act(direct_copy(p, sender, d))

    def arrive(p, sender, part):
        cut = pl.ds(part.start, part.stop - part.start)
        block = got.at[p, sender, cut]
        pltpu.make_async_remote_copy(
            src_ref=block, dst_ref=block, send_sem=level_send.at[p, 0],
            recv_sem=level_recv.at[p, sender], device_id={"tm": partner}).wait_recv()
        return values(got.at[p, sender], part)

    def relay():
        @pl.when(chip == 1)
        def _():
            def step(p, carry):
                state = arrive(p, 0, STATE)
                put(pre.at[p], STATE, state)
                put(incl.at[p, 0], STATE, carry_state(state, values(elem.at[p], full)))
                direct_copy(p, 1, 2, True).start()
                return carry

            lax.fori_loop(0, 2, step, 0)

        @pl.when(chip == 2)
        def _():
            def step(p, carry):
                info = arrive(p, 3, INFO)
                put(suf.at[p], INFO, info)
                put(incl.at[p, 0], INFO, carry_info(values(elem.at[p], full), info))
                direct_copy(p, 2, 2, True).start()
                return carry

            lax.fori_loop(0, 2, step, 0)

    def collect(p):
        @pl.when(chip == 0)
        def _():
            info = arrive(p, 3, INFO)
            info = carry_info(arrive(p, 2, full), info)
            put(suf.at[p], INFO, carry_info(arrive(p, 1, full), info))

        @pl.when(chip == 1)
        def _():
            put(suf.at[p], INFO, arrive(p, 2, INFO))

        @pl.when(chip == 2)
        def _():
            put(pre.at[p], STATE, arrive(p, 1, STATE))

        @pl.when(chip == 3)
        def _():
            state = arrive(p, 0, STATE)
            state = carry_state(state, arrive(p, 1, full))
            put(pre.at[p], STATE, carry_state(state, arrive(p, 2, full)))

    def direct_sent(p):
        direct_each(p, lambda copy: copy.wait_send())
        for sender in (1, 2):
            @pl.when(chip == sender)
            def _():
                direct_copy(p, sender, 2, True).wait_send()

    def for_phases(act):
        def step(p, carry):
            act(p)
            return carry

        lax.fori_loop(0, 2, step, 0)

    def forward(p):
        m0, m1, p00, p01, p11 = values(pre.at[p], STATE)
        for t in range(span):
            num, den = obs[p, 0, t], obs[p, 1, t]
            inv = inverse(1.0 + p00 * den)
            w = den * inv
            e = (num - den * m0) * inv
            k1 = p01 * w
            m0, m1 = m0 + p00 * e, m1 + p01 * e
            p11 = p11 - k1 * p01
            p00, p01 = p00 * inv, p01 * inv
            for slot, value in enumerate((inv, w, e, k1, m0, p00, p01)):
                saved[p, t, slot] = value
            q00, q01, q11 = scaled_noise(t)
            m0 = m0 + m1
            r = p01 + p11
            p00, p01, p11 = (p00 + p01) + (r + q00), r + q01, p11 + q11

        put(after.at[p], STATE, (m0, m1, p00, p01, p11))

    half = pl.ds(pl.multiple_of(core * LANES, LANES), LANES)

    def result_copy(p, k):
        row = pl.multiple_of(((1 - p) * (1 + k) + p * k * (rows // SUB - 1)) * SUB, SUB)
        return pltpu.make_async_remote_copy(
            src_ref=res.at[p, :, other, k * SUB : k * SUB + SUB, :],
            dst_ref=landed.at[:, :, pl.ds(row, SUB), half],
            send_sem=res_send.at[p, k], recv_sem=res_recv.at[p, k], device_id={"tm": partner})

    def backward(p):
        i0, i1, i00, i01, i11 = values(suf.at[p], INFO)
        m0, m1, p00, p01, p11 = values(after.at[p], STATE)
        s, s2 = decay**span, decay ** (2 * span)
        mat = (i00 * s2, i01 * s2, i11 * s2)
        pulled = symv(mat, (m0, m1))
        (n00, n01, n11), (u0, u1) = absorb(mat, (p00, p01, p11),
                                           (i0 * s - pulled[0], i1 * s - pulled[1]))
        for t in reversed(range(span)):
            u1 = u0 + u1
            both = n00 + n01
            n01, n11 = both, both + (n01 + n11)
            inv, w, e, k1, m0, p00, p01 = (saved[p, t, slot] for slot in range(SAVED))
            mean = m0 + p00 * u0 + p01 * u1
            g0, g1 = p00 * n00 + p01 * n01, p00 * n01 + p01 * n11
            res[p, 0, t] = inverse(1.0 + jnp.exp(mean * -(decay**t)))
            res[p, 1, t] = (p00 - (p00 * g0 + p01 * g1)) * decay ** (2 * t)
            u0 = e + inv * u0 - k1 * u1
            l01 = inv * n01 - k1 * n11
            n00 = w + inv * (inv * n00 - k1 * n01) - k1 * l01
            n01 = l01
            if t == 0 or t == frames:
                @pl.when(core == (1 if t == 0 else 0))
                def _():
                    for k in range(2):
                        result_copy(p, k).start()
        for k in range(2):
            row = pl.multiple_of(((1 - p) * (1 + k) + p * k * (rows // SUB - 1)) * SUB, SUB)
            landed[:, :, pl.ds(row, SUB), half] = res[p, :, own, k * SUB : k * SUB + SUB, :]

    to_partner.wait_recv()
    summary(0)
    if chips == 4:
        direct_each(0, lambda copy: copy.start())
    else:
        send_level(0, 0)
    for direction, there in ((0, has_up), (1, has_down)):
        @pl.when(there)
        def _():
            for sender in range(CORES):
                halo_arrived(direction, sender)
    summary(1)
    if chips == 4:
        direct_each(1, lambda copy: copy.start())
        relay()

        @pl.when(chip < 2)
        def _():
            for_phases(forward)
    else:
        send_level(1, 0)
        for level in range(levels):
            for p in range(2):
                take_level(p, level)
                if level + 1 < levels:
                    send_level(p, level + 1)

    def finish(p):
        if chips == 4:
            collect(p)
            pl.when(chip >= 2)(functools.partial(forward, p))
        else:
            forward(p)
        backward(p)

    for_phases(finish)
    for p in range(2):
        for k in range(2):
            result_copy(p, k).wait_recv()
    for p in range(2):
        for k in range(2):
            result_copy(p, k).wait_send()
        if chips == 4:
            direct_sent(p)
        else:
            for level in range(levels):
                each_send(p, level, lambda copy: copy.wait_send())
    for direction, there in ((0, has_down), (1, has_up)):
        @pl.when(there)
        def _():
            for crossed in range(2):
                halo(direction, crossed).wait_send()
    to_partner.wait_send()


def hand_out(landed, occupancy, spread, sems):
    copies = [pltpu.make_async_copy(landed.at[k], out, sems.at[k])
              for k, out in enumerate((occupancy, spread))]
    for copy in copies:
        copy.start()
    for copy in copies:
        copy.wait()


def solution(mesh):
    tm_count, space_count = mesh.shape["tm"], mesh.shape["space"]

    def body(hits, misses):
        frames, rows, cols = hits.shape
        span, chips = CORES * frames, tm_count // CORES
        levels = chips.bit_length() - 1
        cells = (2 * SUB, LANES)
        assert rows == 4 * SUB and cols == CORES * LANES and chips == 1 << levels
        f32 = jnp.float32
        hbm = pl.BlockSpec(memory_space=pltpu.HBM)
        vmem = pl.BlockSpec(memory_space=pltpu.VMEM)
        dma = pltpu.SemaphoreType.DMA
        landed = pl.pallas_call(
            functools.partial(kernel, tm_count, space_count),
            out_shape=pltpu.VMEM((2, frames, rows, cols), f32),
            in_specs=[hbm] * 2,
            out_specs=vmem,
            scratch_shapes=[
                pltpu.VMEM(hits.shape, jnp.int32),
                pltpu.VMEM(hits.shape, jnp.int32),
                pltpu.VMEM((2, frames, rows, cols), f32),
                pltpu.VMEM((2, span, rows + 2 * SUB, LANES), f32),
                pltpu.VMEM((2, frames, rows, LANES), f32),
                pltpu.VMEM((2, 2, span) + cells, f32),
                pltpu.VMEM((2, VALUES) + cells, f32),
                pltpu.VMEM((2, max(levels - 1, 1), VALUES) + cells, f32),
                pltpu.VMEM((2, max(levels, 4), VALUES) + cells, f32),
                pltpu.VMEM((2, VALUES) + cells, f32),
                pltpu.VMEM((2, VALUES) + cells, f32),
                pltpu.VMEM((2, 5) + cells, f32),
                pltpu.VMEM((2, span, SAVED) + cells, f32),
                pltpu.VMEM((2, 2, span) + cells, f32),
                dma((2, 2, 2)),
                dma((2, 2)),
                dma((2, 2)),
                dma((1,)),
                dma((1,)),
                dma((2, 3) if chips == 4 else (2, levels, chips // 2)),
                dma((2, max(levels, 4))),
                dma((2, 2)),
                dma((2, 2)),
            ],
            compiler_params=pltpu.CompilerParams(
                collective_id=0, has_side_effects=True, vmem_limit_bytes=32 * 1024 * 1024),
        )(pltpu.with_memory_space_constraint(hits, pltpu.HBM),
          pltpu.with_memory_space_constraint(misses, pltpu.HBM))
        out = jax.ShapeDtypeStruct(hits.shape, f32)
        return pl.pallas_call(
            hand_out,
            out_shape=(out, out),
            in_specs=[vmem],
            out_specs=(hbm, hbm),
            scratch_shapes=[dma((2,))],
            compiler_params=pltpu.CompilerParams(vmem_limit_bytes=8 * 1024 * 1024),
        )(landed)

    placed = P("tm", "space", None)
    return jax.shard_map(body, mesh=mesh, in_specs=(placed, placed),
                         out_specs=(placed, placed), check_vma=False)
```

```python
import functools
import math

import jax
import jax.numpy as jnp
from jax import lax
from jax.experimental import pallas as pl
from jax.experimental.pallas import tpu as pltpu
from jax.sharding import PartitionSpec as P

RADIUS = 7
SCALE_T = 64
SUB = 8
LANES = 128
CORES = 2
VALUES = 14
STATE = slice(0, 5)
INFO = slice(9, 14)
SAVED = 7
GREETED = ((1, 2, 3), (3,), (3,), (1, 2))

sigma_cells = 3.0
prior_var = 4.0


def dynamics():
    q = math.sqrt(3.0) / SCALE_T
    decay = math.exp(-q)
    p0, p1 = prior_var, prior_var * q * q
    prior = (p0, q * p0, q * q * p0 + p1)
    a, b, c = prior
    noise = (
        a - decay**2 * (a + 2.0 * b + c),
        b - decay**2 * (b + c),
        c - decay**2 * c,
    )
    return decay, prior, noise


def taps():
    raw = [math.exp(-o * o / (2.0 * sigma_cells**2)) for o in range(-RADIUS, RADIUS + 1)]
    total = sum(raw)
    return [r / total for r in raw], total


def inverse(x):
    r = pl.reciprocal(x, approx=True)
    return r * (2.0 - x * r)


def absorb(x, y, g):
    x00, x01, x11 = x
    y00, y01, y11 = y
    d00 = 1.0 + (x00 * y00 + x01 * y01)
    d01 = x00 * y01 + x01 * y11
    d10 = x01 * y00 + x11 * y01
    d11 = 1.0 + (x01 * y01 + x11 * y11)
    inv = inverse(d00 * d11 - d01 * d10)
    det = x00 * x11 - x01 * x01
    out = ((x00 + y11 * det) * inv, (x01 - y01 * det) * inv, (x11 + y00 * det) * inv)
    vec = ((d11 * g[0] - d01 * g[1]) * inv, (d00 * g[1] - d10 * g[0]) * inv)
    return out, vec


def congruent(a, s):
    a00, a01, a10, a11 = a
    s00, s01, s11 = s
    u0, u1 = a00 * s00 + a01 * s01, a00 * s01 + a01 * s11
    v0, v1 = a10 * s00 + a11 * s01, a10 * s01 + a11 * s11
    return u0 * a00 + u1 * a01, u0 * a10 + u1 * a11, v0 * a10 + v1 * a11


def symv(s, v):
    return s[0] * v[0] + s[1] * v[1], s[1] * v[0] + s[2] * v[1]


def matv(a, v):
    return a[0] * v[0] + a[1] * v[1], a[2] * v[0] + a[3] * v[1]


def add(*parts):
    return tuple(sum(p[1:], p[0]) for p in zip(*parts))


def carry_state(state, block):
    mean, cov = state[:2], state[2:]
    shift = symv(cov, block[9:11])
    cov, mean = absorb(cov, block[11:14], add(mean, shift))
    a = block[5:9]
    return add(matv(a, mean), block[0:2]) + add(congruent(a, cov), block[2:5])


def carry_info(block, info):
    vec, mat = info[:2], info[2:]
    pulled = symv(mat, block[0:2])
    s, v = absorb(mat, block[2:5], (vec[0] - pulled[0], vec[1] - pulled[1]))
    a00, a01, a10, a11 = block[5:9]
    back = (a00, a10, a01, a11)
    return add(matv(back, v), block[9:11]) + add(congruent(back, s), block[11:14])


def join(one, two):
    state = carry_state(one[0:5], two)
    info = carry_info(one, two[9:14])
    c, j = one[2:5], two[11:14]
    d00 = 1.0 + (c[0] * j[0] + c[1] * j[1])
    d01 = c[0] * j[1] + c[1] * j[2]
    d10 = c[1] * j[0] + c[2] * j[1]
    d11 = 1.0 + (c[1] * j[1] + c[2] * j[2])
    inv = inverse(d00 * d11 - d01 * d10)
    a00, a01, a10, a11 = one[5:9]
    m = (
        (d11 * a00 - d01 * a10) * inv,
        (d11 * a01 - d01 * a11) * inv,
        (d00 * a10 - d10 * a00) * inv,
        (d00 * a11 - d10 * a01) * inv,
    )
    b00, b01, b10, b11 = two[5:9]
    a = (
        b00 * m[0] + b01 * m[2],
        b00 * m[1] + b01 * m[3],
        b10 * m[0] + b11 * m[2],
        b10 * m[1] + b11 * m[3],
    )
    return state + a + info


def kernel(tm_count, space_count, hits_hbm, misses_hbm, landed, hits, misses, chan, field,
           give, obs, elem, incl, got, pre, suf, after, saved, res, load, halo_send, halo_recv,
           pair_send, pair_recv, level_send, level_recv, res_send, res_recv, hello):
    frames, rows, cols = hits.shape
    parts = ((slice(0, SUB), slice(rows - SUB, rows)), (slice(SUB, rows - SUB),))

    def loads(part):
        return [pltpu.make_async_copy(src.at[:, cut, :], dst.at[:, cut, :], load.at[k, part, j])
                for j, cut in enumerate(parts[part])
                for k, (src, dst) in enumerate(((hits_hbm, hits), (misses_hbm, misses)))]

    for part in range(2):
        for copy in loads(part):
            copy.start()
    span = CORES * frames
    chips = tm_count // CORES
    levels = chips.bit_length() - 1
    me = lax.axis_index("tm")
    tile = lax.axis_index("space")
    chip, core = me // CORES, me % CORES
    partner = me + 1 - 2 * core
    decay, prior, noise = dynamics()
    weights, total = taps()
    has_up = tile > 0
    has_down = tile < space_count - 1
    barrier = pltpu.get_barrier_semaphore()

    @pl.when(has_up)
    def _():
        pl.semaphore_signal(barrier, inc=1, device_id={"space": tile - 1})
        pl.semaphore_signal(barrier, inc=1, device_id={"tm": partner, "space": tile - 1})

    @pl.when(has_down)
    def _():
        pl.semaphore_signal(barrier, inc=1, device_id={"space": tile + 1})
        pl.semaphore_signal(barrier, inc=1, device_id={"tm": partner, "space": tile + 1})

    pl.semaphore_signal(barrier, inc=1, device_id={"tm": partner})

    if chips == 4:
        for sender, targets in enumerate(GREETED):
            @pl.when(chip == sender)
            def _():
                for target in targets:
                    pl.semaphore_signal(barrier, inc=1, device_id={"tm": CORES * target + core})

        greetings = (chip > 0).astype(jnp.int32) * 2 + (chip == 3).astype(jnp.int32)
    else:
        def greet(k, carry):
            pl.semaphore_signal(barrier, inc=1,
                                device_id={"tm": CORES * ((chip + k) % chips) + core})
            return carry

        lax.fori_loop(1, chips, greet, 0)
        greetings = chips - 1

    own = pl.ds(core * frames, frames)
    other = pl.ds((1 - core) * frames, frames)
    cells = (2 * SUB, LANES)

    @pl.when(jnp.logical_not(has_up))
    def _():
        field[:, :, 0:SUB, :] = jnp.zeros((2, span, SUB, LANES), jnp.float32)

    @pl.when(jnp.logical_not(has_down))
    def _():
        field[:, :, SUB + rows :, :] = jnp.zeros((2, span, SUB, LANES), jnp.float32)

    @pl.when(chip == 0)
    def _():
        for p in range(2):
            for k, value in enumerate((0.0, 0.0) + prior):
                pre[p, k] = jnp.full(cells, value, jnp.float32)

    @pl.when(chip == chips - 1)
    def _():
        suf[:, INFO] = jnp.zeros((2, 5) + cells, jnp.float32)

    column = lax.broadcasted_iota(jnp.int32, (cols, cols), 1) + core * LANES
    column = jnp.where(column >= cols, column - cols, column)
    offset = lax.broadcasted_iota(jnp.int32, (cols, cols), 0) - column
    far = offset.astype(jnp.float32)
    band = jnp.where(jnp.abs(offset) <= RADIUS,
                     jnp.exp(-far * far / (2.0 * sigma_cells**2)) / total, 0.0)
    band_high = band.astype(jnp.bfloat16)
    band_low = (band - band_high.astype(jnp.float32)).astype(jnp.bfloat16)

    late = core.astype(jnp.float32)
    base = 1.0 + late * (decay**frames - 1.0)
    base2 = 1.0 + late * (decay ** (2 * frames) - 1.0)
    dot = functools.partial(jnp.dot, preferred_element_type=jnp.float32)

    def prepare(part):
        for copy in loads(part):
            copy.wait()
        for cut in parts[part]:
            size = cut.stop - cut.start
            for f in range(frames):
                h, m = hits[f, cut, :], misses[f, cut, :]
                hp = h.astype(jnp.float32) + 1.0
                mp = m.astype(jnp.float32) + 1.0
                inv = inverse(hp + mp)
                weight = (h + m).astype(jnp.float32) * (hp * inv) * (mp * inv)
                chan[0, f, cut, :] = weight * (jnp.log(hp) - jnp.log(mp)) * (base * decay**f)
                chan[1, f, cut, :] = weight * (base2 * decay ** (2 * f))
        for cut in parts[part]:
            size = cut.stop - cut.start
            flat = chan[:, :, cut, :].reshape(2 * frames * size, cols)
            high = flat.astype(jnp.bfloat16)
            low = (flat - high.astype(jnp.float32)).astype(jnp.bfloat16)
            out = dot(high, band_high) + (dot(low, band_high) + dot(high, band_low))
            out = out.reshape(2, frames, size, cols)
            field[:, own, SUB + cut.start : SUB + cut.stop, :] = out[..., :LANES]
            give[:, :, cut, :] = out[..., LANES:]

    prepare(0)
    neighbours = has_up.astype(jnp.int32) + has_down.astype(jnp.int32)
    pl.semaphore_wait(barrier, 1 + greetings + 2 * neighbours)

    top, bottom = pl.ds(SUB - RADIUS, RADIUS), pl.ds(SUB + rows, RADIUS)

    def halo(direction, crossed):
        step = 1 - 2 * direction
        where = bottom if direction else top
        if crossed:
            row = pl.ds(0, RADIUS) if direction else pl.ds(rows - RADIUS, RADIUS)
            source, target = give.at[:, :, row, :], {"tm": partner, "space": tile + step}
        else:
            row = pl.ds(SUB, RADIUS) if direction else pl.ds(SUB + rows - RADIUS, RADIUS)
            source, target = field.at[:, own, row, :], {"space": tile + step}
        return pltpu.make_async_remote_copy(
            src_ref=source, dst_ref=field.at[:, own, where, :],
            send_sem=halo_send.at[direction, crossed],
            recv_sem=halo_recv.at[direction, core], device_id=target)

    def halo_arrived(direction, sender):
        where = bottom if direction else top
        part = field.at[:, pl.ds(sender * frames, frames), where, :]
        pltpu.make_async_remote_copy(
            src_ref=part, dst_ref=part, send_sem=halo_send.at[direction, 0],
            recv_sem=halo_recv.at[direction, sender], device_id={"tm": partner}).wait_recv()

    for direction, there in ((0, has_down), (1, has_up)):
        @pl.when(there)
        def _():
            for crossed in range(2):
                halo(direction, crossed).start()

    if chips == 4:
        @pl.when(chip > 0)
        def _():
            pl.semaphore_signal(hello.at[0], inc=1, device_id={"tm": core})

    prepare(1)
    to_partner = pltpu.make_async_remote_copy(
        src_ref=give, dst_ref=field.at[:, own, pl.ds(SUB, rows), :],
        send_sem=pair_send.at[0], recv_sem=pair_recv.at[0], device_id={"tm": partner})
    to_partner.start()

    phases = (tuple(range(1, rows // SUB - 1)), (0, rows // SUB - 1))

    def down(c, t, group):
        def at(s):
            first = group * SUB + SUB - RADIUS + s
            return field[c, t, first : first + SUB, :]

        out = weights[RADIUS] * at(RADIUS)
        for s in range(RADIUS):
            out = out + weights[s] * (at(s) + at(2 * RADIUS - s))
        return out

    first = (chip == 0).astype(jnp.float32)

    def scaled_noise(t):
        return tuple(v * decay ** (-2 * (t + 1)) for v in noise)

    def summary(p):
        zero = jnp.zeros(cells, jnp.float32)
        m0 = m1 = a01 = c0 = eta0 = eta1 = j00 = j01 = j11 = zero
        a00 = c1 = zero + 1.0
        p00, p01, p11 = (zero + v * first for v in prior)
        for t in range(span):
            for c in range(2):
                for k, group in enumerate(phases[p]):
                    obs[p, c, t, k * SUB : k * SUB + SUB, :] = down(c, t, group)
            num, den = obs[p, 0, t], obs[p, 1, t]
            inv = inverse(1.0 + p00 * den)
            w = den * inv
            e = (num - den * m0) * inv
            k1 = p01 * w
            m0, m1 = m0 + p00 * e, m1 + p01 * e
            p11 = p11 - k1 * p01
            p00, p01 = p00 * inv, p01 * inv
            eta0, eta1 = eta0 + a00 * e, eta1 + a01 * e
            w0, w1 = w * a00, w * a01
            j00, j01, j11 = j00 + w0 * a00, j01 + w0 * a01, j11 + w1 * a01
            c0, c1 = c0 - k1 * a00, c1 - k1 * a01
            a00, a01 = a00 * inv, a01 * inv
            q00, q01, q11 = scaled_noise(t)
            m0 = m0 + m1
            a00, a01 = a00 + c0, a01 + c1
            r = p01 + p11
            p00, p01, p11 = (p00 + p01) + (r + q00), r + q01, p11 + q11
        s, s2 = decay**span, decay ** (2 * span)
        block = (m0 * s, m1 * s, p00 * s2, p01 * s2, p11 * s2,
                 a00 * s, a01 * s, c0 * s, c1 * s, eta0, eta1, j00, j01, j11)
        for k, value in enumerate(block):
            elem[p, k] = value

    def values(ref, part):
        return tuple(ref[k] for k in range(part.start, part.stop))

    def put(ref, part, items):
        for k, item in zip(range(part.start, part.stop), items):
            ref[k] = item

    full = slice(0, VALUES)

    def level_copy(p, level, d, target, part):
        src = elem.at[p] if level == 0 else incl.at[p, level - 1]
        cut = pl.ds(part.start, part.stop - part.start)
        return pltpu.make_async_remote_copy(
            src_ref=src.at[cut], dst_ref=got.at[p, level, cut],
            send_sem=level_send.at[p, level, d], recv_sem=level_recv.at[p, level],
            device_id={"tm": CORES * target + core})

    def branches(level):
        size = 1 << level
        ends = chip % (2 * size) == size - 1
        starts = chip % (2 * size) == size
        if chips == 2 * size:
            return ((ends, STATE),), ((starts, INFO),)
        lone = chip == size - 1
        last = chip == chips - size
        return (((lone, STATE), (jnp.logical_and(ends, jnp.logical_not(lone)), full)),
                ((last, INFO), (jnp.logical_and(starts, jnp.logical_not(last)), full)))

    def each_send(p, level, act):
        size = 1 << level
        lefts, rights = branches(level)
        for group, step in ((lefts, 1), (rights, -1)):
            for condition, part in group:
                @pl.when(condition)
                def _():
                    for d in range(size):
                        act(level_copy(p, level, d, chip + step * (d + 1), part))

    def send_level(p, level):
        if level:
            out = incl.at[p, level - 1]
            lefts, rights = branches(level)
            for condition, part in lefts:
                @pl.when(condition)
                def _():
                    one, two = values(pre.at[p], part), values(elem.at[p], full)
                    put(out, part, carry_state(one, two) if part is STATE else join(one, two))
            for condition, part in rights:
                @pl.when(condition)
                def _():
                    one, two = values(elem.at[p], full), values(suf.at[p], part)
                    put(out, part, carry_info(one, two) if part is INFO else join(one, two))
        each_send(p, level, lambda copy: copy.start())

    def take_level(p, level):
        size = 1 << level
        right = (chip // size) % 2 == 1
        left = jnp.logical_not(right)
        if chips == 2 * size:
            cases = ((right, STATE, True), (left, INFO, False))
        else:
            low, high = chip < 2 * size, chip >= chips - 2 * size
            cases = (
                (jnp.logical_and(right, low), STATE, True),
                (jnp.logical_and(right, jnp.logical_not(low)), full, True),
                (jnp.logical_and(left, high), INFO, False),
                (jnp.logical_and(left, jnp.logical_not(high)), full, False),
            )
        for condition, part, earlier in cases:
            @pl.when(condition)
            def _():
                level_copy(p, level, 0, chip, part).wait_recv()
                bare = chip % size == (0 if earlier else size - 1)
                mine = pre.at[p] if earlier else suf.at[p]

                def keep():
                    put(mine, part, values(got.at[p, level], part))

                def merge():
                    new = values(got.at[p, level], part)
                    old = values(mine, full)
                    if part is STATE:
                        put(mine, part, carry_state(new, old))
                    elif part is INFO:
                        put(mine, part, carry_info(old, new))
                    else:
                        put(mine, part, join(new, old) if earlier else join(old, new))

                if size == 1:
                    keep()
                else:
                    pl.when(bare)(keep)
                    pl.when(jnp.logical_not(bare))(merge)

    few = (((1, STATE), (3, STATE)), ((0, full), (3, full)), ((0, full), (3, full)), ((2, INFO), (0, INFO)))
    more = few
    hops = (few, more)
    relays = ((1, 2), (1, 2))

    def tell():
        @pl.when(chip == 0)
        def _():
            pl.semaphore_wait(hello.at[0], 3)
            for target in range(1, 4):
                pl.semaphore_signal(hello.at[0], inc=1, device_id={"tm": CORES * target + core})

    def direct_copy(p, sender, d, relayed=False):
        if relayed:
            src, target, part = incl.at[p, 0], 3 - sender, STATE if sender == 1 else INFO
        else:
            src, (target, part) = elem.at[p], hops[p][sender][d]
        cut = pl.ds(part.start, part.stop - part.start)
        return pltpu.make_async_remote_copy(
            src_ref=src.at[cut], dst_ref=got.at[p, sender, cut],
            send_sem=level_send.at[p, d], recv_sem=level_recv.at[p, sender],
            device_id={"tm": CORES * target + core})

    def direct_each(p, act):
        for sender in range(4):
            @pl.when(chip == sender)
            def _():
                for d in range(len(hops[p][sender])):
                    act(direct_copy(p, sender, d))

    def arrive(p, sender, part):
        cut = pl.ds(part.start, part.stop - part.start)
        block = got.at[p, sender, cut]
        pltpu.make_async_remote_copy(
            src_ref=block, dst_ref=block, send_sem=level_send.at[p, 0],
            recv_sem=level_recv.at[p, sender], device_id={"tm": partner}).wait_recv()
        return values(got.at[p, sender], part)

    def relay(p):
        @pl.when(chip == 1)
        def _():
            state = arrive(p, 0, STATE)
            put(pre.at[p], STATE, state)
            put(incl.at[p, 0], STATE, carry_state(state, values(elem.at[p], full)))
            direct_copy(p, 1, 3, True).start()

        @pl.when(chip == 2)
        def _():
            info = arrive(p, 3, INFO)
            put(suf.at[p], INFO, info)
            if 2 in relays[p]:
                put(incl.at[p, 0], INFO, carry_info(values(elem.at[p], full), info))
                direct_copy(p, 2, 3, True).start()

    def collect(p):
        @pl.when(chip == 0)
        def _():
            info = arrive(p, 3, INFO)
            info = carry_info(arrive(p, 2, full), info)
            put(suf.at[p], INFO, carry_info(arrive(p, 1, full), info))

        @pl.when(chip == 1)
        def _():
            if 2 in relays[p]:
                info = arrive(p, 2, INFO)
            else:
                info = arrive(p, 3, INFO)
                info = carry_info(arrive(p, 2, full), info)
            put(suf.at[p], INFO, info)

        @pl.when(chip == 2)
        def _():
            put(pre.at[p], STATE, arrive(p, 1, STATE))

        @pl.when(chip == 3)
        def _():
            state = arrive(p, 0, STATE)
            state = carry_state(state, arrive(p, 1, full))
            put(pre.at[p], STATE, carry_state(state, arrive(p, 2, full)))

    def direct_sent(p):
        direct_each(p, lambda copy: copy.wait_send())
        for sender in relays[p]:
            @pl.when(chip == sender)
            def _():
                direct_copy(p, sender, 3, True).wait_send()

    def for_phases(act):
        def step(p, carry):
            act(p)
            return carry

        lax.fori_loop(0, 2, step, 0)

    def forward(p):
        m0, m1, p00, p01, p11 = values(pre.at[p], STATE)
        for t in range(span):
            num, den = obs[p, 0, t], obs[p, 1, t]
            inv = inverse(1.0 + p00 * den)
            w = den * inv
            e = (num - den * m0) * inv
            k1 = p01 * w
            m0, m1 = m0 + p00 * e, m1 + p01 * e
            p11 = p11 - k1 * p01
            p00, p01 = p00 * inv, p01 * inv
            for slot, value in enumerate((inv, w, e, k1, m0, p00, p01)):
                saved[p, t, slot] = value
            q00, q01, q11 = scaled_noise(t)
            m0 = m0 + m1
            r = p01 + p11
            p00, p01, p11 = (p00 + p01) + (r + q00), r + q01, p11 + q11

        put(after.at[p], STATE, (m0, m1, p00, p01, p11))

    half = pl.ds(pl.multiple_of(core * LANES, LANES), LANES)

    def result_copy(p, k):
        row = pl.multiple_of(((1 - p) * (1 + k) + p * k * (rows // SUB - 1)) * SUB, SUB)
        return pltpu.make_async_remote_copy(
            src_ref=res.at[p, :, other, k * SUB : k * SUB + SUB, :],
            dst_ref=landed.at[:, :, pl.ds(row, SUB), half],
            send_sem=res_send.at[p, k], recv_sem=res_recv.at[p, k], device_id={"tm": partner})

    def backward(p):
        i0, i1, i00, i01, i11 = values(suf.at[p], INFO)
        m0, m1, p00, p01, p11 = values(after.at[p], STATE)
        s, s2 = decay**span, decay ** (2 * span)
        mat = (i00 * s2, i01 * s2, i11 * s2)
        pulled = symv(mat, (m0, m1))
        (n00, n01, n11), (u0, u1) = absorb(mat, (p00, p01, p11),
                                           (i0 * s - pulled[0], i1 * s - pulled[1]))
        for t in reversed(range(span)):
            u1 = u0 + u1
            both = n00 + n01
            n01, n11 = both, both + (n01 + n11)
            inv, w, e, k1, m0, p00, p01 = (saved[p, t, slot] for slot in range(SAVED))
            mean = m0 + p00 * u0 + p01 * u1
            g0, g1 = p00 * n00 + p01 * n01, p00 * n01 + p01 * n11
            res[p, 0, t] = inverse(1.0 + jnp.exp(mean * -(decay**t)))
            res[p, 1, t] = (p00 - (p00 * g0 + p01 * g1)) * decay ** (2 * t)
            u0 = e + inv * u0 - k1 * u1
            l01 = inv * n01 - k1 * n11
            n00 = w + inv * (inv * n00 - k1 * n01) - k1 * l01
            n01 = l01
            if t == 0 or t == frames:
                @pl.when(core == (1 if t == 0 else 0))
                def _():
                    for k in range(2):
                        result_copy(p, k).start()
        for k in range(2):
            row = pl.multiple_of(((1 - p) * (1 + k) + p * k * (rows // SUB - 1)) * SUB, SUB)
            landed[:, :, pl.ds(row, SUB), half] = res[p, :, own, k * SUB : k * SUB + SUB, :]

    to_partner.wait_recv()
    summary(0)
    if chips == 4:
        tell()
        direct_each(0, lambda copy: copy.start())
    else:
        send_level(0, 0)
    for direction, there in ((0, has_up), (1, has_down)):
        @pl.when(there)
        def _():
            for sender in range(CORES):
                halo_arrived(direction, sender)
    summary(1)
    if chips == 4:
        @pl.when(chip > 0)
        def _():
            pl.semaphore_wait(hello.at[0], 1)

        direct_each(1, lambda copy: copy.start())
        relay(0)
        relay(1)

        @pl.when(chip < 2)
        def _():
            for_phases(forward)
    else:
        send_level(1, 0)
        for level in range(levels):
            for p in range(2):
                take_level(p, level)
                if level + 1 < levels:
                    send_level(p, level + 1)

    def finish(p):
        if chips == 4:
            collect(p)
            pl.when(chip >= 2)(functools.partial(forward, p))
        else:
            forward(p)
        backward(p)

    finish(0)
    finish(1)
    for p in range(2):
        for k in range(2):
            result_copy(p, k).wait_recv()
    for p in range(2):
        for k in range(2):
            result_copy(p, k).wait_send()
        if chips == 4:
            direct_sent(p)
        else:
            for level in range(levels):
                each_send(p, level, lambda copy: copy.wait_send())
    for direction, there in ((0, has_down), (1, has_up)):
        @pl.when(there)
        def _():
            for crossed in range(2):
                halo(direction, crossed).wait_send()
    to_partner.wait_send()


def hand_out(landed, occupancy, spread, sems):
    copies = [pltpu.make_async_copy(landed.at[k], out, sems.at[k])
              for k, out in enumerate((occupancy, spread))]
    for copy in copies:
        copy.start()
    for copy in copies:
        copy.wait()


def solution(mesh):
    tm_count, space_count = mesh.shape["tm"], mesh.shape["space"]

    def body(hits, misses):
        frames, rows, cols = hits.shape
        span, chips = CORES * frames, tm_count // CORES
        levels = chips.bit_length() - 1
        cells = (2 * SUB, LANES)
        assert rows == 4 * SUB and cols == CORES * LANES and chips == 1 << levels
        f32 = jnp.float32
        hbm = pl.BlockSpec(memory_space=pltpu.HBM)
        vmem = pl.BlockSpec(memory_space=pltpu.VMEM)
        dma = pltpu.SemaphoreType.DMA
        landed = pl.pallas_call(
            functools.partial(kernel, tm_count, space_count),
            out_shape=pltpu.VMEM((2, frames, rows, cols), f32),
            in_specs=[hbm] * 2,
            out_specs=vmem,
            scratch_shapes=[
                pltpu.VMEM(hits.shape, jnp.int32),
                pltpu.VMEM(hits.shape, jnp.int32),
                pltpu.VMEM((2, frames, rows, cols), f32),
                pltpu.VMEM((2, span, rows + 2 * SUB, LANES), f32),
                pltpu.VMEM((2, frames, rows, LANES), f32),
                pltpu.VMEM((2, 2, span) + cells, f32),
                pltpu.VMEM((2, VALUES) + cells, f32),
                pltpu.VMEM((2, max(levels - 1, 1), VALUES) + cells, f32),
                pltpu.VMEM((2, max(levels, 4), VALUES) + cells, f32),
                pltpu.VMEM((2, VALUES) + cells, f32),
                pltpu.VMEM((2, VALUES) + cells, f32),
                pltpu.VMEM((2, 5) + cells, f32),
                pltpu.VMEM((2, span, SAVED) + cells, f32),
                pltpu.VMEM((2, 2, span) + cells, f32),
                dma((2, 2, 2)),
                dma((2, 2)),
                dma((2, 2)),
                dma((1,)),
                dma((1,)),
                dma((2, 4) if chips == 4 else (2, levels, chips // 2)),
                dma((2, max(levels, 4))),
                dma((2, 2)),
                dma((2, 2)),
                pltpu.SemaphoreType.REGULAR((1,)),
            ],
            compiler_params=pltpu.CompilerParams(
                collective_id=0, has_side_effects=True, vmem_limit_bytes=32 * 1024 * 1024),
        )(pltpu.with_memory_space_constraint(hits, pltpu.HBM),
          pltpu.with_memory_space_constraint(misses, pltpu.HBM))
        out = jax.ShapeDtypeStruct(hits.shape, f32)
        return pl.pallas_call(
            hand_out,
            out_shape=(out, out),
            in_specs=[vmem],
            out_specs=(hbm, hbm),
            scratch_shapes=[dma((2,))],
            compiler_params=pltpu.CompilerParams(vmem_limit_bytes=8 * 1024 * 1024),
        )(landed)

    placed = P("tm", "space", None)
    return jax.shard_map(body, mesh=mesh, in_specs=(placed, placed),
                         out_specs=(placed, placed), check_vma=False)
```

```python
import functools
import math

import jax
import jax.numpy as jnp
from jax import lax
from jax.experimental import pallas as pl
from jax.experimental.pallas import tpu as pltpu
from jax.sharding import PartitionSpec as P

RADIUS = 7
SCALE_T = 64
SUB = 8
LANES = 128
CORES = 2
VALUES = 14
STATE = slice(0, 5)
INFO = slice(9, 14)
SAVED = 7
SLOTS = 4
PHASES = (slice(0, 2), slice(2, 3), slice(3, 4))
GREETED = ((1, 2, 3), (3,), (3,), (1, 2))

sigma_cells = 3.0
prior_var = 4.0


def dynamics():
    q = math.sqrt(3.0) / SCALE_T
    decay = math.exp(-q)
    p0, p1 = prior_var, prior_var * q * q
    prior = (p0, q * p0, q * q * p0 + p1)
    a, b, c = prior
    noise = (
        a - decay**2 * (a + 2.0 * b + c),
        b - decay**2 * (b + c),
        c - decay**2 * c,
    )
    return decay, prior, noise


def taps():
    raw = [math.exp(-o * o / (2.0 * sigma_cells**2)) for o in range(-RADIUS, RADIUS + 1)]
    total = sum(raw)
    return [r / total for r in raw], total


def inverse(x):
    r = pl.reciprocal(x, approx=True)
    return r * (2.0 - x * r)


def absorb(x, y, g):
    x00, x01, x11 = x
    y00, y01, y11 = y
    d00 = 1.0 + (x00 * y00 + x01 * y01)
    d01 = x00 * y01 + x01 * y11
    d10 = x01 * y00 + x11 * y01
    d11 = 1.0 + (x01 * y01 + x11 * y11)
    inv = inverse(d00 * d11 - d01 * d10)
    det = x00 * x11 - x01 * x01
    out = ((x00 + y11 * det) * inv, (x01 - y01 * det) * inv, (x11 + y00 * det) * inv)
    vec = ((d11 * g[0] - d01 * g[1]) * inv, (d00 * g[1] - d10 * g[0]) * inv)
    return out, vec


def congruent(a, s):
    a00, a01, a10, a11 = a
    s00, s01, s11 = s
    u0, u1 = a00 * s00 + a01 * s01, a00 * s01 + a01 * s11
    v0, v1 = a10 * s00 + a11 * s01, a10 * s01 + a11 * s11
    return u0 * a00 + u1 * a01, u0 * a10 + u1 * a11, v0 * a10 + v1 * a11


def symv(s, v):
    return s[0] * v[0] + s[1] * v[1], s[1] * v[0] + s[2] * v[1]


def matv(a, v):
    return a[0] * v[0] + a[1] * v[1], a[2] * v[0] + a[3] * v[1]


def add(*parts):
    return tuple(sum(p[1:], p[0]) for p in zip(*parts))


def carry_state(state, block):
    mean, cov = state[:2], state[2:]
    shift = symv(cov, block[9:11])
    cov, mean = absorb(cov, block[11:14], add(mean, shift))
    a = block[5:9]
    return add(matv(a, mean), block[0:2]) + add(congruent(a, cov), block[2:5])


def carry_info(block, info):
    vec, mat = info[:2], info[2:]
    pulled = symv(mat, block[0:2])
    s, v = absorb(mat, block[2:5], (vec[0] - pulled[0], vec[1] - pulled[1]))
    a00, a01, a10, a11 = block[5:9]
    back = (a00, a10, a01, a11)
    return add(matv(back, v), block[9:11]) + add(congruent(back, s), block[11:14])


def join(one, two):
    state = carry_state(one[0:5], two)
    info = carry_info(one, two[9:14])
    c, j = one[2:5], two[11:14]
    d00 = 1.0 + (c[0] * j[0] + c[1] * j[1])
    d01 = c[0] * j[1] + c[1] * j[2]
    d10 = c[1] * j[0] + c[2] * j[1]
    d11 = 1.0 + (c[1] * j[1] + c[2] * j[2])
    inv = inverse(d00 * d11 - d01 * d10)
    a00, a01, a10, a11 = one[5:9]
    m = (
        (d11 * a00 - d01 * a10) * inv,
        (d11 * a01 - d01 * a11) * inv,
        (d00 * a10 - d10 * a00) * inv,
        (d00 * a11 - d10 * a01) * inv,
    )
    b00, b01, b10, b11 = two[5:9]
    a = (
        b00 * m[0] + b01 * m[2],
        b00 * m[1] + b01 * m[3],
        b10 * m[0] + b11 * m[2],
        b10 * m[1] + b11 * m[3],
    )
    return state + a + info


def kernel(tm_count, space_count, hits_hbm, misses_hbm, landed, hits, misses, chan, field,
           give, window, obs, elem, incl, got, pre, suf, after, saved, res, load, halo_send, halo_recv,
           pair_send, pair_recv, level_send, level_recv, res_send, res_recv, hello):
    frames, rows, cols = hits.shape
    parts = ((slice(0, SUB), slice(rows - SUB, rows)), (slice(SUB, rows - SUB),))

    def loads(part):
        return [pltpu.make_async_copy(src.at[:, cut, :], dst.at[:, cut, :], load.at[k, part, j])
                for j, cut in enumerate(parts[part])
                for k, (src, dst) in enumerate(((hits_hbm, hits), (misses_hbm, misses)))]

    span = CORES * frames
    chips = tm_count // CORES
    levels = chips.bit_length() - 1
    me = lax.axis_index("tm")
    tile = lax.axis_index("space")
    chip, core = me // CORES, me % CORES
    partner = me + 1 - 2 * core
    decay, prior, noise = dynamics()
    weights, total = taps()
    has_up = tile > 0
    has_down = tile < space_count - 1
    barrier = pltpu.get_barrier_semaphore()

    @pl.when(has_up)
    def _():
        pl.semaphore_signal(barrier, inc=1, device_id={"space": tile - 1})
        pl.semaphore_signal(barrier, inc=1, device_id={"tm": partner, "space": tile - 1})

    @pl.when(has_down)
    def _():
        pl.semaphore_signal(barrier, inc=1, device_id={"space": tile + 1})
        pl.semaphore_signal(barrier, inc=1, device_id={"tm": partner, "space": tile + 1})

    pl.semaphore_signal(barrier, inc=1, device_id={"tm": partner})

    if chips == 4:
        for sender, targets in enumerate(GREETED):
            @pl.when(chip == sender)
            def _():
                for target in targets:
                    pl.semaphore_signal(barrier, inc=1, device_id={"tm": CORES * target + core})

        greetings = (chip > 0).astype(jnp.int32) * 2 + (chip == 3).astype(jnp.int32)
    else:
        def greet(k, carry):
            pl.semaphore_signal(barrier, inc=1,
                                device_id={"tm": CORES * ((chip + k) % chips) + core})
            return carry

        lax.fori_loop(1, chips, greet, 0)
        greetings = chips - 1

    for part in range(2):
        for copy in loads(part):
            copy.start()

    own = pl.ds(core * frames, frames)
    other = pl.ds((1 - core) * frames, frames)
    cells = (SUB, LANES)

    @pl.when(jnp.logical_not(has_up))
    def _():
        field[:, :, 0:SUB, :] = jnp.zeros((2, span, SUB, LANES), jnp.float32)

    @pl.when(jnp.logical_not(has_down))
    def _():
        field[:, :, SUB + rows :, :] = jnp.zeros((2, span, SUB, LANES), jnp.float32)

    @pl.when(chip == 0)
    def _():
        for slot in range(SLOTS):
            for k, value in enumerate((0.0, 0.0) + prior):
                pre[slot, k] = jnp.full(cells, value, jnp.float32)

    @pl.when(chip == chips - 1)
    def _():
        suf[:, INFO] = jnp.zeros((SLOTS, 5) + cells, jnp.float32)

    column = lax.broadcasted_iota(jnp.int32, (cols, cols), 1) + core * LANES
    column = jnp.where(column >= cols, column - cols, column)
    offset = lax.broadcasted_iota(jnp.int32, (cols, cols), 0) - column
    far = offset.astype(jnp.float32)
    band = jnp.where(jnp.abs(offset) <= RADIUS,
                     jnp.exp(-far * far / (2.0 * sigma_cells**2)) / total, 0.0)
    band_high = band.astype(jnp.bfloat16)
    band_low = (band - band_high.astype(jnp.float32)).astype(jnp.bfloat16)

    late = core.astype(jnp.float32)
    base = 1.0 + late * (decay**frames - 1.0)
    base2 = 1.0 + late * (decay ** (2 * frames) - 1.0)
    dot = functools.partial(jnp.dot, preferred_element_type=jnp.float32)

    def prepare(part):
        for copy in loads(part):
            copy.wait()
        for cut in parts[part]:
            size = cut.stop - cut.start
            for f in range(frames):
                h, m = hits[f, cut, :], misses[f, cut, :]
                hp = h.astype(jnp.float32) + 1.0
                mp = m.astype(jnp.float32) + 1.0
                inv = inverse(hp + mp)
                weight = (h + m).astype(jnp.float32) * (hp * inv) * (mp * inv)
                chan[0, f, cut, :] = weight * (jnp.log(hp) - jnp.log(mp)) * (base * decay**f)
                chan[1, f, cut, :] = weight * (base2 * decay ** (2 * f))
        for cut in parts[part]:
            size = cut.stop - cut.start
            flat = chan[:, :, cut, :].reshape(2 * frames * size, cols)
            high = flat.astype(jnp.bfloat16)
            low = (flat - high.astype(jnp.float32)).astype(jnp.bfloat16)
            out = dot(high, band_high) + (dot(low, band_high) + dot(high, band_low))
            out = out.reshape(2, frames, size, cols)
            field[:, own, SUB + cut.start : SUB + cut.stop, :] = out[..., :LANES]
            give[:, :, cut, :] = out[..., LANES:]

    prepare(0)
    prepare(1)
    neighbours = has_up.astype(jnp.int32) + has_down.astype(jnp.int32)
    pl.semaphore_wait(barrier, 1 + greetings + 2 * neighbours)

    top, bottom = pl.ds(SUB - RADIUS, RADIUS), pl.ds(SUB + rows, RADIUS)

    def halo(direction, crossed):
        step = 1 - 2 * direction
        where = bottom if direction else top
        if crossed:
            row = pl.ds(0, RADIUS) if direction else pl.ds(rows - RADIUS, RADIUS)
            source, target = give.at[:, :, row, :], {"tm": partner, "space": tile + step}
        else:
            row = pl.ds(SUB, RADIUS) if direction else pl.ds(SUB + rows - RADIUS, RADIUS)
            source, target = field.at[:, own, row, :], {"space": tile + step}
        return pltpu.make_async_remote_copy(
            src_ref=source, dst_ref=field.at[:, own, where, :],
            send_sem=halo_send.at[direction, crossed],
            recv_sem=halo_recv.at[direction, core], device_id=target)

    def halo_arrived(direction, sender):
        where = bottom if direction else top
        part = field.at[:, pl.ds(sender * frames, frames), where, :]
        pltpu.make_async_remote_copy(
            src_ref=part, dst_ref=part, send_sem=halo_send.at[direction, 0],
            recv_sem=halo_recv.at[direction, sender], device_id={"tm": partner}).wait_recv()

    for direction, there in ((0, has_down), (1, has_up)):
        @pl.when(there)
        def _():
            for crossed in range(2):
                halo(direction, crossed).start()

    if chips == 4:
        @pl.when(chip > 0)
        def _():
            pl.semaphore_signal(hello.at[0], inc=1, device_id={"tm": core})

    to_partner = pltpu.make_async_remote_copy(
        src_ref=give, dst_ref=field.at[:, own, pl.ds(SUB, rows), :],
        send_sem=pair_send.at[0], recv_sem=pair_recv.at[0], device_id={"tm": partner})
    to_partner.start()

    early = jnp.where(has_down, 0, rows // SUB - 1)
    groups = (1, 2, early, rows // SUB - 1 - early)

    def down(c, t, slot):
        def at(s):
            low = SUB - RADIUS + s
            if slot < 2:
                low = low + groups[slot] * SUB
                return field[c, t, low : low + SUB, :]
            return window[c, t, low : low + SUB, :]

        out = weights[RADIUS] * at(RADIUS)
        for s in range(RADIUS):
            out = out + weights[s] * (at(s) + at(2 * RADIUS - s))
        return out

    first = (chip == 0).astype(jnp.float32)

    def scaled_noise(t):
        return tuple(v * decay ** (-2 * (t + 1)) for v in noise)

    full = slice(0, VALUES)

    def summary(p):
        slots = PHASES[p]
        if p > 0:
            row = pl.multiple_of(groups[slots.start] * SUB, SUB)
            window[...] = field[:, :, pl.ds(row, 3 * SUB), :]
        zero = jnp.zeros((slots.stop - slots.start,) + cells, jnp.float32)
        m0 = m1 = a01 = c0 = eta0 = eta1 = j00 = j01 = j11 = zero
        a00 = c1 = zero + 1.0
        p00, p01, p11 = (zero + v * first for v in prior)
        for t in range(span):
            for c in range(2):
                for slot in range(slots.start, slots.stop):
                    obs[slot, c, t] = down(c, t, slot)
            num, den = obs[slots, 0, t], obs[slots, 1, t]
            inv = inverse(1.0 + p00 * den)
            w = den * inv
            e = (num - den * m0) * inv
            k1 = p01 * w
            m0, m1 = m0 + p00 * e, m1 + p01 * e
            p11 = p11 - k1 * p01
            p00, p01 = p00 * inv, p01 * inv
            eta0, eta1 = eta0 + a00 * e, eta1 + a01 * e
            w0, w1 = w * a00, w * a01
            j00, j01, j11 = j00 + w0 * a00, j01 + w0 * a01, j11 + w1 * a01
            c0, c1 = c0 - k1 * a00, c1 - k1 * a01
            a00, a01 = a00 * inv, a01 * inv
            q00, q01, q11 = scaled_noise(t)
            m0 = m0 + m1
            a00, a01 = a00 + c0, a01 + c1
            r = p01 + p11
            p00, p01, p11 = (p00 + p01) + (r + q00), r + q01, p11 + q11
        s, s2 = decay**span, decay ** (2 * span)
        block = (m0 * s, m1 * s, p00 * s2, p01 * s2, p11 * s2,
                 a00 * s, a01 * s, c0 * s, c1 * s, eta0, eta1, j00, j01, j11)
        put(elem, p, full, block)

    def values(ref, p, part):
        return tuple(ref[PHASES[p], k] for k in range(part.start, part.stop))

    def put(ref, p, part, items):
        for k, item in zip(range(part.start, part.stop), items):
            ref[PHASES[p], k] = item

    def cut(ref, p, part):
        slots = PHASES[p]
        return ref.at[pl.ds(slots.start, slots.stop - slots.start),
                      pl.ds(part.start, part.stop - part.start)]

    def level_copy(p, level, d, target, part):
        src = elem if level == 0 else incl.at[level - 1]
        return pltpu.make_async_remote_copy(
            src_ref=cut(src, p, part), dst_ref=cut(got.at[level], p, part),
            send_sem=level_send.at[p, level, d], recv_sem=level_recv.at[p, level],
            device_id={"tm": CORES * target + core})

    def branches(level):
        size = 1 << level
        ends = chip % (2 * size) == size - 1
        starts = chip % (2 * size) == size
        if chips == 2 * size:
            return ((ends, STATE),), ((starts, INFO),)
        lone = chip == size - 1
        last = chip == chips - size
        return (((lone, STATE), (jnp.logical_and(ends, jnp.logical_not(lone)), full)),
                ((last, INFO), (jnp.logical_and(starts, jnp.logical_not(last)), full)))

    def each_send(p, level, act):
        size = 1 << level
        lefts, rights = branches(level)
        for group, step in ((lefts, 1), (rights, -1)):
            for condition, part in group:
                @pl.when(condition)
                def _():
                    for d in range(size):
                        act(level_copy(p, level, d, chip + step * (d + 1), part))

    def send_level(p, level):
        if level:
            out = incl.at[level - 1]
            lefts, rights = branches(level)
            for condition, part in lefts:
                @pl.when(condition)
                def _():
                    one, two = values(pre, p, part), values(elem, p, full)
                    put(out, p, part, carry_state(one, two) if part is STATE else join(one, two))
            for condition, part in rights:
                @pl.when(condition)
                def _():
                    one, two = values(elem, p, full), values(suf, p, part)
                    put(out, p, part, carry_info(one, two) if part is INFO else join(one, two))
        each_send(p, level, lambda copy: copy.start())

    def take_level(p, level):
        size = 1 << level
        right = (chip // size) % 2 == 1
        left = jnp.logical_not(right)
        if chips == 2 * size:
            cases = ((right, STATE, True), (left, INFO, False))
        else:
            low, high = chip < 2 * size, chip >= chips - 2 * size
            cases = (
                (jnp.logical_and(right, low), STATE, True),
                (jnp.logical_and(right, jnp.logical_not(low)), full, True),
                (jnp.logical_and(left, high), INFO, False),
                (jnp.logical_and(left, jnp.logical_not(high)), full, False),
            )
        for condition, part, earlier in cases:
            @pl.when(condition)
            def _():
                level_copy(p, level, 0, chip, part).wait_recv()
                bare = chip % size == (0 if earlier else size - 1)
                mine = pre if earlier else suf

                def keep():
                    put(mine, p, part, values(got.at[level], p, part))

                def merge():
                    new = values(got.at[level], p, part)
                    old = values(mine, p, full)
                    if part is STATE:
                        put(mine, p, part, carry_state(new, old))
                    elif part is INFO:
                        put(mine, p, part, carry_info(old, new))
                    else:
                        put(mine, p, part, join(new, old) if earlier else join(old, new))

                if size == 1:
                    keep()
                else:
                    pl.when(bare)(keep)
                    pl.when(jnp.logical_not(bare))(merge)

    straight = (((1, STATE), (3, STATE)), ((0, full), (3, full)), ((0, full), (3, full)), ((2, INFO), (0, INFO)))
    stepped = (((1, STATE),), ((0, full),), ((3, full),), ((2, INFO),))
    hops = (stepped, straight, straight)
    relays = ((3, 2), (2,), (2,))

    def tell():
        @pl.when(chip == 0)
        def _():
            pl.semaphore_wait(hello.at[0], 3)
            for target in range(1, 4):
                pl.semaphore_signal(hello.at[0], inc=1, device_id={"tm": CORES * target + core})

    def direct_copy(p, sender, d, relayed=False):
        if relayed:
            src, target, part = incl.at[0], relays[p][d], STATE if sender == 1 else INFO
            if sender == 2:
                target = 3 - target
            d = d + 2
        else:
            src, (target, part) = elem, hops[p][sender][d]
        return pltpu.make_async_remote_copy(
            src_ref=cut(src, p, part), dst_ref=cut(got.at[sender], p, part),
            send_sem=level_send.at[p, d], recv_sem=level_recv.at[p, sender],
            device_id={"tm": CORES * target + core})

    def direct_each(p, act):
        for sender in range(4):
            @pl.when(chip == sender)
            def _():
                for d in range(len(hops[p][sender])):
                    act(direct_copy(p, sender, d))

    def arrive(p, sender, part):
        block = cut(got.at[sender], p, part)
        pltpu.make_async_remote_copy(
            src_ref=block, dst_ref=block, send_sem=level_send.at[p, 0],
            recv_sem=level_recv.at[p, sender], device_id={"tm": partner}).wait_recv()
        return values(got.at[sender], p, part)

    def relay(p):
        @pl.when(chip == 1)
        def _():
            state = arrive(p, 0, STATE)
            put(pre, p, STATE, state)
            put(incl.at[0], p, STATE, carry_state(state, values(elem, p, full)))
            for d in range(len(relays[p])):
                direct_copy(p, 1, d, True).start()

        @pl.when(chip == 2)
        def _():
            info = arrive(p, 3, INFO)
            put(suf, p, INFO, info)
            put(incl.at[0], p, INFO, carry_info(values(elem, p, full), info))
            for d in range(len(relays[p])):
                direct_copy(p, 2, d, True).start()

    def collect(p):
        @pl.when(chip == 0)
        def _():
            if len(relays[p]) > 1:
                info = arrive(p, 2, INFO)
            else:
                info = arrive(p, 3, INFO)
                info = carry_info(arrive(p, 2, full), info)
            put(suf, p, INFO, carry_info(arrive(p, 1, full), info))

        @pl.when(chip == 1)
        def _():
            put(suf, p, INFO, arrive(p, 2, INFO))

        @pl.when(chip == 2)
        def _():
            put(pre, p, STATE, arrive(p, 1, STATE))

        @pl.when(chip == 3)
        def _():
            if len(relays[p]) > 1:
                state = arrive(p, 1, STATE)
            else:
                state = arrive(p, 0, STATE)
                state = carry_state(state, arrive(p, 1, full))
            put(pre, p, STATE, carry_state(state, arrive(p, 2, full)))

    def direct_sent(p):
        direct_each(p, lambda copy: copy.wait_send())
        for sender in (1, 2):
            @pl.when(chip == sender)
            def _():
                for d in range(len(relays[p])):
                    direct_copy(p, sender, d, True).wait_send()

    def forward(p):
        slots = PHASES[p]
        m0, m1, p00, p01, p11 = values(pre, p, STATE)
        for t in range(span):
            num, den = obs[slots, 0, t], obs[slots, 1, t]
            inv = inverse(1.0 + p00 * den)
            w = den * inv
            e = (num - den * m0) * inv
            k1 = p01 * w
            m0, m1 = m0 + p00 * e, m1 + p01 * e
            p11 = p11 - k1 * p01
            p00, p01 = p00 * inv, p01 * inv
            for k, value in enumerate((inv, w, e, k1, m0, p00, p01)):
                saved[slots, t, k] = value
            q00, q01, q11 = scaled_noise(t)
            m0 = m0 + m1
            r = p01 + p11
            p00, p01, p11 = (p00 + p01) + (r + q00), r + q01, p11 + q11

        put(after, p, STATE, (m0, m1, p00, p01, p11))

    half = pl.ds(pl.multiple_of(core * LANES, LANES), LANES)

    def result_rows(slot):
        return pl.ds(pl.multiple_of(groups[slot] * SUB, SUB) if slot > 1 else groups[slot] * SUB, SUB)

    def result_copy(slot):
        return pltpu.make_async_remote_copy(
            src_ref=res.at[slot, :, other], dst_ref=landed.at[:, :, result_rows(slot), half],
            send_sem=res_send.at[slot], recv_sem=res_recv.at[slot], device_id={"tm": partner})

    def backward(p):
        slots = PHASES[p]
        i0, i1, i00, i01, i11 = values(suf, p, INFO)
        m0, m1, p00, p01, p11 = values(after, p, STATE)
        s, s2 = decay**span, decay ** (2 * span)
        mat = (i00 * s2, i01 * s2, i11 * s2)
        pulled = symv(mat, (m0, m1))
        (n00, n01, n11), (u0, u1) = absorb(mat, (p00, p01, p11),
                                           (i0 * s - pulled[0], i1 * s - pulled[1]))
        for t in reversed(range(span)):
            u1 = u0 + u1
            both = n00 + n01
            n01, n11 = both, both + (n01 + n11)
            inv, w, e, k1, m0, p00, p01 = (saved[slots, t, k] for k in range(SAVED))
            mean = m0 + p00 * u0 + p01 * u1
            g0, g1 = p00 * n00 + p01 * n01, p00 * n01 + p01 * n11
            res[slots, 0, t] = inverse(1.0 + jnp.exp(mean * -(decay**t)))
            res[slots, 1, t] = (p00 - (p00 * g0 + p01 * g1)) * decay ** (2 * t)
            u0 = e + inv * u0 - k1 * u1
            l01 = inv * n01 - k1 * n11
            n00 = w + inv * (inv * n00 - k1 * n01) - k1 * l01
            n01 = l01
            if t == 0 or t == frames:
                @pl.when(core == (1 if t == 0 else 0))
                def _():
                    for slot in range(slots.start, slots.stop):
                        result_copy(slot).start()
        for slot in range(slots.start, slots.stop):
            landed[:, :, result_rows(slot), half] = res[slot, :, own]

    def send(p):
        if chips == 4:
            direct_each(p, lambda copy: copy.start())
        else:
            send_level(p, 0)

    def halos(direction, there):
        @pl.when(there)
        def _():
            for sender in range(CORES):
                halo_arrived(direction, sender)

    to_partner.wait_recv()
    summary(0)
    if chips == 4:
        tell()
    send(0)
    halos(0, jnp.logical_and(has_up, has_down))
    summary(1)
    if chips == 4:
        @pl.when(chip > 0)
        def _():
            pl.semaphore_wait(hello.at[0], 1)

    send(1)
    halos(1, has_down)
    halos(0, jnp.logical_and(has_up, jnp.logical_not(has_down)))
    summary(2)
    send(2)
    order = range(len(PHASES))
    if chips == 4:
        for p in order:
            relay(p)

        @pl.when(chip < 2)
        def _():
            for p in order:
                forward(p)
    else:
        for level in range(levels):
            for p in order:
                take_level(p, level)
                if level + 1 < levels:
                    send_level(p, level + 1)

    def finish(p):
        if chips == 4:
            collect(p)
            pl.when(chip >= 2)(functools.partial(forward, p))
        else:
            forward(p)
        backward(p)

    for p in order:
        finish(p)
    for slot in range(SLOTS):
        result_copy(slot).wait_recv()
    for slot in range(SLOTS):
        result_copy(slot).wait_send()
    for p in order:
        if chips == 4:
            direct_sent(p)
        else:
            for level in range(levels):
                each_send(p, level, lambda copy: copy.wait_send())
    for direction, there in ((0, has_down), (1, has_up)):
        @pl.when(there)
        def _():
            for crossed in range(2):
                halo(direction, crossed).wait_send()
    to_partner.wait_send()


def hand_out(landed, occupancy, spread, sems):
    copies = [pltpu.make_async_copy(landed.at[k], out, sems.at[k])
              for k, out in enumerate((occupancy, spread))]
    for copy in copies:
        copy.start()
    for copy in copies:
        copy.wait()


def solution(mesh):
    tm_count, space_count = mesh.shape["tm"], mesh.shape["space"]

    def body(hits, misses):
        frames, rows, cols = hits.shape
        span, chips = CORES * frames, tm_count // CORES
        levels = chips.bit_length() - 1
        cells = (SUB, LANES)
        assert rows == 4 * SUB and cols == CORES * LANES and chips == 1 << levels
        f32 = jnp.float32
        hbm = pl.BlockSpec(memory_space=pltpu.HBM)
        vmem = pl.BlockSpec(memory_space=pltpu.VMEM)
        dma = pltpu.SemaphoreType.DMA
        landed = pl.pallas_call(
            functools.partial(kernel, tm_count, space_count),
            out_shape=pltpu.VMEM((2, frames, rows, cols), f32),
            in_specs=[hbm] * 2,
            out_specs=vmem,
            scratch_shapes=[
                pltpu.VMEM(hits.shape, jnp.int32),
                pltpu.VMEM(hits.shape, jnp.int32),
                pltpu.VMEM((2, frames, rows, cols), f32),
                pltpu.VMEM((2, span, rows + 2 * SUB, LANES), f32),
                pltpu.VMEM((2, frames, rows, LANES), f32),
                pltpu.VMEM((2, span, 3 * SUB, LANES), f32),
                pltpu.VMEM((SLOTS, 2, span) + cells, f32),
                pltpu.VMEM((SLOTS, VALUES) + cells, f32),
                pltpu.VMEM((max(levels - 1, 1), SLOTS, VALUES) + cells, f32),
                pltpu.VMEM((max(levels, 4), SLOTS, VALUES) + cells, f32),
                pltpu.VMEM((SLOTS, VALUES) + cells, f32),
                pltpu.VMEM((SLOTS, VALUES) + cells, f32),
                pltpu.VMEM((SLOTS, 5) + cells, f32),
                pltpu.VMEM((SLOTS, span, SAVED) + cells, f32),
                pltpu.VMEM((SLOTS, 2, span) + cells, f32),
                dma((2, 2, 2)),
                dma((2, 2)),
                dma((2, 2)),
                dma((1,)),
                dma((1,)),
                dma((3, 4) if chips == 4 else (3, levels, chips // 2)),
                dma((3, max(levels, 4))),
                dma((SLOTS,)),
                dma((SLOTS,)),
                pltpu.SemaphoreType.REGULAR((1,)),
            ],
            compiler_params=pltpu.CompilerParams(
                collective_id=0, has_side_effects=True, vmem_limit_bytes=32 * 1024 * 1024),
        )(pltpu.with_memory_space_constraint(hits, pltpu.HBM),
          pltpu.with_memory_space_constraint(misses, pltpu.HBM))
        out = jax.ShapeDtypeStruct(hits.shape, f32)
        return pl.pallas_call(
            hand_out,
            out_shape=(out, out),
            in_specs=[vmem],
            out_specs=(hbm, hbm),
            scratch_shapes=[dma((2,))],
            compiler_params=pltpu.CompilerParams(vmem_limit_bytes=8 * 1024 * 1024),
        )(landed)

    placed = P("tm", "space", None)
    return jax.shard_map(body, mesh=mesh, in_specs=(placed, placed),
                         out_specs=(placed, placed), check_vma=False)
```

```python
import functools
import math

import jax
import jax.numpy as jnp
from jax import lax
from jax.experimental import pallas as pl
from jax.experimental.pallas import tpu as pltpu
from jax.sharding import PartitionSpec as P

RADIUS = 7
SCALE_T = 64
SUB = 8
LANES = 128
CORES = 2
VALUES = 14
STATE = slice(0, 5)
INFO = slice(9, 14)
SAVED = 7
SLOTS = 4
PHASES = (slice(0, 2), slice(2, 3), slice(3, 4))
GREETED = ((1, 2, 3), (3,), (3,), (1, 2))

sigma_cells = 3.0
prior_var = 4.0


def dynamics():
    q = math.sqrt(3.0) / SCALE_T
    decay = math.exp(-q)
    p0, p1 = prior_var, prior_var * q * q
    prior = (p0, q * p0, q * q * p0 + p1)
    a, b, c = prior
    noise = (
        a - decay**2 * (a + 2.0 * b + c),
        b - decay**2 * (b + c),
        c - decay**2 * c,
    )
    return decay, prior, noise


def taps():
    raw = [math.exp(-o * o / (2.0 * sigma_cells**2)) for o in range(-RADIUS, RADIUS + 1)]
    total = sum(raw)
    return [r / total for r in raw], total


def inverse(x):
    return pl.reciprocal(x, approx=True)


def absorb(x, y, g):
    x00, x01, x11 = x
    y00, y01, y11 = y
    d00 = 1.0 + (x00 * y00 + x01 * y01)
    d01 = x00 * y01 + x01 * y11
    d10 = x01 * y00 + x11 * y01
    d11 = 1.0 + (x01 * y01 + x11 * y11)
    inv = inverse(d00 * d11 - d01 * d10)
    det = x00 * x11 - x01 * x01
    out = ((x00 + y11 * det) * inv, (x01 - y01 * det) * inv, (x11 + y00 * det) * inv)
    vec = ((d11 * g[0] - d01 * g[1]) * inv, (d00 * g[1] - d10 * g[0]) * inv)
    return out, vec


def congruent(a, s):
    a00, a01, a10, a11 = a
    s00, s01, s11 = s
    u0, u1 = a00 * s00 + a01 * s01, a00 * s01 + a01 * s11
    v0, v1 = a10 * s00 + a11 * s01, a10 * s01 + a11 * s11
    return u0 * a00 + u1 * a01, u0 * a10 + u1 * a11, v0 * a10 + v1 * a11


def symv(s, v):
    return s[0] * v[0] + s[1] * v[1], s[1] * v[0] + s[2] * v[1]


def matv(a, v):
    return a[0] * v[0] + a[1] * v[1], a[2] * v[0] + a[3] * v[1]


def add(*parts):
    return tuple(sum(p[1:], p[0]) for p in zip(*parts))


def carry_state(state, block):
    mean, cov = state[:2], state[2:]
    shift = symv(cov, block[9:11])
    cov, mean = absorb(cov, block[11:14], add(mean, shift))
    a = block[5:9]
    return add(matv(a, mean), block[0:2]) + add(congruent(a, cov), block[2:5])


def carry_info(block, info):
    vec, mat = info[:2], info[2:]
    pulled = symv(mat, block[0:2])
    s, v = absorb(mat, block[2:5], (vec[0] - pulled[0], vec[1] - pulled[1]))
    a00, a01, a10, a11 = block[5:9]
    back = (a00, a10, a01, a11)
    return add(matv(back, v), block[9:11]) + add(congruent(back, s), block[11:14])


def join(one, two):
    state = carry_state(one[0:5], two)
    info = carry_info(one, two[9:14])
    c, j = one[2:5], two[11:14]
    d00 = 1.0 + (c[0] * j[0] + c[1] * j[1])
    d01 = c[0] * j[1] + c[1] * j[2]
    d10 = c[1] * j[0] + c[2] * j[1]
    d11 = 1.0 + (c[1] * j[1] + c[2] * j[2])
    inv = inverse(d00 * d11 - d01 * d10)
    a00, a01, a10, a11 = one[5:9]
    m = (
        (d11 * a00 - d01 * a10) * inv,
        (d11 * a01 - d01 * a11) * inv,
        (d00 * a10 - d10 * a00) * inv,
        (d00 * a11 - d10 * a01) * inv,
    )
    b00, b01, b10, b11 = two[5:9]
    a = (
        b00 * m[0] + b01 * m[2],
        b00 * m[1] + b01 * m[3],
        b10 * m[0] + b11 * m[2],
        b10 * m[1] + b11 * m[3],
    )
    return state + a + info


def kernel(tm_count, space_count, hits_hbm, misses_hbm, landed, hits, misses, chan, field,
           give, obs, elem, incl, got, pre, suf, after, saved, res, load, halo_send, halo_recv,
           pair_send, pair_recv, level_send, level_recv, res_send, res_recv, hello):
    frames, rows, cols = hits.shape
    parts = ((slice(0, SUB), slice(rows - SUB, rows)), (slice(SUB, rows - SUB),))

    def loads(part):
        return [pltpu.make_async_copy(src.at[:, cut, :], dst.at[:, cut, :], load.at[k, part, j])
                for j, cut in enumerate(parts[part])
                for k, (src, dst) in enumerate(((hits_hbm, hits), (misses_hbm, misses)))]

    span = CORES * frames
    chips = tm_count // CORES
    levels = chips.bit_length() - 1
    me = lax.axis_index("tm")
    tile = lax.axis_index("space")
    chip, core = me // CORES, me % CORES
    partner = me + 1 - 2 * core
    decay, prior, noise = dynamics()
    weights, total = taps()
    has_up = tile > 0
    has_down = tile < space_count - 1
    barrier = pltpu.get_barrier_semaphore()

    @pl.when(has_up)
    def _():
        pl.semaphore_signal(barrier, inc=1, device_id={"space": tile - 1})
        pl.semaphore_signal(barrier, inc=1, device_id={"tm": partner, "space": tile - 1})

    @pl.when(has_down)
    def _():
        pl.semaphore_signal(barrier, inc=1, device_id={"space": tile + 1})
        pl.semaphore_signal(barrier, inc=1, device_id={"tm": partner, "space": tile + 1})

    pl.semaphore_signal(barrier, inc=1, device_id={"tm": partner})

    if chips == 4:
        for sender, targets in enumerate(GREETED):
            @pl.when(chip == sender)
            def _():
                for target in targets:
                    pl.semaphore_signal(barrier, inc=1, device_id={"tm": CORES * target + core})

        greetings = (chip > 0).astype(jnp.int32) * 2 + (chip == 3).astype(jnp.int32)
    else:
        def greet(k, carry):
            pl.semaphore_signal(barrier, inc=1,
                                device_id={"tm": CORES * ((chip + k) % chips) + core})
            return carry

        lax.fori_loop(1, chips, greet, 0)
        greetings = chips - 1

    for part in range(2):
        for copy in loads(part):
            copy.start()

    own = pl.ds(core * frames, frames)
    other = pl.ds((1 - core) * frames, frames)
    cells = (SUB, LANES)

    @pl.when(jnp.logical_not(has_up))
    def _():
        field[:, :, 0:SUB, :] = jnp.zeros((2, span, SUB, LANES), jnp.float32)

    @pl.when(jnp.logical_not(has_down))
    def _():
        field[:, :, SUB + rows :, :] = jnp.zeros((2, span, SUB, LANES), jnp.float32)

    @pl.when(chip == 0)
    def _():
        for slot in range(SLOTS):
            for k, value in enumerate((0.0, 0.0) + prior):
                pre[slot, k] = jnp.full(cells, value, jnp.float32)

    @pl.when(chip == chips - 1)
    def _():
        suf[:, INFO] = jnp.zeros((SLOTS, 5) + cells, jnp.float32)

    column = lax.broadcasted_iota(jnp.int32, (cols, cols), 1) + core * LANES
    column = jnp.where(column >= cols, column - cols, column)
    offset = lax.broadcasted_iota(jnp.int32, (cols, cols), 0) - column
    far = offset.astype(jnp.float32)
    band = jnp.where(jnp.abs(offset) <= RADIUS,
                     jnp.exp(-far * far / (2.0 * sigma_cells**2)) / total, 0.0)
    band_high = band.astype(jnp.bfloat16)
    band_low = (band - band_high.astype(jnp.float32)).astype(jnp.bfloat16)

    late = core.astype(jnp.float32)
    base = 1.0 + late * (decay**frames - 1.0)
    base2 = 1.0 + late * (decay ** (2 * frames) - 1.0)
    dot = functools.partial(jnp.dot, preferred_element_type=jnp.float32)

    def prepare(part):
        for copy in loads(part):
            copy.wait()
        for cut in parts[part]:
            size = cut.stop - cut.start
            for f in range(frames):
                h, m = hits[f, cut, :], misses[f, cut, :]
                hp = h.astype(jnp.float32) + 1.0
                mp = m.astype(jnp.float32) + 1.0
                inv = inverse(hp + mp)
                weight = (h + m).astype(jnp.float32) * (hp * inv) * (mp * inv)
                chan[0, f, cut, :] = weight * (jnp.log(hp) - jnp.log(mp)) * (base * decay**f)
                chan[1, f, cut, :] = weight * (base2 * decay ** (2 * f))
        for cut in parts[part]:
            size = cut.stop - cut.start
            flat = chan[:, :, cut, :].reshape(2 * frames * size, cols)
            high = flat.astype(jnp.bfloat16)
            low = (flat - high.astype(jnp.float32)).astype(jnp.bfloat16)
            out = dot(high, band_high) + (dot(low, band_high) + dot(high, band_low))
            out = out.reshape(2, frames, size, cols)
            field[:, own, SUB + cut.start : SUB + cut.stop, :] = out[..., :LANES]
            give[:, :, cut, :] = out[..., LANES:]

    prepare(0)
    prepare(1)
    neighbours = has_up.astype(jnp.int32) + has_down.astype(jnp.int32)
    pl.semaphore_wait(barrier, 1 + greetings + 2 * neighbours)

    top, bottom = pl.ds(SUB - RADIUS, RADIUS), pl.ds(SUB + rows, RADIUS)

    def halo(direction, crossed):
        step = 1 - 2 * direction
        where = bottom if direction else top
        if crossed:
            row = pl.ds(0, RADIUS) if direction else pl.ds(rows - RADIUS, RADIUS)
            source, target = give.at[:, :, row, :], {"tm": partner, "space": tile + step}
        else:
            row = pl.ds(SUB, RADIUS) if direction else pl.ds(SUB + rows - RADIUS, RADIUS)
            source, target = field.at[:, own, row, :], {"space": tile + step}
        return pltpu.make_async_remote_copy(
            src_ref=source, dst_ref=field.at[:, own, where, :],
            send_sem=halo_send.at[direction, crossed],
            recv_sem=halo_recv.at[direction, core], device_id=target)

    def halo_arrived(direction, sender):
        where = bottom if direction else top
        part = field.at[:, pl.ds(sender * frames, frames), where, :]
        pltpu.make_async_remote_copy(
            src_ref=part, dst_ref=part, send_sem=halo_send.at[direction, 0],
            recv_sem=halo_recv.at[direction, sender], device_id={"tm": partner}).wait_recv()

    for direction, there in ((0, has_down), (1, has_up)):
        @pl.when(there)
        def _():
            for crossed in range(2):
                halo(direction, crossed).start()

    if chips == 4:
        @pl.when(chip > 0)
        def _():
            pl.semaphore_signal(hello.at[0], inc=1, device_id={"tm": core})

    to_partner = pltpu.make_async_remote_copy(
        src_ref=give, dst_ref=field.at[:, own, pl.ds(SUB, rows), :],
        send_sem=pair_send.at[0], recv_sem=pair_recv.at[0], device_id={"tm": partner})
    to_partner.start()

    early = jnp.where(has_down, 0, rows // SUB - 1)
    groups = (1, 2, early, rows // SUB - 1 - early)

    def down(c, t, slot, row):
        def at(s):
            low = SUB - RADIUS + s
            if slot < 2:
                low = low + groups[slot] * SUB
                return field[c, t, low : low + SUB, :]
            return field[c, t, pl.ds(row + low, SUB), :]

        out = weights[RADIUS] * at(RADIUS)
        for s in range(RADIUS):
            out = out + weights[s] * (at(s) + at(2 * RADIUS - s))
        return out

    first = (chip == 0).astype(jnp.float32)

    def scaled_noise(t):
        return tuple(v * decay ** (-2 * (t + 1)) for v in noise)

    def gains(num, den, m0, p00, p01):
        inv = inverse(1.0 + p00 * den)
        k1 = (p01 * den) * inv
        return inv, den * inv, (num - den * m0) * inv, k1, inv - k1

    def advance(t, den, inv, e, m0, m1, p00, p01, p11):
        q00, q01, q11 = scaled_noise(t)
        lost = p01 * (p01 * den)
        both, rest = p00 + p01, p01 - lost
        return ((m0 + m1) + both * e, m1 + p01 * e, (both + rest) * inv + (p11 + q00),
                rest * inv + (p11 + q01), (p11 + q11) - lost * inv)

    full = slice(0, VALUES)

    def summary(p):
        slots = PHASES[p]
        row = groups[slots.start] * SUB
        zero = jnp.zeros((slots.stop - slots.start,) + cells, jnp.float32)
        m0 = m1 = a01 = c0 = eta0 = eta1 = j00 = j01 = j11 = zero
        a00 = c1 = zero + 1.0
        p00, p01, p11 = (zero + v * first for v in prior)
        for t in range(span):
            for c in range(2):
                for slot in range(slots.start, slots.stop):
                    obs[slot, c, t] = down(c, t, slot, row)
            num, den = obs[slots, 0, t], obs[slots, 1, t]
            inv, w, e, k1, g = gains(num, den, m0, p00, p01)
            eta0, eta1 = eta0 + a00 * e, eta1 + a01 * e
            w0, w1 = w * a00, w * a01
            j00, j01, j11 = j00 + w0 * a00, j01 + w0 * a01, j11 + w1 * a01
            a00, a01, c0, c1 = a00 * g + c0, a01 * g + c1, c0 - k1 * a00, c1 - k1 * a01
            m0, m1, p00, p01, p11 = advance(t, den, inv, e, m0, m1, p00, p01, p11)
        s, s2 = decay**span, decay ** (2 * span)
        block = (m0 * s, m1 * s, p00 * s2, p01 * s2, p11 * s2,
                 a00 * s, a01 * s, c0 * s, c1 * s, eta0, eta1, j00, j01, j11)
        put(elem, p, full, block)

    def values(ref, p, part):
        return tuple(ref[PHASES[p], k] for k in range(part.start, part.stop))

    def put(ref, p, part, items):
        for k, item in zip(range(part.start, part.stop), items):
            ref[PHASES[p], k] = item

    def cut(ref, p, part):
        slots = PHASES[p]
        return ref.at[pl.ds(slots.start, slots.stop - slots.start),
                      pl.ds(part.start, part.stop - part.start)]

    def level_copy(p, level, d, target, part):
        src = elem if level == 0 else incl.at[level - 1]
        return pltpu.make_async_remote_copy(
            src_ref=cut(src, p, part), dst_ref=cut(got.at[level], p, part),
            send_sem=level_send.at[p, level, d], recv_sem=level_recv.at[p, level],
            device_id={"tm": CORES * target + core})

    def branches(level):
        size = 1 << level
        ends = chip % (2 * size) == size - 1
        starts = chip % (2 * size) == size
        if chips == 2 * size:
            return ((ends, STATE),), ((starts, INFO),)
        lone = chip == size - 1
        last = chip == chips - size
        return (((lone, STATE), (jnp.logical_and(ends, jnp.logical_not(lone)), full)),
                ((last, INFO), (jnp.logical_and(starts, jnp.logical_not(last)), full)))

    def each_send(p, level, act):
        size = 1 << level
        lefts, rights = branches(level)
        for group, step in ((lefts, 1), (rights, -1)):
            for condition, part in group:
                @pl.when(condition)
                def _():
                    for d in range(size):
                        act(level_copy(p, level, d, chip + step * (d + 1), part))

    def send_level(p, level):
        if level:
            out = incl.at[level - 1]
            lefts, rights = branches(level)
            for condition, part in lefts:
                @pl.when(condition)
                def _():
                    one, two = values(pre, p, part), values(elem, p, full)
                    put(out, p, part, carry_state(one, two) if part is STATE else join(one, two))
            for condition, part in rights:
                @pl.when(condition)
                def _():
                    one, two = values(elem, p, full), values(suf, p, part)
                    put(out, p, part, carry_info(one, two) if part is INFO else join(one, two))
        each_send(p, level, lambda copy: copy.start())

    def take_level(p, level):
        size = 1 << level
        right = (chip // size) % 2 == 1
        left = jnp.logical_not(right)
        if chips == 2 * size:
            cases = ((right, STATE, True), (left, INFO, False))
        else:
            low, high = chip < 2 * size, chip >= chips - 2 * size
            cases = (
                (jnp.logical_and(right, low), STATE, True),
                (jnp.logical_and(right, jnp.logical_not(low)), full, True),
                (jnp.logical_and(left, high), INFO, False),
                (jnp.logical_and(left, jnp.logical_not(high)), full, False),
            )
        for condition, part, earlier in cases:
            @pl.when(condition)
            def _():
                level_copy(p, level, 0, chip, part).wait_recv()
                bare = chip % size == (0 if earlier else size - 1)
                mine = pre if earlier else suf

                def keep():
                    put(mine, p, part, values(got.at[level], p, part))

                def merge():
                    new = values(got.at[level], p, part)
                    old = values(mine, p, full)
                    if part is STATE:
                        put(mine, p, part, carry_state(new, old))
                    elif part is INFO:
                        put(mine, p, part, carry_info(old, new))
                    else:
                        put(mine, p, part, join(new, old) if earlier else join(old, new))

                if size == 1:
                    keep()
                else:
                    pl.when(bare)(keep)
                    pl.when(jnp.logical_not(bare))(merge)

    straight = (((1, STATE), (3, STATE)), ((0, full), (3, full)), ((0, full), (3, full)), ((2, INFO), (0, INFO)))
    stepped = (((1, STATE),), ((0, full),), ((3, full),), ((2, INFO),))
    hops = (stepped, straight, straight)
    relays = ((2, 3), (2,), (2,))

    def tell():
        @pl.when(chip == 0)
        def _():
            pl.semaphore_wait(hello.at[0], 3)
            for target in range(1, 4):
                pl.semaphore_signal(hello.at[0], inc=1, device_id={"tm": CORES * target + core})

    def direct_copy(p, sender, d, relayed=False):
        if relayed:
            src, target, part = incl.at[0], relays[p][d], STATE if sender == 1 else INFO
            if sender == 2:
                target = 3 - target
            d = d + 2
        else:
            src, (target, part) = elem, hops[p][sender][d]
        return pltpu.make_async_remote_copy(
            src_ref=cut(src, p, part), dst_ref=cut(got.at[sender], p, part),
            send_sem=level_send.at[p, d], recv_sem=level_recv.at[p, sender],
            device_id={"tm": CORES * target + core})

    def direct_each(p, act):
        for sender in range(4):
            @pl.when(chip == sender)
            def _():
                for d in range(len(hops[p][sender])):
                    act(direct_copy(p, sender, d))

    def arrive(p, sender, part):
        block = cut(got.at[sender], p, part)
        pltpu.make_async_remote_copy(
            src_ref=block, dst_ref=block, send_sem=level_send.at[p, 0],
            recv_sem=level_recv.at[p, sender], device_id={"tm": partner}).wait_recv()
        return values(got.at[sender], p, part)

    def relay(p):
        @pl.when(chip == 1)
        def _():
            state = arrive(p, 0, STATE)
            put(pre, p, STATE, state)
            put(incl.at[0], p, STATE, carry_state(state, values(elem, p, full)))
            for d in range(len(relays[p])):
                direct_copy(p, 1, d, True).start()

        @pl.when(chip == 2)
        def _():
            info = arrive(p, 3, INFO)
            put(suf, p, INFO, info)
            put(incl.at[0], p, INFO, carry_info(values(elem, p, full), info))
            for d in range(len(relays[p])):
                direct_copy(p, 2, d, True).start()

    def collect(p):
        @pl.when(chip == 0)
        def _():
            if len(relays[p]) > 1:
                info = arrive(p, 2, INFO)
            else:
                info = arrive(p, 3, INFO)
                info = carry_info(arrive(p, 2, full), info)
            put(suf, p, INFO, carry_info(arrive(p, 1, full), info))

        @pl.when(chip == 1)
        def _():
            put(suf, p, INFO, arrive(p, 2, INFO))

        @pl.when(chip == 2)
        def _():
            put(pre, p, STATE, arrive(p, 1, STATE))

        @pl.when(chip == 3)
        def _():
            if len(relays[p]) > 1:
                state = arrive(p, 1, STATE)
            else:
                state = arrive(p, 0, STATE)
                state = carry_state(state, arrive(p, 1, full))
            put(pre, p, STATE, carry_state(state, arrive(p, 2, full)))

    def direct_sent(p):
        direct_each(p, lambda copy: copy.wait_send())
        for sender in (1, 2):
            @pl.when(chip == sender)
            def _():
                for d in range(len(relays[p])):
                    direct_copy(p, sender, d, True).wait_send()

    def forward(p):
        slots = PHASES[p]
        m0, m1, p00, p01, p11 = values(pre, p, STATE)
        for t in range(span):
            num, den = obs[slots, 0, t], obs[slots, 1, t]
            inv, w, e, k1, g = gains(num, den, m0, p00, p01)
            for k, value in enumerate((g, w, e, k1, m0 + p00 * e, p00 * inv, p01 * inv)):
                saved[slots, t, k] = value
            m0, m1, p00, p01, p11 = advance(t, den, inv, e, m0, m1, p00, p01, p11)

        put(after, p, STATE, (m0, m1, p00, p01, p11))

    half = pl.ds(pl.multiple_of(core * LANES, LANES), LANES)

    def result_rows(slot):
        return pl.ds(pl.multiple_of(groups[slot] * SUB, SUB) if slot > 1 else groups[slot] * SUB, SUB)

    def result_copy(slot):
        return pltpu.make_async_remote_copy(
            src_ref=res.at[slot, :, other], dst_ref=landed.at[:, :, result_rows(slot), half],
            send_sem=res_send.at[slot], recv_sem=res_recv.at[slot], device_id={"tm": partner})

    def backward(p):
        slots = PHASES[p]
        i0, i1, i00, i01, i11 = values(suf, p, INFO)
        m0, m1, p00, p01, p11 = values(after, p, STATE)
        s, s2 = decay**span, decay ** (2 * span)
        mat = (i00 * s2, i01 * s2, i11 * s2)
        pulled = symv(mat, (m0, m1))
        (n00, n01, n11), (u0, u1) = absorb(mat, (p00, p01, p11),
                                           (i0 * s - pulled[0], i1 * s - pulled[1]))
        for t in reversed(range(span)):
            g, w, e, k1, m0, p00, p01 = (saved[slots, t, k] for k in range(SAVED))
            later = u0 + u1
            f01 = n00 + n01
            f11 = f01 + (n01 + n11)
            mean = m0 + p00 * u0 + p01 * later
            g0, g1 = p00 * n00 + p01 * f01, p00 * f01 + p01 * f11
            res[slots, 0, t] = inverse(1.0 + jnp.exp(mean * -(decay**t)))
            res[slots, 1, t] = (p00 - (p00 * g0 + p01 * g1)) * decay ** (2 * t)
            u0, u1 = (e + g * u0) - k1 * u1, later
            n00, n01, n11 = ((w + (g * g) * n00) + ((k1 * k1) * n11 - (2.0 * (g * k1)) * n01),
                             (g * n00 - k1 * n01) + (g * n01 - k1 * n11), f11)
            if t == 0 or t == frames:
                @pl.when(core == (1 if t == 0 else 0))
                def _():
                    for slot in range(slots.start, slots.stop):
                        result_copy(slot).start()
        for slot in range(slots.start, slots.stop):
            landed[:, :, result_rows(slot), half] = res[slot, :, own]

    def send(p):
        if chips == 4:
            direct_each(p, lambda copy: copy.start())
        else:
            send_level(p, 0)

    def halos(direction, there):
        @pl.when(there)
        def _():
            for sender in range(CORES):
                halo_arrived(direction, sender)

    to_partner.wait_recv()
    summary(0)
    if chips == 4:
        tell()
    send(0)
    halos(0, jnp.logical_and(has_up, has_down))
    summary(1)
    if chips == 4:
        @pl.when(chip > 0)
        def _():
            pl.semaphore_wait(hello.at[0], 1)

    send(1)
    halos(1, has_down)
    halos(0, jnp.logical_and(has_up, jnp.logical_not(has_down)))
    summary(2)
    send(2)
    order = range(len(PHASES))
    if chips == 4:
        for p in order:
            relay(p)

        @pl.when(chip < 2)
        def _():
            for p in order:
                forward(p)
    else:
        for level in range(levels):
            for p in order:
                take_level(p, level)
                if level + 1 < levels:
                    send_level(p, level + 1)

    def finish(p):
        if chips == 4:
            collect(p)
            pl.when(chip >= 2)(functools.partial(forward, p))
        else:
            forward(p)
        backward(p)

    def sent(p):
        if chips == 4:
            direct_sent(p)
        else:
            for level in range(levels):
                each_send(p, level, lambda copy: copy.wait_send())

    finish(0)
    sent(0)
    finish(1)
    sent(1)
    finish(2)
    sent(2)
    for direction, there in ((0, has_down), (1, has_up)):
        @pl.when(there)
        def _():
            for crossed in range(2):
                halo(direction, crossed).wait_send()
    to_partner.wait_send()
    for slot in range(SLOTS):
        result_copy(slot).wait_send()
        result_copy(slot).wait_recv()


def hand_out(landed, occupancy, spread, sems):
    copies = [pltpu.make_async_copy(landed.at[k], out, sems.at[k])
              for k, out in enumerate((occupancy, spread))]
    for copy in copies:
        copy.start()
    for copy in copies:
        copy.wait()


def solution(mesh):
    tm_count, space_count = mesh.shape["tm"], mesh.shape["space"]

    def body(hits, misses):
        frames, rows, cols = hits.shape
        span, chips = CORES * frames, tm_count // CORES
        levels = chips.bit_length() - 1
        cells = (SUB, LANES)
        assert rows == 4 * SUB and cols == CORES * LANES and chips == 1 << levels
        f32 = jnp.float32
        hbm = pl.BlockSpec(memory_space=pltpu.HBM)
        vmem = pl.BlockSpec(memory_space=pltpu.VMEM)
        dma = pltpu.SemaphoreType.DMA
        landed = pl.pallas_call(
            functools.partial(kernel, tm_count, space_count),
            out_shape=pltpu.VMEM((2, frames, rows, cols), f32),
            in_specs=[hbm] * 2,
            out_specs=vmem,
            scratch_shapes=[
                pltpu.VMEM(hits.shape, jnp.int32),
                pltpu.VMEM(hits.shape, jnp.int32),
                pltpu.VMEM((2, frames, rows, cols), f32),
                pltpu.VMEM((2, span, rows + 2 * SUB, LANES), f32),
                pltpu.VMEM((2, frames, rows, LANES), f32),
                pltpu.VMEM((SLOTS, 2, span) + cells, f32),
                pltpu.VMEM((SLOTS, VALUES) + cells, f32),
                pltpu.VMEM((max(levels - 1, 1), SLOTS, VALUES) + cells, f32),
                pltpu.VMEM((max(levels, 4), SLOTS, VALUES) + cells, f32),
                pltpu.VMEM((SLOTS, VALUES) + cells, f32),
                pltpu.VMEM((SLOTS, VALUES) + cells, f32),
                pltpu.VMEM((SLOTS, 5) + cells, f32),
                pltpu.VMEM((SLOTS, span, SAVED) + cells, f32),
                pltpu.VMEM((SLOTS, 2, span) + cells, f32),
                dma((2, 2, 2)),
                dma((2, 2)),
                dma((2, 2)),
                dma((1,)),
                dma((1,)),
                dma((3, 4) if chips == 4 else (3, levels, chips // 2)),
                dma((3, max(levels, 4))),
                dma((SLOTS,)),
                dma((SLOTS,)),
                pltpu.SemaphoreType.REGULAR((1,)),
            ],
            compiler_params=pltpu.CompilerParams(
                collective_id=0, has_side_effects=True, vmem_limit_bytes=32 * 1024 * 1024),
        )(pltpu.with_memory_space_constraint(hits, pltpu.HBM),
          pltpu.with_memory_space_constraint(misses, pltpu.HBM))
        out = jax.ShapeDtypeStruct(hits.shape, f32)
        return pl.pallas_call(
            hand_out,
            out_shape=(out, out),
            in_specs=[vmem],
            out_specs=(hbm, hbm),
            scratch_shapes=[dma((2,))],
            compiler_params=pltpu.CompilerParams(vmem_limit_bytes=8 * 1024 * 1024),
        )(landed)

    placed = P("tm", "space", None)
    return jax.shard_map(body, mesh=mesh, in_specs=(placed, placed),
                         out_specs=(placed, placed), check_vma=False)
```

```python
import functools
import math

import jax
import jax.numpy as jnp
from jax import lax
from jax.experimental import pallas as pl
from jax.experimental.pallas import tpu as pltpu
from jax.sharding import PartitionSpec as P

RADIUS = 7
SCALE_T = 64
SUB = 8
LANES = 128
CORES = 2
VALUES = 14
STATE = slice(0, 5)
INFO = slice(9, 14)
SAVED = 7
SLOTS = 4
PHASES = (slice(0, 2), slice(2, 3), slice(3, 4))
GREETED = ((1, 2, 3), (3,), (3,), (1, 2))

sigma_cells = 3.0
prior_var = 4.0


def dynamics():
    q = math.sqrt(3.0) / SCALE_T
    decay = math.exp(-q)
    p0, p1 = prior_var, prior_var * q * q
    prior = (p0, q * p0, q * q * p0 + p1)
    a, b, c = prior
    noise = (
        a - decay**2 * (a + 2.0 * b + c),
        b - decay**2 * (b + c),
        c - decay**2 * c,
    )
    return decay, prior, noise


def taps():
    raw = [math.exp(-o * o / (2.0 * sigma_cells**2)) for o in range(-RADIUS, RADIUS + 1)]
    total = sum(raw)
    return [r / total for r in raw], total


def inverse(x):
    return pl.reciprocal(x, approx=True)


def absorb(x, y, g):
    x00, x01, x11 = x
    y00, y01, y11 = y
    d00 = 1.0 + (x00 * y00 + x01 * y01)
    d01 = x00 * y01 + x01 * y11
    d10 = x01 * y00 + x11 * y01
    d11 = 1.0 + (x01 * y01 + x11 * y11)
    inv = inverse(d00 * d11 - d01 * d10)
    det = x00 * x11 - x01 * x01
    out = ((x00 + y11 * det) * inv, (x01 - y01 * det) * inv, (x11 + y00 * det) * inv)
    vec = ((d11 * g[0] - d01 * g[1]) * inv, (d00 * g[1] - d10 * g[0]) * inv)
    return out, vec


def congruent(a, s):
    a00, a01, a10, a11 = a
    s00, s01, s11 = s
    u0, u1 = a00 * s00 + a01 * s01, a00 * s01 + a01 * s11
    v0, v1 = a10 * s00 + a11 * s01, a10 * s01 + a11 * s11
    return u0 * a00 + u1 * a01, u0 * a10 + u1 * a11, v0 * a10 + v1 * a11


def symv(s, v):
    return s[0] * v[0] + s[1] * v[1], s[1] * v[0] + s[2] * v[1]


def matv(a, v):
    return a[0] * v[0] + a[1] * v[1], a[2] * v[0] + a[3] * v[1]


def add(*parts):
    return tuple(sum(p[1:], p[0]) for p in zip(*parts))


def carry_state(state, block):
    mean, cov = state[:2], state[2:]
    shift = symv(cov, block[9:11])
    cov, mean = absorb(cov, block[11:14], add(mean, shift))
    a = block[5:9]
    return add(matv(a, mean), block[0:2]) + add(congruent(a, cov), block[2:5])


def carry_info(block, info):
    vec, mat = info[:2], info[2:]
    pulled = symv(mat, block[0:2])
    s, v = absorb(mat, block[2:5], (vec[0] - pulled[0], vec[1] - pulled[1]))
    a00, a01, a10, a11 = block[5:9]
    back = (a00, a10, a01, a11)
    return add(matv(back, v), block[9:11]) + add(congruent(back, s), block[11:14])


def join(one, two):
    state = carry_state(one[0:5], two)
    info = carry_info(one, two[9:14])
    c, j = one[2:5], two[11:14]
    d00 = 1.0 + (c[0] * j[0] + c[1] * j[1])
    d01 = c[0] * j[1] + c[1] * j[2]
    d10 = c[1] * j[0] + c[2] * j[1]
    d11 = 1.0 + (c[1] * j[1] + c[2] * j[2])
    inv = inverse(d00 * d11 - d01 * d10)
    a00, a01, a10, a11 = one[5:9]
    m = (
        (d11 * a00 - d01 * a10) * inv,
        (d11 * a01 - d01 * a11) * inv,
        (d00 * a10 - d10 * a00) * inv,
        (d00 * a11 - d10 * a01) * inv,
    )
    b00, b01, b10, b11 = two[5:9]
    a = (
        b00 * m[0] + b01 * m[2],
        b00 * m[1] + b01 * m[3],
        b10 * m[0] + b11 * m[2],
        b10 * m[1] + b11 * m[3],
    )
    return state + a + info


def kernel(tm_count, space_count, hits_hbm, misses_hbm, landed, hits, misses, chan, field,
           give, obs, elem, incl, got, pre, suf, after, saved, res, load, halo_send, halo_recv,
           pair_send, pair_recv, level_send, level_recv, res_send, res_recv, hello):
    frames, rows, cols = hits.shape
    parts = ((slice(0, SUB), slice(rows - SUB, rows)), (slice(SUB, rows - SUB),))

    def loads(part):
        return [pltpu.make_async_copy(src.at[:, cut, :], dst.at[:, cut, :], load.at[k, part, j])
                for j, cut in enumerate(parts[part])
                for k, (src, dst) in enumerate(((hits_hbm, hits), (misses_hbm, misses)))]

    span = CORES * frames
    chips = tm_count // CORES
    levels = chips.bit_length() - 1
    me = lax.axis_index("tm")
    tile = lax.axis_index("space")
    chip, core = me // CORES, me % CORES
    partner = me + 1 - 2 * core
    decay, prior, noise = dynamics()
    weights, total = taps()
    has_up = tile > 0
    has_down = tile < space_count - 1
    barrier = pltpu.get_barrier_semaphore()

    @pl.when(has_up)
    def _():
        pl.semaphore_signal(barrier, inc=1, device_id={"space": tile - 1})
        pl.semaphore_signal(barrier, inc=1, device_id={"tm": partner, "space": tile - 1})

    @pl.when(has_down)
    def _():
        pl.semaphore_signal(barrier, inc=1, device_id={"space": tile + 1})
        pl.semaphore_signal(barrier, inc=1, device_id={"tm": partner, "space": tile + 1})

    pl.semaphore_signal(barrier, inc=1, device_id={"tm": partner})

    if chips == 4:
        for sender, targets in enumerate(GREETED):
            @pl.when(chip == sender)
            def _():
                for target in targets:
                    pl.semaphore_signal(barrier, inc=1, device_id={"tm": CORES * target + core})

        greetings = (chip > 0).astype(jnp.int32) * 2 + (chip == 3).astype(jnp.int32)
    else:
        def greet(k, carry):
            pl.semaphore_signal(barrier, inc=1,
                                device_id={"tm": CORES * ((chip + k) % chips) + core})
            return carry

        lax.fori_loop(1, chips, greet, 0)
        greetings = chips - 1

    for part in range(2):
        for copy in loads(part):
            copy.start()

    own = pl.ds(core * frames, frames)
    other = pl.ds((1 - core) * frames, frames)
    cells = (SUB, LANES)

    @pl.when(jnp.logical_not(has_up))
    def _():
        field[:, :, 0:SUB, :] = jnp.zeros((2, span, SUB, LANES), jnp.float32)

    @pl.when(jnp.logical_not(has_down))
    def _():
        field[:, :, SUB + rows :, :] = jnp.zeros((2, span, SUB, LANES), jnp.float32)

    @pl.when(chip == 0)
    def _():
        for slot in range(SLOTS):
            for k, value in enumerate((0.0, 0.0) + prior):
                pre[slot, k] = jnp.full(cells, value, jnp.float32)

    @pl.when(chip == chips - 1)
    def _():
        suf[:, INFO] = jnp.zeros((SLOTS, 5) + cells, jnp.float32)

    column = lax.broadcasted_iota(jnp.int32, (cols, cols), 1) + core * LANES
    column = jnp.where(column >= cols, column - cols, column)
    offset = lax.broadcasted_iota(jnp.int32, (cols, cols), 0) - column
    far = offset.astype(jnp.float32)
    band = jnp.where(jnp.abs(offset) <= RADIUS,
                     jnp.exp(-far * far / (2.0 * sigma_cells**2)) / total, 0.0)
    band_high = band.astype(jnp.bfloat16)
    band_low = (band - band_high.astype(jnp.float32)).astype(jnp.bfloat16)

    late = core.astype(jnp.float32)
    base = 1.0 + late * (decay**frames - 1.0)
    base2 = 1.0 + late * (decay ** (2 * frames) - 1.0)
    dot = functools.partial(jnp.dot, preferred_element_type=jnp.float32)

    def prepare(part):
        for copy in loads(part):
            copy.wait()
        for cut in parts[part]:
            size = cut.stop - cut.start
            for f in range(frames):
                h, m = hits[f, cut, :], misses[f, cut, :]
                hp = h.astype(jnp.float32) + 1.0
                mp = m.astype(jnp.float32) + 1.0
                inv = inverse(hp + mp)
                weight = (h + m).astype(jnp.float32) * (hp * inv) * (mp * inv)
                chan[0, f, cut, :] = weight * (jnp.log(hp) - jnp.log(mp)) * (base * decay**f)
                chan[1, f, cut, :] = weight * (base2 * decay ** (2 * f))
        for cut in parts[part]:
            size = cut.stop - cut.start
            flat = chan[:, :, cut, :].reshape(2 * frames * size, cols)
            high = flat.astype(jnp.bfloat16)
            low = (flat - high.astype(jnp.float32)).astype(jnp.bfloat16)
            out = dot(high, band_high) + (dot(low, band_high) + dot(high, band_low))
            out = out.reshape(2, frames, size, cols)
            field[:, own, SUB + cut.start : SUB + cut.stop, :] = out[..., :LANES]
            give[:, :, cut, :] = out[..., LANES:]

    prepare(0)
    prepare(1)
    neighbours = has_up.astype(jnp.int32) + has_down.astype(jnp.int32)
    pl.semaphore_wait(barrier, 1 + greetings + 2 * neighbours)

    top, bottom = pl.ds(SUB - RADIUS, RADIUS), pl.ds(SUB + rows, RADIUS)

    def halo(direction, crossed):
        step = 1 - 2 * direction
        where = bottom if direction else top
        if crossed:
            row = pl.ds(0, RADIUS) if direction else pl.ds(rows - RADIUS, RADIUS)
            source, target = give.at[:, :, row, :], {"tm": partner, "space": tile + step}
        else:
            row = pl.ds(SUB, RADIUS) if direction else pl.ds(SUB + rows - RADIUS, RADIUS)
            source, target = field.at[:, own, row, :], {"space": tile + step}
        return pltpu.make_async_remote_copy(
            src_ref=source, dst_ref=field.at[:, own, where, :],
            send_sem=halo_send.at[direction, crossed],
            recv_sem=halo_recv.at[direction, core], device_id=target)

    def halo_arrived(direction, sender):
        where = bottom if direction else top
        part = field.at[:, pl.ds(sender * frames, frames), where, :]
        pltpu.make_async_remote_copy(
            src_ref=part, dst_ref=part, send_sem=halo_send.at[direction, 0],
            recv_sem=halo_recv.at[direction, sender], device_id={"tm": partner}).wait_recv()

    for direction, there in ((0, has_down), (1, has_up)):
        @pl.when(there)
        def _():
            for crossed in range(2):
                halo(direction, crossed).start()

    if chips == 4:
        @pl.when(chip > 0)
        def _():
            pl.semaphore_signal(hello.at[0], inc=1, device_id={"tm": core})

    to_partner = pltpu.make_async_remote_copy(
        src_ref=give, dst_ref=field.at[:, own, pl.ds(SUB, rows), :],
        send_sem=pair_send.at[0], recv_sem=pair_recv.at[0], device_id={"tm": partner})
    to_partner.start()

    early = jnp.where(has_down, 0, rows // SUB - 1)
    groups = (1, 2, early, rows // SUB - 1 - early)

    def down(c, t, slot, row):
        def at(s):
            low = SUB - RADIUS + s
            if slot < 2:
                low = low + groups[slot] * SUB
                return field[c, t, low : low + SUB, :]
            return field[c, t, pl.ds(row + low, SUB), :]

        out = weights[RADIUS] * at(RADIUS)
        for s in range(RADIUS):
            out = out + weights[s] * (at(s) + at(2 * RADIUS - s))
        return out

    first = (chip == 0).astype(jnp.float32)

    def scaled_noise(t):
        return tuple(v * decay ** (-2 * (t + 1)) for v in noise)

    def gains(num, den, m0, p00, p01):
        inv = inverse(1.0 + p00 * den)
        k1 = (p01 * den) * inv
        return inv, den * inv, (num - den * m0) * inv, k1, inv - k1

    def advance(t, den, inv, e, m0, m1, p00, p01, p11):
        q00, q01, q11 = scaled_noise(t)
        lost = p01 * (p01 * den)
        both, rest = p00 + p01, p01 - lost
        return ((m0 + m1) + both * e, m1 + p01 * e, (both + rest) * inv + (p11 + q00),
                rest * inv + (p11 + q01), (p11 + q11) - lost * inv)

    full = slice(0, VALUES)

    def summary(p):
        slots = PHASES[p]
        row = groups[slots.start] * SUB
        zero = jnp.zeros((slots.stop - slots.start,) + cells, jnp.float32)
        m0 = m1 = a01 = c0 = eta0 = eta1 = j00 = j01 = j11 = zero
        a00 = c1 = zero + 1.0
        p00, p01, p11 = (zero + v * first for v in prior)
        for t in range(span):
            for c in range(2):
                for slot in range(slots.start, slots.stop):
                    obs[slot, c, t] = down(c, t, slot, row)
            num, den = obs[slots, 0, t], obs[slots, 1, t]
            inv, w, e, k1, g = gains(num, den, m0, p00, p01)
            eta0, eta1 = eta0 + a00 * e, eta1 + a01 * e
            w0, w1 = w * a00, w * a01
            j00, j01, j11 = j00 + w0 * a00, j01 + w0 * a01, j11 + w1 * a01
            a00, a01, c0, c1 = a00 * g + c0, a01 * g + c1, c0 - k1 * a00, c1 - k1 * a01
            m0, m1, p00, p01, p11 = advance(t, den, inv, e, m0, m1, p00, p01, p11)
        s, s2 = decay**span, decay ** (2 * span)
        block = (m0 * s, m1 * s, p00 * s2, p01 * s2, p11 * s2,
                 a00 * s, a01 * s, c0 * s, c1 * s, eta0, eta1, j00, j01, j11)
        put(elem, p, full, block)

    def values(ref, p, part):
        return tuple(ref[PHASES[p], k] for k in range(part.start, part.stop))

    def put(ref, p, part, items):
        for k, item in zip(range(part.start, part.stop), items):
            ref[PHASES[p], k] = item

    def cut(ref, p, part):
        slots = PHASES[p]
        return ref.at[pl.ds(slots.start, slots.stop - slots.start),
                      pl.ds(part.start, part.stop - part.start)]

    def level_copy(p, level, d, target, part):
        src = elem if level == 0 else incl.at[level - 1]
        return pltpu.make_async_remote_copy(
            src_ref=cut(src, p, part), dst_ref=cut(got.at[level], p, part),
            send_sem=level_send.at[p, level, d], recv_sem=level_recv.at[p, level],
            device_id={"tm": CORES * target + core})

    def branches(level):
        size = 1 << level
        ends = chip % (2 * size) == size - 1
        starts = chip % (2 * size) == size
        if chips == 2 * size:
            return ((ends, STATE),), ((starts, INFO),)
        lone = chip == size - 1
        last = chip == chips - size
        return (((lone, STATE), (jnp.logical_and(ends, jnp.logical_not(lone)), full)),
                ((last, INFO), (jnp.logical_and(starts, jnp.logical_not(last)), full)))

    def each_send(p, level, act):
        size = 1 << level
        lefts, rights = branches(level)
        for group, step in ((lefts, 1), (rights, -1)):
            for condition, part in group:
                @pl.when(condition)
                def _():
                    for d in range(size):
                        act(level_copy(p, level, d, chip + step * (d + 1), part))

    def send_level(p, level):
        if level:
            out = incl.at[level - 1]
            lefts, rights = branches(level)
            for condition, part in lefts:
                @pl.when(condition)
                def _():
                    one, two = values(pre, p, part), values(elem, p, full)
                    put(out, p, part, carry_state(one, two) if part is STATE else join(one, two))
            for condition, part in rights:
                @pl.when(condition)
                def _():
                    one, two = values(elem, p, full), values(suf, p, part)
                    put(out, p, part, carry_info(one, two) if part is INFO else join(one, two))
        each_send(p, level, lambda copy: copy.start())

    def take_level(p, level):
        size = 1 << level
        right = (chip // size) % 2 == 1
        left = jnp.logical_not(right)
        if chips == 2 * size:
            cases = ((right, STATE, True), (left, INFO, False))
        else:
            low, high = chip < 2 * size, chip >= chips - 2 * size
            cases = (
                (jnp.logical_and(right, low), STATE, True),
                (jnp.logical_and(right, jnp.logical_not(low)), full, True),
                (jnp.logical_and(left, high), INFO, False),
                (jnp.logical_and(left, jnp.logical_not(high)), full, False),
            )
        for condition, part, earlier in cases:
            @pl.when(condition)
            def _():
                level_copy(p, level, 0, chip, part).wait_recv()
                bare = chip % size == (0 if earlier else size - 1)
                mine = pre if earlier else suf

                def keep():
                    put(mine, p, part, values(got.at[level], p, part))

                def merge():
                    new = values(got.at[level], p, part)
                    old = values(mine, p, full)
                    if part is STATE:
                        put(mine, p, part, carry_state(new, old))
                    elif part is INFO:
                        put(mine, p, part, carry_info(old, new))
                    else:
                        put(mine, p, part, join(new, old) if earlier else join(old, new))

                if size == 1:
                    keep()
                else:
                    pl.when(bare)(keep)
                    pl.when(jnp.logical_not(bare))(merge)

    straight = (((1, STATE), (3, STATE)), ((0, full), (3, full)), ((0, full), (3, full)), ((2, INFO), (0, INFO)))
    stepped = (((1, STATE),), ((0, full),), ((3, full),), ((2, INFO),))
    hops = (stepped, straight, straight)
    relays = ((2, 3), (2,), (2,))

    def tell():
        @pl.when(chip == 0)
        def _():
            pl.semaphore_wait(hello.at[0], 3)
            for target in range(1, 4):
                pl.semaphore_signal(hello.at[0], inc=1, device_id={"tm": CORES * target + core})

    def direct_copy(p, sender, d, relayed=False):
        if relayed:
            src, target, part = incl.at[0], relays[p][d], STATE if sender == 1 else INFO
            if sender == 2:
                target = 3 - target
            d = d + 2
        else:
            src, (target, part) = elem, hops[p][sender][d]
        return pltpu.make_async_remote_copy(
            src_ref=cut(src, p, part), dst_ref=cut(got.at[sender], p, part),
            send_sem=level_send.at[p, d], recv_sem=level_recv.at[p, sender],
            device_id={"tm": CORES * target + core})

    def direct_each(p, act):
        for sender in range(4):
            @pl.when(chip == sender)
            def _():
                for d in range(len(hops[p][sender])):
                    act(direct_copy(p, sender, d))

    def arrive(p, sender, part):
        block = cut(got.at[sender], p, part)
        pltpu.make_async_remote_copy(
            src_ref=block, dst_ref=block, send_sem=level_send.at[p, 0],
            recv_sem=level_recv.at[p, sender], device_id={"tm": partner}).wait_recv()
        return values(got.at[sender], p, part)

    def relay(p):
        @pl.when(chip == 1)
        def _():
            state = arrive(p, 0, STATE)
            put(pre, p, STATE, state)
            put(incl.at[0], p, STATE, carry_state(state, values(elem, p, full)))
            for d in range(len(relays[p])):
                direct_copy(p, 1, d, True).start()

        @pl.when(chip == 2)
        def _():
            info = arrive(p, 3, INFO)
            put(suf, p, INFO, info)
            put(incl.at[0], p, INFO, carry_info(values(elem, p, full), info))
            for d in range(len(relays[p])):
                direct_copy(p, 2, d, True).start()

    def collect(p):
        @pl.when(chip == 0)
        def _():
            if len(relays[p]) > 1:
                info = arrive(p, 2, INFO)
            else:
                info = arrive(p, 3, INFO)
                info = carry_info(arrive(p, 2, full), info)
            put(suf, p, INFO, carry_info(arrive(p, 1, full), info))

        @pl.when(chip == 1)
        def _():
            put(suf, p, INFO, arrive(p, 2, INFO))

        @pl.when(chip == 2)
        def _():
            put(pre, p, STATE, arrive(p, 1, STATE))

        @pl.when(chip == 3)
        def _():
            if len(relays[p]) > 1:
                state = arrive(p, 1, STATE)
            else:
                state = arrive(p, 0, STATE)
                state = carry_state(state, arrive(p, 1, full))
            put(pre, p, STATE, carry_state(state, arrive(p, 2, full)))

    def direct_sent(p):
        direct_each(p, lambda copy: copy.wait_send())
        for sender in (1, 2):
            @pl.when(chip == sender)
            def _():
                for d in range(len(relays[p])):
                    direct_copy(p, sender, d, True).wait_send()

    def forward(p):
        slots = PHASES[p]
        m0, m1, p00, p01, p11 = values(pre, p, STATE)
        for t in range(span):
            num, den = obs[slots, 0, t], obs[slots, 1, t]
            inv, w, e, k1, g = gains(num, den, m0, p00, p01)
            for k, value in enumerate((g, w, e, k1, m0 + p00 * e, p00 * inv, p01 * inv)):
                saved[slots, t, k] = value
            m0, m1, p00, p01, p11 = advance(t, den, inv, e, m0, m1, p00, p01, p11)

        put(after, p, STATE, (m0, m1, p00, p01, p11))

    half = pl.ds(pl.multiple_of(core * LANES, LANES), LANES)

    def result_rows(slot):
        return pl.ds(pl.multiple_of(groups[slot] * SUB, SUB) if slot > 1 else groups[slot] * SUB, SUB)

    def result_copy(slot):
        return pltpu.make_async_remote_copy(
            src_ref=res.at[slot, :, other], dst_ref=landed.at[:, :, result_rows(slot), half],
            send_sem=res_send.at[slot], recv_sem=res_recv.at[slot], device_id={"tm": partner})

    def backward(p):
        slots = PHASES[p]
        i0, i1, i00, i01, i11 = values(suf, p, INFO)
        m0, m1, p00, p01, p11 = values(after, p, STATE)
        s, s2 = decay**span, decay ** (2 * span)
        mat = (i00 * s2, i01 * s2, i11 * s2)
        pulled = symv(mat, (m0, m1))
        (n00, n01, n11), (u0, u1) = absorb(mat, (p00, p01, p11),
                                           (i0 * s - pulled[0], i1 * s - pulled[1]))
        for t in reversed(range(span)):
            g, w, e, k1, m0, p00, p01 = (saved[slots, t, k] for k in range(SAVED))
            later = u0 + u1
            f01 = n00 + n01
            f11 = f01 + (n01 + n11)
            mean = m0 + p00 * u0 + p01 * later
            g0, g1 = p00 * n00 + p01 * f01, p00 * f01 + p01 * f11
            res[slots, 0, t] = inverse(1.0 + jnp.exp(mean * -(decay**t)))
            res[slots, 1, t] = (p00 - (p00 * g0 + p01 * g1)) * decay ** (2 * t)
            u0, u1 = (e + g * u0) - k1 * u1, later
            n00, n01, n11 = ((w + (g * g) * n00) + ((k1 * k1) * n11 - (2.0 * (g * k1)) * n01),
                             (g * n00 - k1 * n01) + (g * n01 - k1 * n11), f11)
            if t == 0 or t == frames:
                @pl.when(core == (1 if t == 0 else 0))
                def _():
                    for slot in range(slots.start, slots.stop):
                        result_copy(slot).start()
        for slot in range(slots.start, slots.stop):
            landed[:, :, result_rows(slot), half] = res[slot, :, own]

    def send(p):
        if chips == 4:
            direct_each(p, lambda copy: copy.start())
        else:
            send_level(p, 0)

    def halos(direction, there):
        @pl.when(there)
        def _():
            for sender in range(CORES):
                halo_arrived(direction, sender)

    to_partner.wait_recv()
    summary(0)
    if chips == 4:
        tell()
    send(0)
    halos(0, jnp.logical_and(has_up, has_down))
    summary(1)
    if chips == 4:
        @pl.when(chip > 0)
        def _():
            pl.semaphore_wait(hello.at[0], 1)

    send(1)
    halos(1, has_down)
    halos(0, jnp.logical_and(has_up, jnp.logical_not(has_down)))
    summary(2)
    send(2)
    order = range(len(PHASES))
    if chips == 4:
        for p in order:
            relay(p)

        @pl.when(chip < 2)
        def _():
            for p in order:
                forward(p)
    else:
        for level in range(levels):
            for p in order:
                take_level(p, level)
                if level + 1 < levels:
                    send_level(p, level + 1)

    def finish(p):
        if chips == 4:
            collect(p)
            pl.when(chip >= 2)(functools.partial(forward, p))
        else:
            forward(p)
        backward(p)

    def sent(p):
        if chips == 4:
            direct_sent(p)
        else:
            for level in range(levels):
                each_send(p, level, lambda copy: copy.wait_send())

    if chips == 4:
        @pl.when(chip == 0)
        def _():
            for p in (1, 2, 0):
                finish(p)

        @pl.when(chip > 0)
        def _():
            for p in order:
                finish(p)
    else:
        for p in order:
            finish(p)
    for p in order:
        sent(p)
    for direction, there in ((0, has_down), (1, has_up)):
        @pl.when(there)
        def _():
            for crossed in range(2):
                halo(direction, crossed).wait_send()
    to_partner.wait_send()
    for slot in range(SLOTS):
        result_copy(slot).wait_send()
        result_copy(slot).wait_recv()


def hand_out(landed, occupancy, spread, sems):
    copies = [pltpu.make_async_copy(landed.at[k], out, sems.at[k])
              for k, out in enumerate((occupancy, spread))]
    for copy in copies:
        copy.start()
    for copy in copies:
        copy.wait()


def solution(mesh):
    tm_count, space_count = mesh.shape["tm"], mesh.shape["space"]

    def body(hits, misses):
        frames, rows, cols = hits.shape
        span, chips = CORES * frames, tm_count // CORES
        levels = chips.bit_length() - 1
        cells = (SUB, LANES)
        assert rows == 4 * SUB and cols == CORES * LANES and chips == 1 << levels
        f32 = jnp.float32
        hbm = pl.BlockSpec(memory_space=pltpu.HBM)
        vmem = pl.BlockSpec(memory_space=pltpu.VMEM)
        dma = pltpu.SemaphoreType.DMA
        landed = pl.pallas_call(
            functools.partial(kernel, tm_count, space_count),
            out_shape=pltpu.VMEM((2, frames, rows, cols), f32),
            in_specs=[hbm] * 2,
            out_specs=vmem,
            scratch_shapes=[
                pltpu.VMEM(hits.shape, jnp.int32),
                pltpu.VMEM(hits.shape, jnp.int32),
                pltpu.VMEM((2, frames, rows, cols), f32),
                pltpu.VMEM((2, span, rows + 2 * SUB, LANES), f32),
                pltpu.VMEM((2, frames, rows, LANES), f32),
                pltpu.VMEM((SLOTS, 2, span) + cells, f32),
                pltpu.VMEM((SLOTS, VALUES) + cells, f32),
                pltpu.VMEM((max(levels - 1, 1), SLOTS, VALUES) + cells, f32),
                pltpu.VMEM((max(levels, 4), SLOTS, VALUES) + cells, f32),
                pltpu.VMEM((SLOTS, VALUES) + cells, f32),
                pltpu.VMEM((SLOTS, VALUES) + cells, f32),
                pltpu.VMEM((SLOTS, 5) + cells, f32),
                pltpu.VMEM((SLOTS, span, SAVED) + cells, f32),
                pltpu.VMEM((SLOTS, 2, span) + cells, f32),
                dma((2, 2, 2)),
                dma((2, 2)),
                dma((2, 2)),
                dma((1,)),
                dma((1,)),
                dma((3, 4) if chips == 4 else (3, levels, chips // 2)),
                dma((3, max(levels, 4))),
                dma((SLOTS,)),
                dma((SLOTS,)),
                pltpu.SemaphoreType.REGULAR((1,)),
            ],
            compiler_params=pltpu.CompilerParams(
                collective_id=0, has_side_effects=True, vmem_limit_bytes=32 * 1024 * 1024),
        )(pltpu.with_memory_space_constraint(hits, pltpu.HBM),
          pltpu.with_memory_space_constraint(misses, pltpu.HBM))
        out = jax.ShapeDtypeStruct(hits.shape, f32)
        return pl.pallas_call(
            hand_out,
            out_shape=(out, out),
            in_specs=[vmem],
            out_specs=(hbm, hbm),
            scratch_shapes=[dma((2,))],
            compiler_params=pltpu.CompilerParams(vmem_limit_bytes=8 * 1024 * 1024),
        )(landed)

    placed = P("tm", "space", None)
    return jax.shard_map(body, mesh=mesh, in_specs=(placed, placed),
                         out_specs=(placed, placed), check_vma=False)
```

```python
import functools
import math

import jax
import jax.numpy as jnp
from jax import lax
from jax.experimental import pallas as pl
from jax.experimental.pallas import tpu as pltpu
from jax.sharding import PartitionSpec as P

RADIUS = 7
SCALE_T = 64
SUB = 8
LANES = 128
CORES = 2
VALUES = 14
STATE = slice(0, 5)
INFO = slice(9, 14)
SAVED = 7
SLOTS = 4
PHASES = (slice(0, 2), slice(2, 3), slice(3, 4))
GREETED = ((1, 2, 3), (3,), (3,), (1, 2))

sigma_cells = 3.0
prior_var = 4.0


def dynamics():
    q = math.sqrt(3.0) / SCALE_T
    decay = math.exp(-q)
    p0, p1 = prior_var, prior_var * q * q
    prior = (p0, q * p0, q * q * p0 + p1)
    a, b, c = prior
    noise = (
        a - decay**2 * (a + 2.0 * b + c),
        b - decay**2 * (b + c),
        c - decay**2 * c,
    )
    return decay, prior, noise


def taps():
    raw = [math.exp(-o * o / (2.0 * sigma_cells**2)) for o in range(-RADIUS, RADIUS + 1)]
    total = sum(raw)
    return [r / total for r in raw], total


def inverse(x):
    return pl.reciprocal(x, approx=True)


def absorb(x, y, g):
    x00, x01, x11 = x
    y00, y01, y11 = y
    d00 = 1.0 + (x00 * y00 + x01 * y01)
    d01 = x00 * y01 + x01 * y11
    d10 = x01 * y00 + x11 * y01
    d11 = 1.0 + (x01 * y01 + x11 * y11)
    inv = inverse(d00 * d11 - d01 * d10)
    det = x00 * x11 - x01 * x01
    out = ((x00 + y11 * det) * inv, (x01 - y01 * det) * inv, (x11 + y00 * det) * inv)
    vec = ((d11 * g[0] - d01 * g[1]) * inv, (d00 * g[1] - d10 * g[0]) * inv)
    return out, vec


def congruent(a, s):
    a00, a01, a10, a11 = a
    s00, s01, s11 = s
    u0, u1 = a00 * s00 + a01 * s01, a00 * s01 + a01 * s11
    v0, v1 = a10 * s00 + a11 * s01, a10 * s01 + a11 * s11
    return u0 * a00 + u1 * a01, u0 * a10 + u1 * a11, v0 * a10 + v1 * a11


def symv(s, v):
    return s[0] * v[0] + s[1] * v[1], s[1] * v[0] + s[2] * v[1]


def matv(a, v):
    return a[0] * v[0] + a[1] * v[1], a[2] * v[0] + a[3] * v[1]


def add(*parts):
    return tuple(sum(p[1:], p[0]) for p in zip(*parts))


def carry_state(state, block):
    mean, cov = state[:2], state[2:]
    shift = symv(cov, block[9:11])
    cov, mean = absorb(cov, block[11:14], add(mean, shift))
    a = block[5:9]
    return add(matv(a, mean), block[0:2]) + add(congruent(a, cov), block[2:5])


def carry_info(block, info):
    vec, mat = info[:2], info[2:]
    pulled = symv(mat, block[0:2])
    s, v = absorb(mat, block[2:5], (vec[0] - pulled[0], vec[1] - pulled[1]))
    a00, a01, a10, a11 = block[5:9]
    back = (a00, a10, a01, a11)
    return add(matv(back, v), block[9:11]) + add(congruent(back, s), block[11:14])


def join(one, two):
    state = carry_state(one[0:5], two)
    info = carry_info(one, two[9:14])
    c, j = one[2:5], two[11:14]
    d00 = 1.0 + (c[0] * j[0] + c[1] * j[1])
    d01 = c[0] * j[1] + c[1] * j[2]
    d10 = c[1] * j[0] + c[2] * j[1]
    d11 = 1.0 + (c[1] * j[1] + c[2] * j[2])
    inv = inverse(d00 * d11 - d01 * d10)
    a00, a01, a10, a11 = one[5:9]
    m = (
        (d11 * a00 - d01 * a10) * inv,
        (d11 * a01 - d01 * a11) * inv,
        (d00 * a10 - d10 * a00) * inv,
        (d00 * a11 - d10 * a01) * inv,
    )
    b00, b01, b10, b11 = two[5:9]
    a = (
        b00 * m[0] + b01 * m[2],
        b00 * m[1] + b01 * m[3],
        b10 * m[0] + b11 * m[2],
        b10 * m[1] + b11 * m[3],
    )
    return state + a + info


def kernel(tm_count, space_count, hits_hbm, misses_hbm, landed, hits, misses, chan, field,
           give, obs, elem, incl, got, pre, suf, after, saved, res, load, halo_send, halo_recv,
           pair_send, pair_recv, level_send, level_recv, res_send, res_recv, hello):
    frames, rows, cols = hits.shape
    parts = ((slice(0, SUB), slice(rows - SUB, rows)), (slice(SUB, rows - SUB),))

    def loads(part):
        return [pltpu.make_async_copy(src.at[:, cut, :], dst.at[:, cut, :], load.at[k, part, j])
                for j, cut in enumerate(parts[part])
                for k, (src, dst) in enumerate(((hits_hbm, hits), (misses_hbm, misses)))]

    span = CORES * frames
    chips = tm_count // CORES
    levels = chips.bit_length() - 1
    me = lax.axis_index("tm")
    tile = lax.axis_index("space")
    chip, core = me // CORES, me % CORES
    partner = me + 1 - 2 * core
    decay, prior, noise = dynamics()
    weights, total = taps()
    has_up = tile > 0
    has_down = tile < space_count - 1
    barrier = pltpu.get_barrier_semaphore()

    @pl.when(has_up)
    def _():
        pl.semaphore_signal(barrier, inc=1, device_id={"space": tile - 1})
        pl.semaphore_signal(barrier, inc=1, device_id={"tm": partner, "space": tile - 1})

    @pl.when(has_down)
    def _():
        pl.semaphore_signal(barrier, inc=1, device_id={"space": tile + 1})
        pl.semaphore_signal(barrier, inc=1, device_id={"tm": partner, "space": tile + 1})

    pl.semaphore_signal(barrier, inc=1, device_id={"tm": partner})

    if chips == 4:
        for sender, targets in enumerate(GREETED):
            @pl.when(chip == sender)
            def _():
                for target in targets:
                    pl.semaphore_signal(barrier, inc=1, device_id={"tm": CORES * target + core})

        greetings = (chip > 0).astype(jnp.int32) * 2 + (chip == 3).astype(jnp.int32)
    else:
        def greet(k, carry):
            pl.semaphore_signal(barrier, inc=1,
                                device_id={"tm": CORES * ((chip + k) % chips) + core})
            return carry

        lax.fori_loop(1, chips, greet, 0)
        greetings = chips - 1

    for part in range(2):
        for copy in loads(part):
            copy.start()

    own = pl.ds(core * frames, frames)
    other = pl.ds((1 - core) * frames, frames)
    cells = (SUB, LANES)

    @pl.when(jnp.logical_not(has_up))
    def _():
        field[:, :, 0:SUB, :] = jnp.zeros((2, span, SUB, LANES), jnp.float32)

    @pl.when(jnp.logical_not(has_down))
    def _():
        field[:, :, SUB + rows :, :] = jnp.zeros((2, span, SUB, LANES), jnp.float32)

    @pl.when(chip == 0)
    def _():
        for slot in range(SLOTS):
            for k, value in enumerate((0.0, 0.0) + prior):
                pre[slot, k] = jnp.full(cells, value, jnp.float32)

    @pl.when(chip == chips - 1)
    def _():
        suf[:, INFO] = jnp.zeros((SLOTS, 5) + cells, jnp.float32)

    column = lax.broadcasted_iota(jnp.int32, (cols, cols), 1) + core * LANES
    column = jnp.where(column >= cols, column - cols, column)
    offset = lax.broadcasted_iota(jnp.int32, (cols, cols), 0) - column
    far = offset.astype(jnp.float32)
    band = jnp.where(jnp.abs(offset) <= RADIUS,
                     jnp.exp(-far * far / (2.0 * sigma_cells**2)) / total, 0.0)
    band_high = band.astype(jnp.bfloat16)
    band_low = (band - band_high.astype(jnp.float32)).astype(jnp.bfloat16)

    late = core.astype(jnp.float32)
    base = 1.0 + late * (decay**frames - 1.0)
    base2 = 1.0 + late * (decay ** (2 * frames) - 1.0)
    dot = functools.partial(jnp.dot, preferred_element_type=jnp.float32)

    def prepare(part):
        for copy in loads(part):
            copy.wait()
        for cut in parts[part]:
            size = cut.stop - cut.start
            for f in range(frames):
                h, m = hits[f, cut, :], misses[f, cut, :]
                hp = h.astype(jnp.float32) + 1.0
                mp = m.astype(jnp.float32) + 1.0
                inv = inverse(hp + mp)
                weight = (h + m).astype(jnp.float32) * (hp * inv) * (mp * inv)
                chan[0, f, cut, :] = weight * jnp.log(hp * inverse(mp)) * (base * decay**f)
                chan[1, f, cut, :] = weight * (base2 * decay ** (2 * f))
        for cut in parts[part]:
            size = cut.stop - cut.start
            flat = chan[:, :, cut, :].reshape(2 * frames * size, cols)
            high = flat.astype(jnp.bfloat16)
            low = (flat - high.astype(jnp.float32)).astype(jnp.bfloat16)
            out = dot(high, band_high) + (dot(low, band_high) + dot(high, band_low))
            out = out.reshape(2, frames, size, cols)
            field[:, own, SUB + cut.start : SUB + cut.stop, :] = out[..., :LANES]
            give[:, :, cut, :] = out[..., LANES:]

    prepare(0)
    prepare(1)
    neighbours = has_up.astype(jnp.int32) + has_down.astype(jnp.int32)
    pl.semaphore_wait(barrier, 1 + greetings + 2 * neighbours)

    top, bottom = pl.ds(SUB - RADIUS, RADIUS), pl.ds(SUB + rows, RADIUS)

    def halo(direction, crossed):
        step = 1 - 2 * direction
        where = bottom if direction else top
        if crossed:
            row = pl.ds(0, RADIUS) if direction else pl.ds(rows - RADIUS, RADIUS)
            source, target = give.at[:, :, row, :], {"tm": partner, "space": tile + step}
        else:
            row = pl.ds(SUB, RADIUS) if direction else pl.ds(SUB + rows - RADIUS, RADIUS)
            source, target = field.at[:, own, row, :], {"space": tile + step}
        return pltpu.make_async_remote_copy(
            src_ref=source, dst_ref=field.at[:, own, where, :],
            send_sem=halo_send.at[direction, crossed],
            recv_sem=halo_recv.at[direction, core], device_id=target)

    def halo_arrived(direction, sender):
        where = bottom if direction else top
        part = field.at[:, pl.ds(sender * frames, frames), where, :]
        pltpu.make_async_remote_copy(
            src_ref=part, dst_ref=part, send_sem=halo_send.at[direction, 0],
            recv_sem=halo_recv.at[direction, sender], device_id={"tm": partner}).wait_recv()

    for direction, there in ((0, has_down), (1, has_up)):
        @pl.when(there)
        def _():
            for crossed in range(2):
                halo(direction, crossed).start()

    if chips == 4:
        @pl.when(chip > 0)
        def _():
            pl.semaphore_signal(hello.at[0], inc=1, device_id={"tm": core})

    to_partner = pltpu.make_async_remote_copy(
        src_ref=give, dst_ref=field.at[:, own, pl.ds(SUB, rows), :],
        send_sem=pair_send.at[0], recv_sem=pair_recv.at[0], device_id={"tm": partner})
    to_partner.start()

    early = jnp.where(has_down, 0, rows // SUB - 1)
    groups = (1, 2, early, rows // SUB - 1 - early)

    def down(c, t, slot, row):
        def at(s):
            low = SUB - RADIUS + s
            if slot < 2:
                low = low + groups[slot] * SUB
                return field[c, t, low : low + SUB, :]
            return field[c, t, pl.ds(row + low, SUB), :]

        out = weights[RADIUS] * at(RADIUS)
        for s in range(RADIUS):
            out = out + weights[s] * (at(s) + at(2 * RADIUS - s))
        return out

    first = (chip == 0).astype(jnp.float32)

    def scaled_noise(t):
        return tuple(v * decay ** (-2 * (t + 1)) for v in noise)

    def gains(num, den, m0, p00, p01):
        inv = inverse(1.0 + p00 * den)
        k1 = (p01 * den) * inv
        return inv, den * inv, (num - den * m0) * inv, k1, inv - k1

    def advance(t, den, inv, e, m0, m1, p00, p01, p11):
        q00, q01, q11 = scaled_noise(t)
        lost = p01 * (p01 * den)
        both, rest = p00 + p01, p01 - lost
        return ((m0 + m1) + both * e, m1 + p01 * e, (both + rest) * inv + (p11 + q00),
                rest * inv + (p11 + q01), (p11 + q11) - lost * inv)

    full = slice(0, VALUES)

    def summary(p):
        slots = PHASES[p]
        row = groups[slots.start] * SUB
        zero = jnp.zeros((slots.stop - slots.start,) + cells, jnp.float32)
        m0 = m1 = a01 = c0 = eta0 = eta1 = j00 = j01 = j11 = zero
        a00 = c1 = zero + 1.0
        p00, p01, p11 = (zero + v * first for v in prior)
        for t in range(span):
            for c in range(2):
                for slot in range(slots.start, slots.stop):
                    obs[slot, c, t] = down(c, t, slot, row)
            num, den = obs[slots, 0, t], obs[slots, 1, t]
            inv, w, e, k1, g = gains(num, den, m0, p00, p01)
            eta0, eta1 = eta0 + a00 * e, eta1 + a01 * e
            w0, w1 = w * a00, w * a01
            j00, j01, j11 = j00 + w0 * a00, j01 + w0 * a01, j11 + w1 * a01
            a00, a01, c0, c1 = a00 * g + c0, a01 * g + c1, c0 - k1 * a00, c1 - k1 * a01
            m0, m1, p00, p01, p11 = advance(t, den, inv, e, m0, m1, p00, p01, p11)
        s, s2 = decay**span, decay ** (2 * span)
        block = (m0 * s, m1 * s, p00 * s2, p01 * s2, p11 * s2,
                 a00 * s, a01 * s, c0 * s, c1 * s, eta0, eta1, j00, j01, j11)
        put(elem, p, full, block)

    def values(ref, p, part):
        return tuple(ref[PHASES[p], k] for k in range(part.start, part.stop))

    def put(ref, p, part, items):
        for k, item in zip(range(part.start, part.stop), items):
            ref[PHASES[p], k] = item

    def cut(ref, p, part):
        slots = PHASES[p]
        return ref.at[pl.ds(slots.start, slots.stop - slots.start),
                      pl.ds(part.start, part.stop - part.start)]

    def level_copy(p, level, d, target, part):
        src = elem if level == 0 else incl.at[level - 1]
        return pltpu.make_async_remote_copy(
            src_ref=cut(src, p, part), dst_ref=cut(got.at[level], p, part),
            send_sem=level_send.at[p, level, d], recv_sem=level_recv.at[p, level],
            device_id={"tm": CORES * target + core})

    def branches(level):
        size = 1 << level
        ends = chip % (2 * size) == size - 1
        starts = chip % (2 * size) == size
        if chips == 2 * size:
            return ((ends, STATE),), ((starts, INFO),)
        lone = chip == size - 1
        last = chip == chips - size
        return (((lone, STATE), (jnp.logical_and(ends, jnp.logical_not(lone)), full)),
                ((last, INFO), (jnp.logical_and(starts, jnp.logical_not(last)), full)))

    def each_send(p, level, act):
        size = 1 << level
        lefts, rights = branches(level)
        for group, step in ((lefts, 1), (rights, -1)):
            for condition, part in group:
                @pl.when(condition)
                def _():
                    for d in range(size):
                        act(level_copy(p, level, d, chip + step * (d + 1), part))

    def send_level(p, level):
        if level:
            out = incl.at[level - 1]
            lefts, rights = branches(level)
            for condition, part in lefts:
                @pl.when(condition)
                def _():
                    one, two = values(pre, p, part), values(elem, p, full)
                    put(out, p, part, carry_state(one, two) if part is STATE else join(one, two))
            for condition, part in rights:
                @pl.when(condition)
                def _():
                    one, two = values(elem, p, full), values(suf, p, part)
                    put(out, p, part, carry_info(one, two) if part is INFO else join(one, two))
        each_send(p, level, lambda copy: copy.start())

    def take_level(p, level):
        size = 1 << level
        right = (chip // size) % 2 == 1
        left = jnp.logical_not(right)
        if chips == 2 * size:
            cases = ((right, STATE, True), (left, INFO, False))
        else:
            low, high = chip < 2 * size, chip >= chips - 2 * size
            cases = (
                (jnp.logical_and(right, low), STATE, True),
                (jnp.logical_and(right, jnp.logical_not(low)), full, True),
                (jnp.logical_and(left, high), INFO, False),
                (jnp.logical_and(left, jnp.logical_not(high)), full, False),
            )
        for condition, part, earlier in cases:
            @pl.when(condition)
            def _():
                level_copy(p, level, 0, chip, part).wait_recv()
                bare = chip % size == (0 if earlier else size - 1)
                mine = pre if earlier else suf

                def keep():
                    put(mine, p, part, values(got.at[level], p, part))

                def merge():
                    new = values(got.at[level], p, part)
                    old = values(mine, p, full)
                    if part is STATE:
                        put(mine, p, part, carry_state(new, old))
                    elif part is INFO:
                        put(mine, p, part, carry_info(old, new))
                    else:
                        put(mine, p, part, join(new, old) if earlier else join(old, new))

                if size == 1:
                    keep()
                else:
                    pl.when(bare)(keep)
                    pl.when(jnp.logical_not(bare))(merge)

    straight = (((1, STATE), (3, STATE)), ((0, full), (3, full)), ((0, full), (3, full)), ((2, INFO), (0, INFO)))
    stepped = (((1, STATE),), ((0, full),), ((3, full),), ((2, INFO),))
    hops = (stepped, straight, straight)
    relays = ((2, 3), (2,), (2,))

    def tell():
        @pl.when(chip == 0)
        def _():
            pl.semaphore_wait(hello.at[0], 3)
            for target in range(1, 4):
                pl.semaphore_signal(hello.at[0], inc=1, device_id={"tm": CORES * target + core})

    def direct_copy(p, sender, d, relayed=False):
        if relayed:
            src, target, part = incl.at[0], relays[p][d], STATE if sender == 1 else INFO
            if sender == 2:
                target = 3 - target
            d = d + 2
        else:
            src, (target, part) = elem, hops[p][sender][d]
        return pltpu.make_async_remote_copy(
            src_ref=cut(src, p, part), dst_ref=cut(got.at[sender], p, part),
            send_sem=level_send.at[p, d], recv_sem=level_recv.at[p, sender],
            device_id={"tm": CORES * target + core})

    def direct_each(p, act):
        for sender in range(4):
            @pl.when(chip == sender)
            def _():
                for d in range(len(hops[p][sender])):
                    act(direct_copy(p, sender, d))

    def arrive(p, sender, part):
        block = cut(got.at[sender], p, part)
        pltpu.make_async_remote_copy(
            src_ref=block, dst_ref=block, send_sem=level_send.at[p, 0],
            recv_sem=level_recv.at[p, sender], device_id={"tm": partner}).wait_recv()
        return values(got.at[sender], p, part)

    def relay(p):
        @pl.when(chip == 1)
        def _():
            state = arrive(p, 0, STATE)
            put(pre, p, STATE, state)
            put(incl.at[0], p, STATE, carry_state(state, values(elem, p, full)))
            for d in range(len(relays[p])):
                direct_copy(p, 1, d, True).start()

        @pl.when(chip == 2)
        def _():
            info = arrive(p, 3, INFO)
            put(suf, p, INFO, info)
            put(incl.at[0], p, INFO, carry_info(values(elem, p, full), info))
            for d in range(len(relays[p])):
                direct_copy(p, 2, d, True).start()

    def collect(p):
        @pl.when(chip == 0)
        def _():
            if len(relays[p]) > 1:
                info = arrive(p, 2, INFO)
            else:
                info = arrive(p, 3, INFO)
                info = carry_info(arrive(p, 2, full), info)
            put(suf, p, INFO, carry_info(arrive(p, 1, full), info))

        @pl.when(chip == 1)
        def _():
            put(suf, p, INFO, arrive(p, 2, INFO))

        @pl.when(chip == 2)
        def _():
            put(pre, p, STATE, arrive(p, 1, STATE))

        @pl.when(chip == 3)
        def _():
            if len(relays[p]) > 1:
                state = arrive(p, 1, STATE)
            else:
                state = arrive(p, 0, STATE)
                state = carry_state(state, arrive(p, 1, full))
            put(pre, p, STATE, carry_state(state, arrive(p, 2, full)))

    def direct_sent(p):
        direct_each(p, lambda copy: copy.wait_send())
        for sender in (1, 2):
            @pl.when(chip == sender)
            def _():
                for d in range(len(relays[p])):
                    direct_copy(p, sender, d, True).wait_send()

    def forward(p):
        slots = PHASES[p]
        m0, m1, p00, p01, p11 = values(pre, p, STATE)
        for t in range(span):
            num, den = obs[slots, 0, t], obs[slots, 1, t]
            inv, w, e, k1, g = gains(num, den, m0, p00, p01)
            for k, value in enumerate((g, w, e, k1, m0 + p00 * e, p00 * inv, p01 * inv)):
                saved[slots, t, k] = value
            m0, m1, p00, p01, p11 = advance(t, den, inv, e, m0, m1, p00, p01, p11)

        put(after, p, STATE, (m0, m1, p00, p01, p11))

    half = pl.ds(pl.multiple_of(core * LANES, LANES), LANES)

    def result_rows(slot):
        return pl.ds(pl.multiple_of(groups[slot] * SUB, SUB) if slot > 1 else groups[slot] * SUB, SUB)

    def result_copy(slot):
        return pltpu.make_async_remote_copy(
            src_ref=res.at[slot, :, other], dst_ref=landed.at[:, :, result_rows(slot), half],
            send_sem=res_send.at[slot], recv_sem=res_recv.at[slot], device_id={"tm": partner})

    def backward(p):
        slots = PHASES[p]
        i0, i1, i00, i01, i11 = values(suf, p, INFO)
        m0, m1, p00, p01, p11 = values(after, p, STATE)
        s, s2 = decay**span, decay ** (2 * span)
        mat = (i00 * s2, i01 * s2, i11 * s2)
        pulled = symv(mat, (m0, m1))
        (n00, n01, n11), (u0, u1) = absorb(mat, (p00, p01, p11),
                                           (i0 * s - pulled[0], i1 * s - pulled[1]))
        for t in reversed(range(span)):
            g, w, e, k1, m0, p00, p01 = (saved[slots, t, k] for k in range(SAVED))
            later = u0 + u1
            f01 = n00 + n01
            f11 = f01 + (n01 + n11)
            mean = m0 + p00 * u0 + p01 * later
            g0, g1 = p00 * n00 + p01 * f01, p00 * f01 + p01 * f11
            res[slots, 0, t] = inverse(1.0 + jnp.exp(mean * -(decay**t)))
            res[slots, 1, t] = (p00 - (p00 * g0 + p01 * g1)) * decay ** (2 * t)
            u0, u1 = (e + g * u0) - k1 * u1, later
            n00, n01, n11 = ((w + (g * g) * n00) + ((k1 * k1) * n11 - (2.0 * (g * k1)) * n01),
                             (g * n00 - k1 * n01) + (g * n01 - k1 * n11), f11)
            if t == 0 or t == frames:
                @pl.when(core == (1 if t == 0 else 0))
                def _():
                    for slot in range(slots.start, slots.stop):
                        result_copy(slot).start()
        for slot in range(slots.start, slots.stop):
            landed[:, :, result_rows(slot), half] = res[slot, :, own]

    def send(p):
        if chips == 4:
            direct_each(p, lambda copy: copy.start())
        else:
            send_level(p, 0)

    def halos(direction, there):
        @pl.when(there)
        def _():
            for sender in range(CORES):
                halo_arrived(direction, sender)

    to_partner.wait_recv()
    summary(0)
    if chips == 4:
        tell()
    send(0)
    halos(0, jnp.logical_and(has_up, has_down))
    summary(1)
    if chips == 4:
        @pl.when(chip > 0)
        def _():
            pl.semaphore_wait(hello.at[0], 1)

    send(1)
    halos(1, has_down)
    halos(0, jnp.logical_and(has_up, jnp.logical_not(has_down)))
    summary(2)
    send(2)
    order = range(len(PHASES))
    if chips == 4:
        for p in order:
            relay(p)

        @pl.when(chip < 2)
        def _():
            for p in order:
                forward(p)
    else:
        for level in range(levels):
            for p in order:
                take_level(p, level)
                if level + 1 < levels:
                    send_level(p, level + 1)

    def finish(p):
        if chips == 4:
            collect(p)
            pl.when(chip >= 2)(functools.partial(forward, p))
        else:
            forward(p)
        backward(p)

    def sent(p):
        if chips == 4:
            direct_sent(p)
        else:
            for level in range(levels):
                each_send(p, level, lambda copy: copy.wait_send())

    if chips == 4:
        @pl.when(chip == 0)
        def _():
            for p in (1, 2, 0):
                finish(p)

        @pl.when(chip > 0)
        def _():
            for p in order:
                finish(p)
    else:
        for p in order:
            finish(p)
    for p in order:
        sent(p)
    for direction, there in ((0, has_down), (1, has_up)):
        @pl.when(there)
        def _():
            for crossed in range(2):
                halo(direction, crossed).wait_send()
    to_partner.wait_send()
    for slot in range(SLOTS):
        result_copy(slot).wait_send()
        result_copy(slot).wait_recv()


def hand_out(landed, occupancy, spread, sems):
    copies = [pltpu.make_async_copy(landed.at[k], out, sems.at[k])
              for k, out in enumerate((occupancy, spread))]
    for copy in copies:
        copy.start()
    for copy in copies:
        copy.wait()


def solution(mesh):
    tm_count, space_count = mesh.shape["tm"], mesh.shape["space"]

    def body(hits, misses):
        frames, rows, cols = hits.shape
        span, chips = CORES * frames, tm_count // CORES
        levels = chips.bit_length() - 1
        cells = (SUB, LANES)
        assert rows == 4 * SUB and cols == CORES * LANES and chips == 1 << levels
        f32 = jnp.float32
        hbm = pl.BlockSpec(memory_space=pltpu.HBM)
        vmem = pl.BlockSpec(memory_space=pltpu.VMEM)
        dma = pltpu.SemaphoreType.DMA
        landed = pl.pallas_call(
            functools.partial(kernel, tm_count, space_count),
            out_shape=pltpu.VMEM((2, frames, rows, cols), f32),
            in_specs=[hbm] * 2,
            out_specs=vmem,
            scratch_shapes=[
                pltpu.VMEM(hits.shape, jnp.int32),
                pltpu.VMEM(hits.shape, jnp.int32),
                pltpu.VMEM((2, frames, rows, cols), f32),
                pltpu.VMEM((2, span, rows + 2 * SUB, LANES), f32),
                pltpu.VMEM((2, frames, rows, LANES), f32),
                pltpu.VMEM((SLOTS, 2, span) + cells, f32),
                pltpu.VMEM((SLOTS, VALUES) + cells, f32),
                pltpu.VMEM((max(levels - 1, 1), SLOTS, VALUES) + cells, f32),
                pltpu.VMEM((max(levels, 4), SLOTS, VALUES) + cells, f32),
                pltpu.VMEM((SLOTS, VALUES) + cells, f32),
                pltpu.VMEM((SLOTS, VALUES) + cells, f32),
                pltpu.VMEM((SLOTS, 5) + cells, f32),
                pltpu.VMEM((SLOTS, span, SAVED) + cells, f32),
                pltpu.VMEM((SLOTS, 2, span) + cells, f32),
                dma((2, 2, 2)),
                dma((2, 2)),
                dma((2, 2)),
                dma((1,)),
                dma((1,)),
                dma((3, 4) if chips == 4 else (3, levels, chips // 2)),
                dma((3, max(levels, 4))),
                dma((SLOTS,)),
                dma((SLOTS,)),
                pltpu.SemaphoreType.REGULAR((1,)),
            ],
            compiler_params=pltpu.CompilerParams(
                collective_id=0, has_side_effects=True, vmem_limit_bytes=32 * 1024 * 1024),
        )(pltpu.with_memory_space_constraint(hits, pltpu.HBM),
          pltpu.with_memory_space_constraint(misses, pltpu.HBM))
        out = jax.ShapeDtypeStruct(hits.shape, f32)
        return pl.pallas_call(
            hand_out,
            out_shape=(out, out),
            in_specs=[vmem],
            out_specs=(hbm, hbm),
            scratch_shapes=[dma((2,))],
            compiler_params=pltpu.CompilerParams(vmem_limit_bytes=8 * 1024 * 1024),
        )(landed)

    placed = P("tm", "space", None)
    return jax.shard_map(body, mesh=mesh, in_specs=(placed, placed),
                         out_specs=(placed, placed), check_vma=False)
```
